256 devices in a mesh: dp: 2 (over y_lo), ctx: 128 (over y_hi, z, x, core).
Axes of the slice: x: 4, y: 4 (y_hi: 2, y_lo: 2; y = y_hi * 2 + y_lo), z: 8, core: 2. Of those that a mesh axis runs over, the one named last changes fastest.
Arguments:
- features: bfloat16 [2, 256, 512, 512], P('dp', 'ctx'), may hold values from -20 to 20
- w_qkv: bfloat16 [512, 1536], replicated, may hold values from -0.7 to 0.7
- w_out: bfloat16 [512, 512], replicated, may hold values from -0.25 to 0.25
- layout: int32 [4, 4, 4], replicated, may hold values from 0 to 1, as said below
- grad_out: bfloat16 [2, 256, 512, 512], P('dp', 'ctx'), may hold values from -6 to 6
Outputs:
- layer_out: bfloat16 [2, 256, 512, 512], P('dp', 'ctx')
- grad_features: bfloat16 [2, 256, 512, 512], P('dp', 'ctx')
- grad_qkv: float32 [512, 1536], P('ctx')
- grad_wout: float32 [512, 512], P('ctx')
The draws below stay inside these ranges and needn't reach their ends.
Inputs may be any that keep to these rules, and one draw needn't show every extreme that they name: layout[h, a, b] is 1 where a == b and 0 where b > a.
All inputs are finite; a program needn't handle non-finite values.
Results may differ from the reference program's by a relative error of at most 0.015.
Values may be sent and summed in bfloat16 or wider, within the bound.
A program may use at most 128 MiB of HBM per device.

```python
import jax
import jax.numpy as jnp
from jax import lax

D = 512
HEADS = 8
HEAD = 64
ROW_HEADS = 4
ROW_LEN = 512
BLOCK = 128
NBLK = 4
GRID_ROWS = 256
CLIPS = 2


def draw_features(key, part):
    key_a = jax.random.fold_in(jax.random.fold_in(key, 11), 0)
    own = jax.random.normal(key_a, (CLIPS, GRID_ROWS, ROW_LEN, D), jnp.float32)
    values = own
    return jnp.clip(values, -20.0, 20.0).astype(jnp.bfloat16)


def draw_w_qkv(key, part):
    key_a = jax.random.fold_in(jax.random.fold_in(key, 23), 0)
    spread = D ** (-0.5)
    weights = jax.random.normal(key_a, (D, 3 * D), jnp.float32) * spread
    return jnp.clip(weights, -0.7, 0.7).astype(jnp.bfloat16)


def draw_layout(key, part):
    random_bits = jax.random.randint(jax.random.fold_in(key, 37), (ROW_HEADS, NBLK, NBLK), 0, 2)
    row_idx = jnp.arange(NBLK)[:, None]
    col_idx = jnp.arange(NBLK)[None, :]
    below = jnp.where(row_idx > col_idx, random_bits, 0)
    return jnp.where(row_idx == col_idx, 1, below).astype(jnp.int32)


def steps_of(stream_key, extent, cuts, low, top_value):
    loudness = 1.0
    for dim, parts in cuts:
        draws = jax.random.uniform(jax.random.fold_in(jax.random.fold_in(stream_key, 6), dim), (parts,), jnp.float32, low / len(cuts), top_value / len(cuts))
        loudness = loudness * jnp.repeat(jnp.exp(draws), extent[dim] // parts).reshape((-1,) + (1,) * (len(extent) - 1 - dim))
    return loudness


def bell_draw(rng, extent, scale, limit, pieces=(), dtype=jnp.bfloat16):
    drawn = scale * jax.random.normal(rng, extent, jnp.float32)
    if pieces:
        drawn = drawn * steps_of(rng, extent, pieces, -0.22, 0.18)
    return jnp.clip(drawn, -limit, limit).astype(dtype)


def setup_inputs(seed: int = 0) -> dict:
    keys = jax.random.split(jax.random.key(seed), 6)
    return {
        "features": draw_features(jax.random.fold_in(keys[5], 71), 0),
        "w_qkv": draw_w_qkv(jax.random.fold_in(keys[5], 71), 0),
        "w_out": bell_draw(keys[2], (D, D), D ** -0.5, 0.25),
        "layout": draw_layout(jax.random.fold_in(keys[5], 71), 0),
        "grad_out": bell_draw(keys[4], (CLIPS, GRID_ROWS, ROW_LEN, D), 1.0, 6.0, ((0, 2), (1, 128))),
    }


def attend(queries, key_rows, value_rows, d_out, allowed):
    scale_factor = HEAD ** -0.5
    q_wide = queries.astype(jnp.float32)
    k_wide = key_rows.astype(jnp.float32)
    v_wide = value_rows.astype(jnp.float32)
    g_wide = d_out.astype(jnp.float32)
    scores = jnp.einsum('hid,hjd->hij', q_wide, k_wide) * scale_factor
    scores = jnp.where(allowed, scores, jnp.float32(-1e30))
    row_top = jnp.max(scores, axis=-1, keepdims=True)
    weights = jnp.where(allowed, jnp.exp(scores - row_top), jnp.float32(0.0))
    probs = weights / jnp.sum(weights, axis=-1, keepdims=True)
    p_low = probs.astype(jnp.bfloat16).astype(jnp.float32)
    attended = jnp.einsum('hij,hjd->hid', p_low, v_wide).astype(jnp.bfloat16)
    d_prob = jnp.einsum('hid,hjd->hij', g_wide, v_wide)
    d_score = probs * (d_prob - jnp.sum(probs * d_prob, axis=-1, keepdims=True))
    ds_low = d_score.astype(jnp.bfloat16).astype(jnp.float32)
    d_query = (jnp.einsum('hij,hjd->hid', ds_low, k_wide) * scale_factor).astype(jnp.bfloat16)
    d_key = (jnp.einsum('hij,hid->hjd', ds_low, q_wide) * scale_factor).astype(jnp.bfloat16)
    d_value = jnp.einsum('hij,hid->hjd', p_low, g_wide).astype(jnp.bfloat16)
    return attended, d_query, d_key, d_value


def reference(features, w_qkv, w_out, layout, grad_out):
    total = CLIPS * GRID_ROWS * ROW_LEN
    col_heads = HEADS - ROW_HEADS
    flat_in = features.reshape(total, D)
    flat_grad = grad_out.reshape(total, D)
    projected = jnp.dot(flat_in, w_qkv, preferred_element_type=jnp.float32).astype(jnp.bfloat16)
    projected = projected.reshape(CLIPS, GRID_ROWS, ROW_LEN, 3, HEADS, HEAD)
    d_att = jnp.dot(flat_grad, w_out.T, preferred_element_type=jnp.float32).astype(jnp.bfloat16)
    d_att = d_att.reshape(CLIPS, GRID_ROWS, ROW_LEN, HEADS, HEAD)

    positions = jnp.arange(ROW_LEN)
    causal = positions[None, :] <= positions[:, None]
    blocks = positions // BLOCK
    layout_full = layout[:, blocks][:, :, blocks]
    row_allowed = causal[None] & (layout_full == 1)
    row_in = projected[:, :, :, :, :ROW_HEADS].transpose(0, 1, 3, 4, 2, 5)
    row_in = row_in.reshape(CLIPS * GRID_ROWS, 3, ROW_HEADS, ROW_LEN, HEAD)
    row_dout = d_att[:, :, :, :ROW_HEADS].transpose(0, 1, 3, 2, 4).reshape(CLIPS * GRID_ROWS, ROW_HEADS, ROW_LEN, HEAD)

    def row_item(operands):
        return attend(operands[0][0], operands[0][1], operands[0][2], operands[1], row_allowed)

    row_res = lax.map(row_item, (row_in, row_dout))
    row_att = row_res[0].reshape(CLIPS, GRID_ROWS, ROW_HEADS, ROW_LEN, HEAD).transpose(0, 1, 3, 2, 4)
    row_grad = jnp.stack(row_res[1:], 1).reshape(CLIPS, GRID_ROWS, 3, ROW_HEADS, ROW_LEN, HEAD)
    row_grad = row_grad.transpose(0, 1, 4, 2, 3, 5)

    grid_pos = jnp.arange(GRID_ROWS)
    col_allowed = (grid_pos[None, :] <= grid_pos[:, None])[None]
    col_in = projected[:, :, :, :, ROW_HEADS:].transpose(0, 2, 3, 4, 1, 5)
    col_in = col_in.reshape(CLIPS * ROW_LEN, 3, col_heads, GRID_ROWS, HEAD)
    col_dout = d_att[:, :, :, ROW_HEADS:].transpose(0, 2, 3, 1, 4).reshape(CLIPS * ROW_LEN, col_heads, GRID_ROWS, HEAD)

    def col_item(operands):
        return attend(operands[0][0], operands[0][1], operands[0][2], operands[1], col_allowed)

    col_res = lax.map(col_item, (col_in, col_dout))
    col_att = col_res[0].reshape(CLIPS, ROW_LEN, col_heads, GRID_ROWS, HEAD).transpose(0, 3, 1, 2, 4)
    col_grad = jnp.stack(col_res[1:], 1).reshape(CLIPS, ROW_LEN, 3, col_heads, GRID_ROWS, HEAD)
    col_grad = col_grad.transpose(0, 4, 1, 2, 3, 5)

    attended = jnp.concatenate([row_att, col_att], 3).reshape(total, D)
    d_proj = jnp.concatenate([row_grad, col_grad], 4).reshape(total, 3 * D)
    layer_out = jnp.dot(attended, w_out, preferred_element_type=jnp.float32).astype(jnp.bfloat16)
    grad_features = jnp.dot(d_proj, w_qkv.T, preferred_element_type=jnp.float32).astype(jnp.bfloat16)
    grad_qkv = jnp.dot(flat_in.T, d_proj, preferred_element_type=jnp.float32)
    grad_wout = jnp.dot(attended.T, flat_grad, preferred_element_type=jnp.float32)
    shape_full = (CLIPS, GRID_ROWS, ROW_LEN, D)
    return layer_out.reshape(shape_full), grad_features.reshape(shape_full), grad_qkv, grad_wout
```

```python
import functools

import jax
import jax.numpy as jnp
from jax import lax
from jax.experimental import pallas as pl
from jax.experimental.pallas import tpu as pltpu
from jax.sharding import PartitionSpec as P

HEADS = 8
HEAD = 64
BLOCK = 128
HALF = 256
SCALE = HEAD**-0.5
NEG = -1e30
BF = jnp.bfloat16
F32 = jnp.float32
VMEM_LIMIT = 56 * 1024 * 1024


def nn(a, b):
    return jnp.dot(a, b, preferred_element_type=F32)


def nt(a, b):
    return lax.dot_general(a, b, (((1,), (1,)), ((), ())), preferred_element_type=F32)


def eye(n):
    r = lax.broadcasted_iota(jnp.int32, (n, n), 0)
    c = lax.broadcasted_iota(jnp.int32, (n, n), 1)
    return (r == c).astype(F32).astype(BF)


def turned(x, ident):
    return nt(ident, x).astype(BF)


def wire_matrix():
    t = lax.broadcasted_iota(jnp.int32, (256, 256), 0)
    k = lax.broadcasted_iota(jnp.int32, (256, 256), 1)
    src = ((t >> 2) & 1) * 128 + (t >> 3) * 4 + (t & 3)
    return (k == src).astype(F32).astype(BF)


def unwire_matrix():
    t = lax.broadcasted_iota(jnp.int32, (256, 256), 1)
    k = lax.broadcasted_iota(jnp.int32, (256, 256), 0)
    src = ((t >> 2) & 1) * 128 + (t >> 3) * 4 + (t & 3)
    return (k == src).astype(F32).astype(BF)


def column_matrix():
    t = lax.broadcasted_iota(jnp.int32, (256, 256), 0)
    k = lax.broadcasted_iota(jnp.int32, (256, 256), 1)
    return (k == (t & 63) * 4 + (t >> 6)).astype(F32).astype(BF)


def uncolumn_matrix():
    t = lax.broadcasted_iota(jnp.int32, (256, 256), 1)
    k = lax.broadcasted_iota(jnp.int32, (256, 256), 0)
    return (k == (t & 63) * 4 + (t >> 6)).astype(F32).astype(BF)


def rows_of_head(x, h):
    r = lax.broadcasted_iota(jnp.int32, x.shape, 0)
    return jnp.where((r >> 6) == h, x, jnp.zeros_like(x))


def lanes_of_head(x, h):
    c = lax.broadcasted_iota(jnp.int32, x.shape, 1)
    return jnp.where((c >> 6) == h, x, jnp.zeros_like(x))


def attend_head(h, k_all, v_all, k_t, v_t, q_t, d_t, q_all, d_all, mask):
    scores = nn(k_all, rows_of_head(q_t, h)) * SCALE
    scores = jnp.where(mask, scores, NEG)
    top = jnp.max(scores, axis=0, keepdims=True)
    weights = jnp.exp(scores - top)
    probs = weights * (1.0 / jnp.sum(weights, axis=0, keepdims=True))
    p_low = probs.astype(BF)
    out_t = nn(v_t[h * HEAD : (h + 1) * HEAD], p_low)
    d_prob = nn(v_all, rows_of_head(d_t, h))
    delta = jnp.sum(probs * d_prob, axis=0, keepdims=True)
    ds_low = (probs * (d_prob - delta)).astype(BF)
    dq_t = nn(k_t[h * HEAD : (h + 1) * HEAD], ds_low) * SCALE
    dv = nn(p_low, lanes_of_head(d_all, h))
    dk = nn(ds_low, lanes_of_head(q_all, h))
    return out_t, dq_t, dk, dv


def to_wire_kernel(x_ref, o_ref):
    perm = wire_matrix()
    for b in range(4):
        x = jnp.concatenate(
            [x_ref[128 * b : 128 * b + 128], x_ref[512 + 128 * b : 512 + 128 * b + 128]], 0
        )
        o_ref[256 * b : 256 * b + 256] = nn(perm, x).astype(BF)


def dout_kernel(g_ref, w_ref, o_ref):
    perm = wire_matrix()
    for b in range(4):
        x = jnp.concatenate(
            [g_ref[128 * b : 128 * b + 128], g_ref[512 + 128 * b : 512 + 128 * b + 128]], 0
        )
        d = nt(x, w_ref[HALF:]).astype(BF)
        o_ref[256 * b : 256 * b + 256] = nn(perm, d).astype(BF)


def row_kernel(lay_ref, f_ref, g_ref, w_ref, wo_ref, att_ref, gf_ref, gq_ref, gwo_ref, dk_ref, dv_ref):
    step = pl.program_id(0)
    feats = f_ref[0]
    grads = g_ref[0]
    n = feats.shape[0]
    ident = eye(256)
    wq, wk, wv = (w_ref[:, s * 512 : s * 512 + HALF] for s in range(3))
    q_all = nn(feats, wq).astype(BF)
    k_all = nn(feats, wk).astype(BF)
    v_all = nn(feats, wv).astype(BF)
    d_all = nt(grads, wo_ref[:HALF]).astype(BF)
    q_t, k_t, v_t, d_t = (turned(x, ident) for x in (q_all, k_all, v_all, d_all))
    dk_ref[...] = jnp.zeros_like(dk_ref)
    dv_ref[...] = jnp.zeros_like(dv_ref)
    att_parts, dq_parts = [], []
    width = 256
    for chunk in range(n // width):
        nj = (chunk + 1) * width
        cols = slice(chunk * width, (chunk + 1) * width)
        key = lax.broadcasted_iota(jnp.int32, (nj, width), 0)
        qry = lax.broadcasted_iota(jnp.int32, (nj, width), 1) + chunk * width
        causal = key <= qry
        lane = lax.broadcasted_iota(jnp.int32, (1, width), 1)
        outs, dqs = [], []
        for h in range(4):
            tiles = []
            for jb in range(nj // BLOCK):
                line = jnp.where(
                    lane < BLOCK, lay_ref[h, 2 * chunk, jb], lay_ref[h, 2 * chunk + 1, jb]
                )
                tiles.append(jnp.broadcast_to(line, (BLOCK, width)))
            mask = jnp.logical_and(causal, jnp.concatenate(tiles, 0) == 1)
            out_t, dq_t, dk, dv = attend_head(
                h, k_all[:nj], v_all[:nj], k_t[:, :nj], v_t[:, :nj],
                q_t[:, cols], d_t[:, cols], q_all[cols], d_all[cols], mask,
            )
            dk_ref[:nj] += dk
            dv_ref[:nj] += dv
            outs.append(out_t)
            dqs.append(dq_t)
        att_parts.append(jnp.concatenate(outs, 0).astype(BF))
        dq_parts.append(jnp.concatenate(dqs, 0).astype(BF))
    att_t = jnp.concatenate(att_parts, 1)
    dq_tt = jnp.concatenate(dq_parts, 1)
    att_ref[0] = jnp.concatenate([nt(ident, p) for p in att_parts], 0).astype(BF)
    dq = jnp.concatenate([nt(ident, p) for p in dq_parts], 0).astype(BF)
    del dq_tt
    dk = (dk_ref[...] * SCALE).astype(BF)
    dv = dv_ref[...].astype(BF)
    gf_ref[0] = nt(dq, wq) + nt(dk, wk) + nt(dv, wv)
    feats_t = jnp.concatenate([turned(feats[:, :256], ident), turned(feats[:, 256:], ident)], 0)

    @pl.when(step == 0)
    def _():
        gq_ref[...] = jnp.zeros_like(gq_ref)
        gwo_ref[...] = jnp.zeros_like(gwo_ref)

    for s, d in enumerate((dq, dk, dv)):
        gq_ref[:, s * HALF : (s + 1) * HALF] += nn(feats_t, d)
    gwo_ref[...] += nn(att_t, grads)


def col_kernel(f_ref, d_ref, w_ref, att_ref, gf_ref, gq_ref, fcol, dcol, acol, gcol):
    ident = eye(256)
    perm = column_matrix()
    for b in range(4):
        rows = slice(256 * b, 256 * b + 256)
        x = nn(perm, f_ref[rows]).astype(BF)
        d = nn(perm, d_ref[rows]).astype(BF)
        for c in range(4):
            fcol[c, 64 * b : 64 * b + 64] = x[64 * c : 64 * c + 64]
            dcol[c, 64 * b : 64 * b + 64] = d[64 * c : 64 * c + 64]
    wq, wk, wv = (w_ref[:, s * 512 + HALF : s * 512 + 512] for s in range(3))
    key = lax.broadcasted_iota(jnp.int32, (256, 256), 0)
    qry = lax.broadcasted_iota(jnp.int32, (256, 256), 1)
    mask = key <= qry
    gq_ref[...] = jnp.zeros_like(gq_ref)

    @pl.loop(0, 4)
    def _(c):
        feats = fcol[c]
        q_all = nn(feats, wq).astype(BF)
        k_all = nn(feats, wk).astype(BF)
        v_all = nn(feats, wv).astype(BF)
        d_all = dcol[c]
        q_t, k_t, v_t, d_t = (turned(x, ident) for x in (q_all, k_all, v_all, d_all))
        outs, dqs, dk, dv = [], [], None, None
        for h in range(4):
            out_t, dq_t, dk_h, dv_h = attend_head(
                h, k_all, v_all, k_t, v_t, q_t, d_t, q_all, d_all, mask
            )
            outs.append(out_t)
            dqs.append(dq_t)
            dk = dk_h if dk is None else dk + dk_h
            dv = dv_h if dv is None else dv + dv_h
        att = nt(ident, jnp.concatenate(outs, 0).astype(BF)).astype(BF)
        dq = nt(ident, jnp.concatenate(dqs, 0).astype(BF)).astype(BF)
        dk = (dk * SCALE).astype(BF)
        dv = dv.astype(BF)
        acol[c] = att
        gcol[c] = (nt(dq, wq) + nt(dk, wk) + nt(dv, wv)).astype(BF)
        feats_t = jnp.concatenate([turned(feats[:, :256], ident), turned(feats[:, 256:], ident)], 0)
        for s, d in enumerate((dq, dk, dv)):
            gq_ref[:, s * HALF : (s + 1) * HALF] += nn(feats_t, d)

    back = uncolumn_matrix()
    for b in range(4):
        rows = slice(256 * b, 256 * b + 256)
        a = jnp.concatenate([acol[c, 64 * b : 64 * b + 64] for c in range(4)], 0)
        g = jnp.concatenate([gcol[c, 64 * b : 64 * b + 64] for c in range(4)], 0)
        att_ref[rows] = nn(back, a).astype(BF)
        gf_ref[rows] = nn(back, g).astype(BF)


def out_kernel(arow_ref, awire_ref, g_ref, wo_ref, out_ref, gwo_ref):
    perm = unwire_matrix()
    ident = eye(256)
    gwo = None
    for b in range(4):
        a = nn(perm, awire_ref[256 * b : 256 * b + 256]).astype(BF)
        pieces = []
        for r in range(2):
            rows = slice(512 * r + 128 * b, 512 * r + 128 * b + 128)
            col = a[128 * r : 128 * r + 128]
            out_ref[rows] = (nn(arow_ref[rows], wo_ref[:HALF]) + nn(col, wo_ref[HALF:])).astype(BF)
            pieces.append(g_ref[rows])
        term = nn(turned(a, ident), jnp.concatenate(pieces, 0))
        gwo = term if gwo is None else gwo + term
    gwo_ref[...] = gwo


def gf_kernel(gf_ref, gwire_ref, out_ref):
    perm = unwire_matrix()
    for b in range(4):
        g = nn(perm, gwire_ref[256 * b : 256 * b + 256])
        for r in range(2):
            rows = slice(512 * r + 128 * b, 512 * r + 128 * b + 128)
            out_ref[rows] = (gf_ref[rows] + g[128 * r : 128 * r + 128]).astype(BF)


def scatter_kernel(n_y, n_z, n_x, g_ref, o_ref, cbuf, a_buf, xbuf, b_buf, ybuf, d_buf, zbuf, e_buf, lbuf,
                   ssem, csem, xsem, ysem, zsem, lsem):
    dp = lax.axis_index("dp")
    ctx = lax.axis_index("ctx")
    core = ctx % 2
    x = (ctx // 2) % n_x
    z = (ctx // (2 * n_x)) % n_z
    yh = ctx // (2 * n_x * n_z)
    half = g_ref.shape[-1] // 2

    def dev(yh_, z_, x_, core_, dp_):
        return (dp_, ((yh_ * n_z + z_) * n_x + x_) * 2 + core_)

    mate = dev(yh, z, x, 1 - core, dp)
    x_peers = [dev(yh, z, (x + s) % n_x, core, dp) for s in range(1, n_x)]
    y_peers = [((yh + s // 2) % 2, (dp + s) % 2) for s in range(1, 4)]
    z_peers = [(z + s) % n_z for s in range(1, n_z)]
    everyone = (
        [mate]
        + x_peers
        + [dev(a, z, x, core, b) for a, b in y_peers]
        + [dev(yh, a, x, core, dp) for a in z_peers]
    )
    barrier = pltpu.get_barrier_semaphore()
    for d in everyone:
        pl.semaphore_signal(barrier, inc=1, device_id=d, device_id_type=pl.DeviceIdType.MESH)
    pl.semaphore_wait(barrier, len(everyone))

    def remote(src, dst, s, r, d):
        return pltpu.make_async_remote_copy(
            src_ref=src, dst_ref=dst, send_sem=s, recv_sem=r, device_id=d,
            device_id_type=pl.DeviceIdType.MESH,
        )

    copy = remote(g_ref.at[:, :, :, :, pl.ds(pl.multiple_of((1 - core) * half, 128), half)], cbuf,
                  ssem.at[0], csem.at[0], mate)
    copy.start()
    copy.wait()
    mine = pl.ds(pl.multiple_of(core * half, 128), half)
    for zz in range(n_z):
        a_buf[:, :, zz] = (
            g_ref[:, zz, :, :, mine].astype(F32) + cbuf[:, zz].astype(F32)
        ).astype(BF).swapaxes(0, 1)
    copies = []
    for s in range(1, n_x):
        to = (x + s) % n_x
        copies.append(remote(a_buf.at[to], xbuf.at[s - 1], ssem.at[s], xsem.at[s - 1],
                             dev(yh, z, to, core, dp)))
    for c in copies:
        c.start()
    for c in copies:
        c.wait()
    for yy in range(n_y):
        total = a_buf[x, yy].astype(F32)
        for s in range(1, n_x):
            total = total + xbuf[s - 1, yy].astype(F32)
        b_buf[yy] = total.astype(BF)
    here = yh * 2 + dp
    copies = []
    for s in range(1, 4):
        to = (here + s) % 4
        copies.append(remote(b_buf.at[to // 2], ybuf.at[here], ssem.at[3 + s], ysem.at[s - 1],
                             dev(to // 2, z, x, core, to % 2)))
    for c in copies:
        c.start()
    ybuf[here] = b_buf[yh]
    for c in copies:
        c.wait()
    total = ybuf[0].astype(F32)
    for s in range(1, 4):
        total = total + ybuf[s].astype(F32)
    d_buf[...] = total.astype(BF)
    copies = []
    for s in range(1, n_z):
        to = (z + s) % n_z
        copies.append(remote(d_buf.at[to], zbuf.at[z], ssem.at[6 + s], zsem.at[s - 1],
                             dev(yh, to, x, core, dp)))
    for c in copies:
        c.start()
    zbuf[z] = d_buf[z]
    for c in copies:
        c.wait()
    total = zbuf[0].astype(F32)
    for s in range(1, n_z):
        total = total + zbuf[s].astype(F32)
    e_buf[...] = total
    copy = remote(e_buf, lbuf, ssem.at[7 + n_z - 1], lsem.at[0], mate)
    copy.start()
    copy.wait()
    own, other = e_buf[...], lbuf[...]
    first = jnp.where(core == 0, own, other)
    second = jnp.where(core == 0, other, own)
    full = jnp.concatenate([first, second], 1)
    o_ref[...] = jnp.where(core == 0, full[:4], full[4:])


def scatter_sum(g, cid):
    rows, cols = g.shape
    n_y, n_z, n_x, half = 2, 8, 4, cols // 2
    g = g.reshape(n_y, n_z, n_x, 8, cols)
    vm = pl.BlockSpec(memory_space=pltpu.VMEM)
    sem = pltpu.SemaphoreType.DMA
    return pl.pallas_call(
        functools.partial(scatter_kernel, n_y, n_z, n_x),
        out_shape=jax.ShapeDtypeStruct((4, cols), F32),
        in_specs=[vm],
        out_specs=vm,
        scratch_shapes=[
            pltpu.VMEM((n_y, n_z, n_x, 8, half), BF),
            pltpu.VMEM((n_x, n_y, n_z, 8, half), BF),
            pltpu.VMEM((n_x - 1, n_y, n_z, 8, half), BF),
            pltpu.VMEM((n_y, n_z, 8, half), BF),
            pltpu.VMEM((4, n_z, 8, half), BF),
            pltpu.VMEM((n_z, 8, half), BF),
            pltpu.VMEM((n_z, 8, half), BF),
            pltpu.VMEM((8, half), F32),
            pltpu.VMEM((8, half), F32),
            sem((7 + n_z,)),
            sem((1,)),
            sem((n_x - 1,)),
            sem((3,)),
            sem((n_z - 1,)),
            sem((1,)),
        ],
        compiler_params=pltpu.CompilerParams(
            collective_id=cid, has_side_effects=True, vmem_limit_bytes=VMEM_LIMIT
        ),
        cost_estimate=pl.CostEstimate(flops=rows * cols, bytes_accessed=8 * rows * cols, transcendentals=0),
        name="scatter_sum",
    )(g)


def call(kernel, outs, *args, scratch=(), cost=1_000_000, name=None):
    return pl.pallas_call(
        kernel,
        out_shape=[jax.ShapeDtypeStruct(s, d) for s, d in outs],
        scratch_shapes=list(scratch),
        compiler_params=pltpu.CompilerParams(vmem_limit_bytes=VMEM_LIMIT),
        cost_estimate=pl.CostEstimate(flops=cost, bytes_accessed=4_000_000, transcendentals=0),
        name=name,
    )(*args)


def row_part(features, grad_out, w_qkv, w_out, layout):
    n = features.shape[0]
    whole = lambda *shape: pl.BlockSpec(shape, lambda r: (0,) * len(shape))
    per_row = lambda *shape: pl.BlockSpec((1,) + shape, lambda r: (r, 0, 0))
    return pl.pallas_call(
        row_kernel,
        grid=(n,),
        in_specs=[
            pl.BlockSpec(memory_space=pltpu.SMEM),
            per_row(512, 512),
            per_row(512, 512),
            whole(512, 1536),
            whole(512, 512),
        ],
        out_specs=[per_row(512, 256), per_row(512, 512), whole(512, 768), whole(256, 512)],
        out_shape=[
            jax.ShapeDtypeStruct((n, 512, 256), BF),
            jax.ShapeDtypeStruct((n, 512, 512), F32),
            jax.ShapeDtypeStruct((512, 768), F32),
            jax.ShapeDtypeStruct((256, 512), F32),
        ],
        scratch_shapes=[pltpu.VMEM((512, 256), F32), pltpu.VMEM((512, 256), F32)],
        compiler_params=pltpu.CompilerParams(
            dimension_semantics=("arbitrary",), vmem_limit_bytes=VMEM_LIMIT
        ),
        cost_estimate=pl.CostEstimate(
            flops=12_000_000_000, bytes_accessed=12_000_000, transcendentals=2_000_000
        ),
        name="row_heads",
    )(layout, features, grad_out, w_qkv, w_out)


def col_part(f_got, d_got, w_qkv):
    return call(
        col_kernel,
        [((1024, 256), BF), ((1024, 512), BF), ((512, 768), F32)],
        f_got, d_got, w_qkv,
        scratch=[
            pltpu.VMEM((4, 256, 512), BF),
            pltpu.VMEM((4, 256, 256), BF),
            pltpu.VMEM((4, 256, 256), BF),
            pltpu.VMEM((4, 256, 512), BF),
        ],
        cost=6_000_000_000,
        name="col_heads",
    )


def on_device(features, w_qkv, w_out, layout, grad_out):
    n_clips, n_rows, length, width = features.shape
    total = n_clips * n_rows * length
    n_ctx = lax.axis_size("ctx")
    feats = features.reshape(total, width)
    grads = grad_out.reshape(total, width)

    def swap(x):
        x = x.reshape(n_ctx, total // n_ctx, x.shape[-1])
        x = lax.all_to_all(x, "ctx", split_axis=0, concat_axis=0, tiled=True)
        return x.reshape(total, x.shape[-1])

    (f_wire,) = call(to_wire_kernel, [((total, width), BF)], feats, name="to_wire")
    f_got = swap(f_wire)
    (d_wire,) = call(dout_kernel, [((total, HALF), BF)], grads, w_out, name="dout")
    d_got = swap(d_wire)
    att_row, gf_row, gq_row, gwo_row = row_part(
        features.reshape(n_rows, length, width), grad_out.reshape(n_rows, length, width),
        w_qkv, w_out, layout,
    )
    att_wire, gf_wire, gq_col = col_part(f_got, d_got, w_qkv)
    att_got = swap(att_wire)
    gf_got = swap(gf_wire)
    layer_out, gwo_col = call(
        out_kernel, [((total, width), BF), ((HALF, width), F32)],
        att_row.reshape(total, HALF), att_got, grads, w_out, name="home_out",
    )
    (grad_features,) = call(
        gf_kernel, [((total, width), BF)], gf_row.reshape(total, width), gf_got, name="home_gf"
    )
    gq = jnp.stack([gq_row.reshape(512, 3, HALF), gq_col.reshape(512, 3, HALF)], 2)
    terms = jnp.concatenate([gq.reshape(512, 1536), jnp.concatenate([gwo_row, gwo_col], 0)], 1)
    rows = scatter_sum(terms.astype(BF), 1)
    shape = (n_clips, n_rows, length, width)
    return layer_out.reshape(shape), grad_features.reshape(shape), rows[:, :1536], rows[:, 1536:]


def solution(mesh):
    return jax.shard_map(
        on_device,
        mesh=mesh,
        in_specs=(P("dp", "ctx", None, None), P(), P(), P(), P("dp", "ctx", None, None)),
        out_specs=(
            P("dp", "ctx", None, None),
            P("dp", "ctx", None, None),
            P("ctx", None),
            P("ctx", None),
        ),
        check_vma=False,
    )
```

```python
import functools

import jax
import jax.numpy as jnp
from jax import lax
from jax.experimental import pallas as pl
from jax.experimental.pallas import tpu as pltpu
from jax.sharding import PartitionSpec as P

HEADS = 8
HEAD = 64
BLOCK = 128
HALF = 256
SCALE = HEAD**-0.5
NEG = -1e30
BF = jnp.bfloat16
F32 = jnp.float32
VMEM_LIMIT = 58 * 1024 * 1024
MESH = pl.DeviceIdType.MESH
N_Y, N_Z, N_X = 2, 8, 4


def nn(a, b):
    return jnp.dot(a, b, preferred_element_type=F32)


def nt(a, b):
    return lax.dot_general(a, b, (((1,), (1,)), ((), ())), preferred_element_type=F32)


def eye(n):
    r = lax.broadcasted_iota(jnp.int32, (n, n), 0)
    c = lax.broadcasted_iota(jnp.int32, (n, n), 1)
    return (r == c).astype(F32).astype(BF)


def turned(x, ident):
    return nt(ident, x).astype(BF)


def wire_matrix():
    t = lax.broadcasted_iota(jnp.int32, (256, 256), 0)
    k = lax.broadcasted_iota(jnp.int32, (256, 256), 1)
    src = ((t >> 2) & 1) * 128 + (t >> 3) * 4 + (t & 3)
    return (k == src).astype(F32).astype(BF)


def unwire_matrix():
    t = lax.broadcasted_iota(jnp.int32, (256, 256), 1)
    k = lax.broadcasted_iota(jnp.int32, (256, 256), 0)
    src = ((t >> 2) & 1) * 128 + (t >> 3) * 4 + (t & 3)
    return (k == src).astype(F32).astype(BF)


def column_matrix():
    t = lax.broadcasted_iota(jnp.int32, (256, 256), 0)
    k = lax.broadcasted_iota(jnp.int32, (256, 256), 1)
    return (k == (t & 63) * 4 + (t >> 6)).astype(F32).astype(BF)


def uncolumn_matrix():
    t = lax.broadcasted_iota(jnp.int32, (256, 256), 1)
    k = lax.broadcasted_iota(jnp.int32, (256, 256), 0)
    return (k == (t & 63) * 4 + (t >> 6)).astype(F32).astype(BF)


def rows_of_head(x, h):
    r = lax.broadcasted_iota(jnp.int32, x.shape, 0)
    return jnp.where((r >> 6) == h, x, jnp.zeros_like(x))


def lanes_of_head(x, h):
    c = lax.broadcasted_iota(jnp.int32, x.shape, 1)
    return jnp.where((c >> 6) == h, x, jnp.zeros_like(x))


def softmax_t(scores, mask):
    scores = jnp.where(mask, scores * SCALE, NEG)
    top = jnp.max(scores, axis=0, keepdims=True)
    weights = jnp.exp(scores - top)
    return weights * (1.0 / jnp.sum(weights, axis=0, keepdims=True))


def score_grad(probs, d_prob):
    delta = jnp.sum(probs * d_prob, axis=0, keepdims=True)
    return (probs * (d_prob - delta)).astype(BF)


def head_rows(h):
    return slice(h * HEAD, (h + 1) * HEAD)


class Place:
    def __init__(self):
        self.dp = lax.axis_index("dp")
        self.ctx = lax.axis_index("ctx")
        self.core = self.ctx % 2
        self.x = (self.ctx // 2) % N_X
        self.z = (self.ctx // (2 * N_X)) % N_Z
        self.yh = self.ctx // (2 * N_X * N_Z)

    def at(self, yh=None, z=None, x=None, core=None, dp=None):
        yh = self.yh if yh is None else yh
        z = self.z if z is None else z
        x = self.x if x is None else x
        core = self.core if core is None else core
        dp = self.dp if dp is None else dp
        return (dp, ((yh * N_Z + z) * N_X + x) * 2 + core)


def remote(src, dst, send, recv, device):
    return pltpu.make_async_remote_copy(
        src_ref=src, dst_ref=dst, send_sem=send, recv_sem=recv, device_id=device, device_id_type=MESH
    )


class Scatter:
    def __init__(self, place, g, bufs, sems):
        self.place, self.g = place, g
        self.c, self.a, self.xb, self.b, self.yb, self.d, self.zb, self.e, self.last = bufs
        self.send, self.cs, self.xs, self.ys, self.zs, self.ls = sems
        self.half = g.shape[-1] // 2
        self.copies = []

    def launch(self, copies):
        for c in copies:
            c.start()
        self.copies = copies

    def arrive(self):
        for c in self.copies:
            c.wait()

    def to_core(self):
        p, half = self.place, self.half
        theirs = pl.ds(pl.multiple_of((1 - p.core) * half, 128), half)
        self.launch([
            remote(self.g.at[:, :, :, :, theirs], self.c, self.send.at[0], self.cs.at[0],
                   p.at(core=1 - p.core))
        ])

    def to_x(self):
        p, half = self.place, self.half
        self.arrive()
        mine = pl.ds(pl.multiple_of(p.core * half, 128), half)

        @pl.loop(0, N_Z)
        def _(zz):
            for yy in range(N_Y):
                self.a[:, yy, zz] = (
                    self.g[yy, zz, :, :, mine].astype(F32) + self.c[yy, zz].astype(F32)
                ).astype(BF)

        copies = []
        for s in range(1, N_X):
            to = (p.x + s) % N_X
            copies.append(remote(self.a.at[to], self.xb.at[s - 1], self.send.at[s],
                                 self.xs.at[s - 1], p.at(x=to)))
        self.launch(copies)

    def to_y(self):
        p = self.place
        self.arrive()

        @pl.loop(0, N_Y)
        def _(yy):
            total = self.a[p.x, yy].astype(F32)
            for s in range(N_X - 1):
                total = total + self.xb[s, yy].astype(F32)
            self.b[yy] = total.astype(BF)

        here = p.yh * 2 + p.dp
        copies = []
        for s in range(1, 4):
            to = (here + s) % 4
            copies.append(remote(self.b.at[to // 2], self.yb.at[here], self.send.at[3 + s],
                                 self.ys.at[s - 1], p.at(yh=to // 2, dp=to % 2)))
        self.launch(copies)
        self.yb[here] = self.b[p.yh]

    def to_z(self):
        p = self.place
        self.arrive()
        total = self.yb[0].astype(F32)
        for s in range(1, 4):
            total = total + self.yb[s].astype(F32)
        self.d[...] = total.astype(BF)
        copies = []
        for s in range(1, N_Z):
            to = (p.z + s) % N_Z
            copies.append(remote(self.d.at[to], self.zb.at[p.z], self.send.at[6 + s],
                                 self.zs.at[s - 1], p.at(z=to)))
        self.launch(copies)
        self.zb[p.z] = self.d[p.z]

    def to_mate(self):
        p = self.place
        self.arrive()
        total = self.zb[0].astype(F32)
        for s in range(1, N_Z):
            total = total + self.zb[s].astype(F32)
        self.e[...] = total
        self.launch([
            remote(self.e, self.last, self.send.at[6 + N_Z], self.ls.at[0], p.at(core=1 - p.core))
        ])

    def result(self):
        self.arrive()
        first = self.place.core == 0
        own, other = self.e[...], self.last[...]
        full = jnp.concatenate([jnp.where(first, own, other), jnp.where(first, other, own)], 1)
        return jnp.where(first, full[:4], full[4:])


def scatter_scratch(cols):
    half = cols // 2
    sem = pltpu.SemaphoreType.DMA
    bufs = [
        pltpu.VMEM((N_Y, N_Z, N_X, 8, half), BF),
        pltpu.VMEM((N_X, N_Y, N_Z, 8, half), BF),
        pltpu.VMEM((N_X - 1, N_Y, N_Z, 8, half), BF),
        pltpu.VMEM((N_Y, N_Z, 8, half), BF),
        pltpu.VMEM((4, N_Z, 8, half), BF),
        pltpu.VMEM((N_Z, 8, half), BF),
        pltpu.VMEM((N_Z, 8, half), BF),
        pltpu.VMEM((8, half), F32),
        pltpu.VMEM((8, half), F32),
    ]
    sems = [sem((7 + N_Z,)), sem((1,)), sem((N_X - 1,)), sem((3,)), sem((N_Z - 1,)), sem((1,))]
    return dict(g=pltpu.VMEM((N_Y, N_Z, N_X, 8, cols), BF), bufs=bufs, sems=sems)


class Swap:
    def __init__(self, place, src, dst, send, recv):
        self.place, self.src, self.dst, self.send, self.recv = place, src, dst, send, recv
        self.n = src.shape[0]

    def start(self):
        p, n = self.place, self.n

        def step(s, carry):
            to = (p.ctx + s) % n
            remote(self.src.at[to], self.dst.at[p.ctx], self.send, self.recv, (p.dp, to)).start()
            return carry

        lax.fori_loop(1, n, step, 0)
        self.dst[p.ctx] = self.src[p.ctx]

    def all_but_one(self, ref, sem):
        part = ref.at[pl.ds(0, self.n - 1)]
        pltpu.make_async_copy(part, part, sem).wait()

    def arrived(self):
        self.all_but_one(self.dst, self.recv)

    def gone(self):
        self.all_but_one(self.src, self.send)


def to_wire(ref, get, perm):
    for b in range(4):
        x = get(b)
        y = nn(perm, x).astype(BF)
        ref[32 * b : 32 * b + 32] = y.reshape(32, 8, y.shape[-1])


def block_of(ref, b):
    return jnp.concatenate([ref[r, 128 * b : 128 * b + 128] for r in range(2)], 0)


def to_columns(wire, col, perm):
    for b in range(4):
        x = wire[32 * b : 32 * b + 32]
        y = nn(perm, x.reshape(256, x.shape[-1])).astype(BF)
        for c in range(4):
            col[c, 64 * b : 64 * b + 64] = y[64 * c : 64 * c + 64]


def from_columns(col, wire, perm):
    for b in range(4):
        x = jnp.concatenate([col[c, 64 * b : 64 * b + 64] for c in range(4)], 0)
        y = nn(perm, x).astype(BF)
        wire[32 * b : 32 * b + 32] = y.reshape(32, 8, y.shape[-1])


def turned_wide(x, ident):
    return jnp.concatenate([turned(x[:, :256], ident), turned(x[:, 256:], ident)], 0)


def row_heads(s, r, lay, feats, grads, w, wo, ident):
    n = feats.shape[0]
    wq, wk, wv = (w[:, i * 512 : i * 512 + HALF] for i in range(3))
    q_all = nn(feats, wq).astype(BF)
    k_all = nn(feats, wk).astype(BF)
    v_all = nn(feats, wv).astype(BF)
    d_all = nt(grads, wo[:HALF]).astype(BF)
    q_t, k_t, v_t, d_t = (turned(x, ident) for x in (q_all, k_all, v_all, d_all))
    s["dk"][...] = jnp.zeros_like(s["dk"])
    s["dv"][...] = jnp.zeros_like(s["dv"])
    att_parts, dq_parts = [], []
    width = 256
    for chunk in range(n // width):
        nj = (chunk + 1) * width
        cols = slice(chunk * width, (chunk + 1) * width)
        key = lax.broadcasted_iota(jnp.int32, (nj, width), 0)
        qry = lax.broadcasted_iota(jnp.int32, (nj, width), 1) + chunk * width
        causal = key <= qry
        lane = lax.broadcasted_iota(jnp.int32, (1, width), 1)
        outs, dqs = [], []
        for h in range(4):
            tiles = []
            for jb in range(nj // BLOCK):
                line = jnp.where(lane < BLOCK, lay[h, 2 * chunk, jb], lay[h, 2 * chunk + 1, jb])
                tiles.append(jnp.broadcast_to(line, (BLOCK, width)))
            mask = jnp.logical_and(causal, jnp.concatenate(tiles, 0) == 1)
            probs = softmax_t(nn(k_all[:nj], rows_of_head(q_t[:, cols], h)), mask)
            p_low = probs.astype(BF)
            outs.append(nn(v_t[head_rows(h), :nj], p_low))
            ds_low = score_grad(probs, nn(v_all[:nj], rows_of_head(d_t[:, cols], h)))
            dqs.append(nn(k_t[head_rows(h), :nj], ds_low) * SCALE)
            s["dv"][:nj] += nn(p_low, lanes_of_head(d_all[cols], h))
            s["dk"][:nj] += nn(ds_low, lanes_of_head(q_all[cols], h))
        att_parts.append(jnp.concatenate(outs, 0).astype(BF))
        dq_parts.append(jnp.concatenate(dqs, 0).astype(BF))
    s["att_row"][r] = jnp.concatenate([nt(ident, p) for p in att_parts], 0).astype(BF)
    dq = jnp.concatenate([nt(ident, p) for p in dq_parts], 0).astype(BF)
    dk = (s["dk"][...] * SCALE).astype(BF)
    dv = s["dv"][...].astype(BF)
    s["gf_row"][r] = nt(dq, wq) + nt(dk, wk) + nt(dv, wv)
    feats_t = turned_wide(feats, ident)
    for i, d in enumerate((dq, dk, dv)):
        s["gq_acc"][:, i * HALF : (i + 1) * HALF] += nn(feats_t, d)
    s["gwo_acc"][...] += nn(jnp.concatenate(att_parts, 1), grads)


def put_gq(s, offset):
    for i in range(3):
        part = s["gq_acc"][:, i * HALF : (i + 1) * HALF].astype(BF)
        s["gq"]["g"][:, :, :, :, i * 512 + offset : i * 512 + offset + HALF] = part.reshape(
            N_Y, N_Z, N_X, 8, HALF
        )


def put_gwo(s, half):
    part = s["gwo_acc"][...].astype(BF)
    s["gwo"]["g"][half] = part.reshape(N_Z, N_X, 8, 512)


def whole_kernel(lay, feats, grads, w, wo, out, gf_out, gq_out, gwo_out, s):
    p = Place()
    n_ctx = s["f_wire"].shape[0]
    barrier = pltpu.get_barrier_semaphore()

    def greet(step, carry):
        pl.semaphore_signal(
            barrier, inc=1, device_id=(p.dp, (p.ctx + step) % n_ctx), device_id_type=MESH
        )
        return carry

    lax.fori_loop(1, n_ctx, greet, 0)
    for yh in (p.yh, 1 - p.yh):
        pl.semaphore_signal(barrier, inc=1, device_id=p.at(yh=yh, dp=1 - p.dp), device_id_type=MESH)

    perm = wire_matrix()
    to_wire(s["f_wire"], lambda b: block_of(feats, b), perm)
    pl.semaphore_wait(barrier, n_ctx + 1)
    sems = s["swap"]
    f_swap = Swap(p, s["f_wire"], s["f_got"], sems.at[0], sems.at[1])
    d_swap = Swap(p, s["d_wire"], s["d_got"], sems.at[2], sems.at[3])
    a_swap = Swap(p, s["a_wire"], s["a_got"], sems.at[4], sems.at[5])
    g_swap = Swap(p, s["g_wire"], s["g_got"], sems.at[6], sems.at[7])
    f_swap.start()
    to_wire(s["d_wire"], lambda b: nt(block_of(grads, b), wo[HALF:]).astype(BF), perm)
    d_swap.start()

    ident = eye(256)
    s["gq_acc"][...] = jnp.zeros_like(s["gq_acc"])
    s["gwo_acc"][...] = jnp.zeros_like(s["gwo_acc"])

    @pl.loop(0, 2)
    def _(r):
        row_heads(s, r, lay, feats[r], grads[r], w, wo, ident)

    put_gq(s, 0)
    put_gwo(s, 0)

    key = lax.broadcasted_iota(jnp.int32, (256, 256), 0)
    qry = lax.broadcasted_iota(jnp.int32, (256, 256), 1)
    mask = key <= qry
    wq, wk, wv = (w[:, i * 512 + HALF : i * 512 + 512] for i in range(3))
    split, join = column_matrix(), uncolumn_matrix()
    f_swap.arrived()
    to_columns(s["f_got"], s["f_col"], split)

    @pl.loop(0, 4)
    def _(c):
        x = s["f_col"][c]
        q_all = nn(x, wq).astype(BF)
        k_all = nn(x, wk).astype(BF)
        v_all = nn(x, wv).astype(BF)
        s["q"][c], s["k"][c], s["v"][c] = q_all, k_all, v_all
        q_t, v_t = turned(q_all, ident), turned(v_all, ident)
        outs = []
        for h in range(4):
            probs = softmax_t(nn(k_all, rows_of_head(q_t, h)), mask)
            s["probs"][c, h] = probs
            outs.append(nn(v_t[head_rows(h)], probs.astype(BF)))
        s["a_col"][c] = nt(ident, jnp.concatenate(outs, 0).astype(BF)).astype(BF)

    from_columns(s["a_col"], s["a_wire"], join)
    a_swap.start()

    d_swap.arrived()
    to_columns(s["d_got"], s["d_col"], split)
    s["gq_acc"][...] = jnp.zeros_like(s["gq_acc"])

    @pl.loop(0, 4)
    def _(c):
        x = s["f_col"][c]
        q_all, k_all, v_all, d_all = s["q"][c], s["k"][c], s["v"][c], s["d_col"][c]
        k_t, d_t = turned(k_all, ident), turned(d_all, ident)
        dqs, dk, dv = [], None, None
        for h in range(4):
            probs = s["probs"][c, h]
            ds_low = score_grad(probs, nn(v_all, rows_of_head(d_t, h)))
            dqs.append(nn(k_t[head_rows(h)], ds_low) * SCALE)
            dv_h = nn(probs.astype(BF), lanes_of_head(d_all, h))
            dk_h = nn(ds_low, lanes_of_head(q_all, h))
            dk = dk_h if dk is None else dk + dk_h
            dv = dv_h if dv is None else dv + dv_h
        dq = nt(ident, jnp.concatenate(dqs, 0).astype(BF)).astype(BF)
        dk = (dk * SCALE).astype(BF)
        dv = dv.astype(BF)
        s["g_col"][c] = (nt(dq, wq) + nt(dk, wk) + nt(dv, wv)).astype(BF)
        x_t = turned_wide(x, ident)
        for i, d in enumerate((dq, dk, dv)):
            s["gq_acc"][:, i * HALF : (i + 1) * HALF] += nn(x_t, d)

    from_columns(s["g_col"], s["g_wire"], join)
    g_swap.start()
    put_gq(s, HALF)
    gq = Scatter(p, s["gq"]["g"], s["gq"]["bufs"], s["gq"]["sems"])
    gwo = Scatter(p, s["gwo"]["g"], s["gwo"]["bufs"], s["gwo"]["sems"])
    gq.to_core()

    unwire = unwire_matrix()
    a_swap.arrived()
    s["gwo_acc"][...] = jnp.zeros_like(s["gwo_acc"])
    for b in range(4):
        x = s["a_got"][32 * b : 32 * b + 32]
        a = nn(unwire, x.reshape(256, HALF)).astype(BF)
        s["gwo_acc"][...] += nn(turned(a, ident), block_of(grads, b))
        s["att_col"][0, 128 * b : 128 * b + 128] = a[:128]
        s["att_col"][1, 128 * b : 128 * b + 128] = a[128:]
    put_gwo(s, 1)
    gwo.to_core()
    gq.to_x()
    for r in range(2):
        out[r] = (nn(s["att_row"][r], wo[:HALF]) + nn(s["att_col"][r], wo[HALF:])).astype(BF)
    gwo.to_x()
    gq.to_y()
    gwo.to_y()
    gq.to_z()
    gwo.to_z()
    gq.to_mate()
    gwo.to_mate()
    gq_out[...] = gq.result()
    gwo_out[...] = gwo.result()

    g_swap.arrived()
    for b in range(4):
        x = s["g_got"][32 * b : 32 * b + 32]
        g = nn(unwire, x.reshape(256, 512))
        for r in range(2):
            rows = slice(128 * b, 128 * b + 128)
            gf_out[r, rows] = (s["gf_row"][r, rows] + g[128 * r : 128 * r + 128]).astype(BF)
    for swap in (f_swap, d_swap, a_swap, g_swap):
        swap.gone()


def on_device(features, w_qkv, w_out, layout, grad_out):
    n_clips, n_rows, length, width = features.shape
    n_ctx = lax.axis_size("ctx")
    vm = pl.BlockSpec(memory_space=pltpu.VMEM)
    vmem = pltpu.VMEM
    scratch = dict(
        f_wire=vmem((n_ctx, 8, 512), BF),
        f_got=vmem((n_ctx, 8, 512), BF),
        d_wire=vmem((n_ctx, 8, 256), BF),
        d_got=vmem((n_ctx, 8, 256), BF),
        a_wire=vmem((n_ctx, 8, 256), BF),
        a_got=vmem((n_ctx, 8, 256), BF),
        g_wire=vmem((n_ctx, 8, 512), BF),
        g_got=vmem((n_ctx, 8, 512), BF),
        swap=pltpu.SemaphoreType.DMA((8,)),
        dk=vmem((512, 256), F32),
        dv=vmem((512, 256), F32),
        att_row=vmem((2, 512, 256), BF),
        att_col=vmem((2, 512, 256), BF),
        gf_row=vmem((2, 512, 512), F32),
        gq_acc=vmem((512, 768), F32),
        gwo_acc=vmem((256, 512), F32),
        f_col=vmem((4, 256, 512), BF),
        d_col=vmem((4, 256, 256), BF),
        a_col=vmem((4, 256, 256), BF),
        g_col=vmem((4, 256, 512), BF),
        q=vmem((4, 256, 256), BF),
        k=vmem((4, 256, 256), BF),
        v=vmem((4, 256, 256), BF),
        probs=vmem((4, 4, 256, 256), F32),
        gq=scatter_scratch(1536),
        gwo=scatter_scratch(512),
    )
    flat, tree = jax.tree.flatten(scratch, is_leaf=lambda x: not isinstance(x, (dict, list)))
    n_out = 4

    def kernel(lay, feats, grads, w, wo, *rest):
        outs, refs = rest[:n_out], rest[n_out:]
        whole_kernel(lay, feats, grads, w, wo, *outs, jax.tree.unflatten(tree, refs))

    shape = (n_rows, length, width)
    out, gf, gq, gwo = pl.pallas_call(
        kernel,
        out_shape=[
            jax.ShapeDtypeStruct(shape, BF),
            jax.ShapeDtypeStruct(shape, BF),
            jax.ShapeDtypeStruct((4, 1536), F32),
            jax.ShapeDtypeStruct((4, 512), F32),
        ],
        in_specs=[pl.BlockSpec(memory_space=pltpu.SMEM), vm, vm, vm, vm],
        out_specs=[vm] * n_out,
        scratch_shapes=flat,
        compiler_params=pltpu.CompilerParams(
            collective_id=1, has_side_effects=True, vmem_limit_bytes=VMEM_LIMIT
        ),
        name="whole_layer",
    )(layout, features.reshape(shape), grad_out.reshape(shape), w_qkv, w_out)
    full = (n_clips,) + shape
    return out.reshape(full), gf.reshape(full), gq, gwo


def solution(mesh):
    return jax.shard_map(
        on_device,
        mesh=mesh,
        in_specs=(P("dp", "ctx", None, None), P(), P(), P(), P("dp", "ctx", None, None)),
        out_specs=(
            P("dp", "ctx", None, None),
            P("dp", "ctx", None, None),
            P("ctx", None),
            P("ctx", None),
        ),
        check_vma=False,
    )
```

```python
import functools

import jax
import jax.numpy as jnp
from jax import lax
from jax.experimental import pallas as pl
from jax.experimental.pallas import tpu as pltpu
from jax.sharding import PartitionSpec as P

HEADS = 8
HEAD = 64
BLOCK = 128
HALF = 256
SCALE = HEAD**-0.5
NEG = -1e30
BF = jnp.bfloat16
F32 = jnp.float32
VMEM_LIMIT = 58 * 1024 * 1024
MESH = pl.DeviceIdType.MESH
N_Y, N_Z, N_X = 2, 8, 4
SCALE_LOG2E = SCALE * 1.4426950408889634


def nn(a, b):
    return jnp.dot(a, b, preferred_element_type=F32)


def nt(a, b):
    return lax.dot_general(a, b, (((1,), (1,)), ((), ())), preferred_element_type=F32)


def eye(n):
    r = lax.broadcasted_iota(jnp.int32, (n, n), 0)
    c = lax.broadcasted_iota(jnp.int32, (n, n), 1)
    return (r == c).astype(F32).astype(BF)


def turned(x, ident):
    return nt(ident, x).astype(BF)


def wire_matrix():
    t = lax.broadcasted_iota(jnp.int32, (256, 256), 0)
    k = lax.broadcasted_iota(jnp.int32, (256, 256), 1)
    src = ((t >> 2) & 1) * 128 + (t >> 3) * 4 + (t & 3)
    return (k == src).astype(F32).astype(BF)


def unwire_matrix():
    t = lax.broadcasted_iota(jnp.int32, (256, 256), 1)
    k = lax.broadcasted_iota(jnp.int32, (256, 256), 0)
    src = ((t >> 2) & 1) * 128 + (t >> 3) * 4 + (t & 3)
    return (k == src).astype(F32).astype(BF)


def column_matrix():
    t = lax.broadcasted_iota(jnp.int32, (256, 256), 0)
    k = lax.broadcasted_iota(jnp.int32, (256, 256), 1)
    return (k == (t & 63) * 4 + (t >> 6)).astype(F32).astype(BF)


def uncolumn_matrix():
    t = lax.broadcasted_iota(jnp.int32, (256, 256), 1)
    k = lax.broadcasted_iota(jnp.int32, (256, 256), 0)
    return (k == (t & 63) * 4 + (t >> 6)).astype(F32).astype(BF)


def lanes_of_head(x, h):
    c = lax.broadcasted_iota(jnp.int32, x.shape, 1)
    return jnp.where((c >> 6) == h, x, jnp.zeros_like(x))


def soften(pieces):
    high = pieces[0]
    for x in pieces[1:]:
        high = jnp.maximum(high, x)
    top = jnp.max(high, axis=0, keepdims=True)
    return [jnp.exp2((x - top) * SCALE_LOG2E).astype(BF) for x in pieces]


def stacked(pieces, n_keys):
    rest = n_keys - BLOCK * len(pieces)
    if rest:
        pieces = pieces + [jnp.zeros((rest, BLOCK), BF)]
    return jnp.concatenate(pieces, 0)


def padded(x, h):
    parts = [jnp.zeros((HEAD * h, x.shape[1]), BF)] if h else []
    parts.append(x)
    if h < 3:
        parts.append(jnp.zeros((HEAD * (3 - h), x.shape[1]), BF))
    return jnp.concatenate(parts, 0)


def with_ones(v_t):
    return jnp.concatenate([v_t, jnp.ones((16, v_t.shape[1]), BF)], 0)


def by_head(x):
    return jnp.concatenate([lanes_of_head(x, h) for h in range(4)], 0)


def head_rows(h):
    return slice(h * HEAD, (h + 1) * HEAD)


class Place:
    def __init__(self):
        self.dp = lax.axis_index("dp")
        self.ctx = lax.axis_index("ctx")
        self.core = self.ctx % 2
        self.x = (self.ctx // 2) % N_X
        self.z = (self.ctx // (2 * N_X)) % N_Z
        self.yh = self.ctx // (2 * N_X * N_Z)

    def at(self, yh=None, z=None, x=None, core=None, dp=None):
        yh = self.yh if yh is None else yh
        z = self.z if z is None else z
        x = self.x if x is None else x
        core = self.core if core is None else core
        dp = self.dp if dp is None else dp
        return (dp, ((yh * N_Z + z) * N_X + x) * 2 + core)


def remote(src, dst, send, recv, device):
    return pltpu.make_async_remote_copy(
        src_ref=src, dst_ref=dst, send_sem=send, recv_sem=recv, device_id=device, device_id_type=MESH
    )


class Scatter:
    def __init__(self, place, g, bufs, sems):
        self.place, self.g = place, g
        self.c, self.a, self.xb, self.b, self.yb, self.d, self.zb, self.e, self.last = bufs
        self.send, self.cs, self.xs, self.ys, self.zs, self.ls = sems
        self.half = g.shape[-1] // 2
        self.copies = []

    def launch(self, copies):
        for c in copies:
            c.start()
        self.copies = copies

    def arrive(self):
        for c in self.copies:
            c.wait()

    def to_core(self):
        p, half = self.place, self.half
        theirs = pl.ds(pl.multiple_of((1 - p.core) * half, 128), half)
        self.launch([
            remote(self.g.at[:, :, :, :, theirs], self.c, self.send.at[0], self.cs.at[0],
                   p.at(core=1 - p.core))
        ])

    def to_x(self):
        p, half = self.place, self.half
        self.arrive()
        mine = pl.ds(pl.multiple_of(p.core * half, 128), half)

        @pl.loop(0, N_Z)
        def _(zz):
            for yy in range(N_Y):
                self.a[:, yy, zz] = (
                    self.g[yy, zz, :, :, mine].astype(F32) + self.c[yy, zz].astype(F32)
                ).astype(BF)

        copies = []
        for s in range(1, N_X):
            to = (p.x + s) % N_X
            copies.append(remote(self.a.at[to], self.xb.at[s - 1], self.send.at[s],
                                 self.xs.at[s - 1], p.at(x=to)))
        self.launch(copies)

    def to_y(self):
        p = self.place
        self.arrive()

        @pl.loop(0, N_Y)
        def _(yy):
            total = self.a[p.x, yy].astype(F32)
            for s in range(N_X - 1):
                total = total + self.xb[s, yy].astype(F32)
            self.b[yy] = total.astype(BF)

        here = p.yh * 2 + p.dp
        copies = []
        for s in range(1, 4):
            to = (here + s) % 4
            copies.append(remote(self.b.at[to // 2], self.yb.at[here], self.send.at[3 + s],
                                 self.ys.at[s - 1], p.at(yh=to // 2, dp=to % 2)))
        self.launch(copies)
        self.yb[here] = self.b[p.yh]

    def to_z(self):
        p = self.place
        self.arrive()
        total = self.yb[0].astype(F32)
        for s in range(1, 4):
            total = total + self.yb[s].astype(F32)
        self.d[...] = total.astype(BF)
        copies = []
        for s in range(1, N_Z):
            to = (p.z + s) % N_Z
            copies.append(remote(self.d.at[to], self.zb.at[p.z], self.send.at[6 + s],
                                 self.zs.at[s - 1], p.at(z=to)))
        self.launch(copies)
        self.zb[p.z] = self.d[p.z]

    def to_mate(self):
        p = self.place
        self.arrive()
        total = self.zb[0].astype(F32)
        for s in range(1, N_Z):
            total = total + self.zb[s].astype(F32)
        self.e[...] = total
        self.launch([
            remote(self.e, self.last, self.send.at[6 + N_Z], self.ls.at[0], p.at(core=1 - p.core))
        ])

    def result(self):
        self.arrive()
        first = self.place.core == 0
        own, other = self.e[...], self.last[...]
        full = jnp.concatenate([jnp.where(first, own, other), jnp.where(first, other, own)], 1)
        return jnp.where(first, full[:4], full[4:])


def scatter_scratch(cols):
    half = cols // 2
    sem = pltpu.SemaphoreType.DMA
    bufs = [
        pltpu.VMEM((N_Y, N_Z, N_X, 8, half), BF),
        pltpu.VMEM((N_X, N_Y, N_Z, 8, half), BF),
        pltpu.VMEM((N_X - 1, N_Y, N_Z, 8, half), BF),
        pltpu.VMEM((N_Y, N_Z, 8, half), BF),
        pltpu.VMEM((4, N_Z, 8, half), BF),
        pltpu.VMEM((N_Z, 8, half), BF),
        pltpu.VMEM((N_Z, 8, half), BF),
        pltpu.VMEM((8, half), F32),
        pltpu.VMEM((8, half), F32),
    ]
    sems = [sem((7 + N_Z,)), sem((1,)), sem((N_X - 1,)), sem((3,)), sem((N_Z - 1,)), sem((1,))]
    return dict(g=pltpu.VMEM((N_Y, N_Z, N_X, 8, cols), BF), bufs=bufs, sems=sems)


class Swap:
    def __init__(self, place, src, dst, send, recv):
        self.place, self.src, self.dst, self.send, self.recv = place, src, dst, send, recv
        self.n = src.shape[0]

    def start(self):
        p, n = self.place, self.n

        def step(s, carry):
            to = (p.ctx + s) % n
            remote(self.src.at[to], self.dst.at[p.ctx], self.send, self.recv, (p.dp, to)).start()
            return carry

        lax.fori_loop(1, n, step, 0)
        self.dst[p.ctx] = self.src[p.ctx]

    def all_but_one(self, ref, sem):
        part = ref.at[pl.ds(0, self.n - 1)]
        pltpu.make_async_copy(part, part, sem).wait()

    def arrived(self):
        self.all_but_one(self.dst, self.recv)

    def gone(self):
        self.all_but_one(self.src, self.send)


def to_wire(ref, get, perm):
    for b in range(4):
        x = get(b)
        y = nn(perm, x).astype(BF)
        ref[32 * b : 32 * b + 32] = y.reshape(32, 8, y.shape[-1])


def block_of(ref, b):
    return jnp.concatenate([ref[r, 128 * b : 128 * b + 128] for r in range(2)], 0)


def to_columns(wire, col, perm):
    for b in range(4):
        x = wire[32 * b : 32 * b + 32]
        y = nn(perm, x.reshape(256, x.shape[-1])).astype(BF)
        for c in range(4):
            col[c, 64 * b : 64 * b + 64] = y[64 * c : 64 * c + 64]


def from_columns(col, wire, perm):
    for b in range(4):
        x = jnp.concatenate([col[c, 64 * b : 64 * b + 64] for c in range(4)], 0)
        y = nn(perm, x).astype(BF)
        wire[32 * b : 32 * b + 32] = y.reshape(32, 8, y.shape[-1])


def turned_wide(x, ident):
    return jnp.concatenate([turned(x[:, :256], ident), turned(x[:, 256:], ident)], 0)


def side_by_side(w, offset):
    return jnp.concatenate([w[:, i * 512 + offset : i * 512 + offset + HALF] for i in range(3)], 1)


def row_heads(s, r, lay, feats, grads, w, wo, ident):
    n = feats.shape[0]
    qkv = nn(feats, w).astype(BF)
    q_all, k_all, v_all = (qkv[:, i * HALF : (i + 1) * HALF] for i in range(3))
    d_t = nt(wo[:HALF], grads).astype(BF).astype(F32)
    q_t, k_t, v_t = (turned(x, ident) for x in (q_all, k_all, v_all))
    tri = lax.broadcasted_iota(jnp.int32, (BLOCK, BLOCK), 0) <= lax.broadcasted_iota(
        jnp.int32, (BLOCK, BLOCK), 1
    )
    chunks = []
    width = 2 * BLOCK
    for chunk in range(n // width):
        nj = (chunk + 1) * width
        cols = slice(chunk * width, (chunk + 1) * width)
        weights, ds_all, outs, dqs, dts_all = [], [], [], [], []
        for h in range(4):
            scores = nn(k_all[:nj], padded(q_t[head_rows(h), cols], h))
            blocks = []
            for half in range(2):
                ib = 2 * chunk + half
                lanes = slice(BLOCK * half, BLOCK * half + BLOCK)
                pieces = []
                for jb in range(ib):
                    bias = jnp.where(lay[h, ib, jb] == 1, 0.0, NEG)
                    pieces.append(scores[BLOCK * jb : BLOCK * jb + BLOCK, lanes] + bias)
                pieces.append(jnp.where(tri, scores[BLOCK * ib : BLOCK * ib + BLOCK, lanes], NEG))
                blocks.append(soften(pieces))
            wts = jnp.concatenate([stacked(x, nj) for x in blocks], 1)
            product = nn(with_ones(v_t[head_rows(h), :nj]), wts)
            inv = 1.0 / product[HEAD : HEAD + 1]
            out = product[:HEAD] * inv
            dts = (d_t[head_rows(h), cols] * inv).astype(BF)
            delta = jnp.sum(out * dts.astype(F32), axis=0, keepdims=True)
            d_prob = nn(v_all[:nj], padded(dts, h))
            ds_blocks = []
            for half in range(2):
                lanes = slice(BLOCK * half, BLOCK * half + BLOCK)
                ds_blocks.append([
                    (x.astype(F32) * (d_prob[BLOCK * j : BLOCK * j + BLOCK, lanes] - delta[:, lanes])).astype(BF)
                    for j, x in enumerate(blocks[half])
                ])
            ds = jnp.concatenate([stacked(x, nj) for x in ds_blocks], 1)
            dqs.append(nn(k_t[head_rows(h), :nj], ds) * SCALE)
            weights.append(wts)
            ds_all.append(ds)
            outs.append(out)
            dts_all.append(dts)
        att_t = jnp.concatenate(outs, 0).astype(BF)
        s["att_row_t"][r, :, cols] = att_t
        s["att_row"][r, cols] = nt(ident, att_t).astype(BF)
        dq = nt(ident, jnp.concatenate(dqs, 0).astype(BF)).astype(BF)
        chunks.append((
            jnp.concatenate(weights, 1), by_head(turned(jnp.concatenate(dts_all, 0), ident)),
            jnp.concatenate(ds_all, 1), by_head(q_all[cols]), dq,
        ))
    first, second = chunks
    dv_low = nn(second[0][:width], second[1]) + nn(first[0], first[1])
    dk_low = nn(second[2][:width], second[3]) + nn(first[2], first[3])
    dv = jnp.concatenate([dv_low, nn(second[0][width:], second[1])], 0).astype(BF)
    dk = (jnp.concatenate([dk_low, nn(second[2][width:], second[3])], 0) * SCALE).astype(BF)
    d_proj = jnp.concatenate([jnp.concatenate([first[4], second[4]], 0), dk, dv], 1)
    s["dp_row"][r] = d_proj
    s["gf_row"][r] = nt(d_proj, w)


def weight_grads(feats_t, d_proj, put):
    for i in range(3):
        put(i, nn(feats_t, d_proj[:, i * HALF : (i + 1) * HALF]).astype(BF))


def put_block(ref, i, part):
    ref[:, :, :, :, i * HALF : (i + 1) * HALF] = part.reshape(N_Y, N_Z, N_X, 8, HALF)


def col_forward(s, c, w, mask, ident):
    qkv = nn(s["f_col"][c], w).astype(BF)
    s["qkv"][c] = qkv
    q_all, k_all, v_all = (qkv[:, i * HALF : (i + 1) * HALF] for i in range(3))
    q_t, v_t = turned(q_all, ident), turned(v_all, ident)
    outs = []
    for h in range(4):
        scores = nn(k_all, padded(q_t[head_rows(h)], h))
        early = soften([jnp.where(mask, scores[:BLOCK, :BLOCK], NEG)])
        late = soften([scores[:BLOCK, BLOCK:], jnp.where(mask, scores[BLOCK:, BLOCK:], NEG)])
        wts = jnp.concatenate([stacked(early, 256), stacked(late, 256)], 1)
        s["wts"][c, :, 256 * h : 256 * h + 256] = wts
        product = nn(with_ones(v_t[head_rows(h)]), wts)
        inv = 1.0 / product[HEAD : HEAD + 1]
        s["inv"][c, h : h + 1] = inv
        outs.append(product[:HEAD] * inv)
    out = jnp.concatenate(outs, 0)
    s["o"][c] = out
    s["a_col"][c] = nt(ident, out.astype(BF)).astype(BF)


def col_backward(s, c, w, mask, ident):
    qkv = s["qkv"][c]
    q_all, k_all, v_all = (qkv[:, i * HALF : (i + 1) * HALF] for i in range(3))
    k_t, d_t = turned(k_all, ident), nt(ident, s["d_col"][c])
    dqs, dts_all, ds_all = [], [], []
    for h in range(4):
        dts = (d_t[head_rows(h)] * s["inv"][c, h : h + 1]).astype(BF)
        delta = jnp.sum(s["o"][c, head_rows(h)] * dts.astype(F32), axis=0, keepdims=True)
        d_prob = nn(v_all, padded(dts, h))

        def grad(j, i):
            rows, lanes = slice(BLOCK * j, BLOCK * j + BLOCK), slice(BLOCK * i, BLOCK * i + BLOCK)
            wts = s["wts"][c, rows, 256 * h + BLOCK * i : 256 * h + BLOCK * i + BLOCK]
            return (wts.astype(F32) * (d_prob[rows, lanes] - delta[:, lanes])).astype(BF)

        ds = jnp.concatenate([stacked([grad(0, 0)], 256), stacked([grad(0, 1), grad(1, 1)], 256)], 1)
        dqs.append(nn(k_t[head_rows(h)], ds) * SCALE)
        dts_all.append(dts)
        ds_all.append(ds)
    dq = nt(ident, jnp.concatenate(dqs, 0).astype(BF)).astype(BF)
    dv = nn(s["wts"][c], by_head(turned(jnp.concatenate(dts_all, 0), ident))).astype(BF)
    dk = (nn(jnp.concatenate(ds_all, 1), by_head(q_all)) * SCALE).astype(BF)
    d_proj = jnp.concatenate([dq, dk, dv], 1)
    s["dp_col"][c] = d_proj
    s["g_col"][c] = nt(d_proj, w).astype(BF)


def whole_kernel(lay, feats, grads, w, wo, out, gf_out, gq_out, gwo_out, s):
    p = Place()
    n_ctx = s["f_wire"].shape[0]
    barrier = pltpu.get_barrier_semaphore()

    def greet(step, carry):
        pl.semaphore_signal(
            barrier, inc=1, device_id=(p.dp, (p.ctx + step) % n_ctx), device_id_type=MESH
        )
        return carry

    lax.fori_loop(1, n_ctx, greet, 0)
    for yh in (p.yh, 1 - p.yh):
        pl.semaphore_signal(barrier, inc=1, device_id=p.at(yh=yh, dp=1 - p.dp), device_id_type=MESH)

    perm = wire_matrix()
    to_wire(s["f_wire"], lambda b: block_of(feats, b), perm)
    pl.semaphore_wait(barrier, n_ctx + 1)
    sems = s["swap"]
    f_swap = Swap(p, s["f_wire"], s["f_got"], sems.at[0], sems.at[1])
    d_swap = Swap(p, s["d_wire"], s["d_got"], sems.at[2], sems.at[3])
    a_swap = Swap(p, s["a_wire"], s["a_got"], sems.at[4], sems.at[5])
    g_swap = Swap(p, s["g_wire"], s["g_got"], sems.at[6], sems.at[7])
    f_swap.start()
    to_wire(s["d_wire"], lambda b: nt(block_of(grads, b), wo[HALF:]).astype(BF), perm)
    d_swap.start()

    ident = eye(256)
    s["w_row"][...] = side_by_side(w, 0)
    s["w_col"][...] = side_by_side(w, HALF)
    w_row, w_col = s["w_row"], s["w_col"]

    @pl.loop(0, 2)
    def _(r):
        row_heads(s, r, lay, feats[r], grads[r], w_row[...], wo, ident)

    gq_row, gq_col, gwo = (Scatter(p, s[k]["g"], s[k]["bufs"], s[k]["sems"]) for k in ("gq_row", "gq_col", "gwo"))
    feats_t = jnp.concatenate([turned_wide(feats[r], ident) for r in range(2)], 1)
    weight_grads(feats_t, s["dp_row"][...].reshape(1024, 768), lambda i, x: put_block(gq_row.g, i, x))
    gq_row.to_core()
    part = nn(s["att_row_t"][0], grads[0]) + nn(s["att_row_t"][1], grads[1])
    gwo.g[0] = part.astype(BF).reshape(N_Z, N_X, 8, 512)

    mask = lax.broadcasted_iota(jnp.int32, (BLOCK, BLOCK), 0) <= lax.broadcasted_iota(
        jnp.int32, (BLOCK, BLOCK), 1
    )
    split, join = column_matrix(), uncolumn_matrix()
    f_swap.arrived()
    to_columns(s["f_got"], s["f_col"], split)

    @pl.loop(0, 4)
    def _(c):
        col_forward(s, c, w_col[...], mask, ident)

    from_columns(s["a_col"], s["a_wire"], join)
    gq_row.to_x()
    a_swap.start()

    d_swap.arrived()
    to_columns(s["d_got"], s["d_col"], split)

    @pl.loop(0, 4)
    def _(c):
        col_backward(s, c, w_col[...], mask, ident)

    from_columns(s["g_col"], s["g_wire"], join)
    gq_row.to_y()
    g_swap.start()
    gq_row.to_z()
    feats_t = jnp.concatenate([turned_wide(s["f_col"][c], ident) for c in range(4)], 1)
    weight_grads(feats_t, s["dp_col"][...].reshape(1024, 768), lambda i, x: put_block(gq_col.g, i, x))
    gq_col.to_core()

    unwire = unwire_matrix()
    gq_row.to_mate()
    a_swap.arrived()
    part = None
    for b in range(4):
        x = s["a_got"][32 * b : 32 * b + 32]
        a = nn(unwire, x.reshape(256, HALF)).astype(BF)
        term = nn(turned(a, ident), block_of(grads, b))
        part = term if part is None else part + term
        s["att_col"][0, 128 * b : 128 * b + 128] = a[:128]
        s["att_col"][1, 128 * b : 128 * b + 128] = a[128:]
    gwo.g[1] = part.astype(BF).reshape(N_Z, N_X, 8, 512)
    gwo.to_core()
    gq_col.to_x()
    for r in range(2):
        both = jnp.concatenate([s["att_row"][r], s["att_col"][r]], 1)
        out[r] = nn(both, wo[...]).astype(BF)
    gwo.to_x()
    rows = gq_row.result()
    for i in range(3):
        gq_out[:, i * 512 : i * 512 + HALF] = rows[:, i * HALF : (i + 1) * HALF]
    gq_col.to_y()
    gwo.to_y()
    gq_col.to_z()
    gwo.to_z()
    gq_col.to_mate()
    gwo.to_mate()
    rows = gq_col.result()
    for i in range(3):
        gq_out[:, i * 512 + HALF : i * 512 + 512] = rows[:, i * HALF : (i + 1) * HALF]
    gwo_out[...] = gwo.result()

    g_swap.arrived()
    for b in range(4):
        x = s["g_got"][32 * b : 32 * b + 32]
        g = nn(unwire, x.reshape(256, 512))
        for r in range(2):
            rows = slice(128 * b, 128 * b + 128)
            gf_out[r, rows] = (s["gf_row"][r, rows] + g[128 * r : 128 * r + 128]).astype(BF)
    for swap in (f_swap, d_swap, a_swap, g_swap):
        swap.gone()


def on_device(features, w_qkv, w_out, layout, grad_out):
    n_clips, n_rows, length, width = features.shape
    n_ctx = lax.axis_size("ctx")
    vm = pl.BlockSpec(memory_space=pltpu.VMEM)
    vmem = pltpu.VMEM
    scratch = dict(
        f_wire=vmem((n_ctx, 8, 512), BF),
        f_got=vmem((n_ctx, 8, 512), BF),
        d_wire=vmem((n_ctx, 8, 256), BF),
        d_got=vmem((n_ctx, 8, 256), BF),
        a_wire=vmem((n_ctx, 8, 256), BF),
        a_got=vmem((n_ctx, 8, 256), BF),
        g_wire=vmem((n_ctx, 8, 512), BF),
        g_got=vmem((n_ctx, 8, 512), BF),
        swap=pltpu.SemaphoreType.DMA((8,)),
        w_row=vmem((512, 768), BF),
        w_col=vmem((512, 768), BF),
        att_row=vmem((2, 512, 256), BF),
        att_row_t=vmem((2, 256, 512), BF),
        att_col=vmem((2, 512, 256), BF),
        gf_row=vmem((2, 512, 512), F32),
        dp_row=vmem((2, 512, 768), BF),
        f_col=vmem((4, 256, 512), BF),
        d_col=vmem((4, 256, 256), BF),
        a_col=vmem((4, 256, 256), BF),
        g_col=vmem((4, 256, 512), BF),
        qkv=vmem((4, 256, 768), BF),
        wts=vmem((4, 256, 1024), BF),
        inv=vmem((4, 8, 256), F32),
        o=vmem((4, 256, 256), F32),
        dp_col=vmem((4, 256, 768), BF),
        gq_row=scatter_scratch(768),
        gq_col=scatter_scratch(768),
        gwo=scatter_scratch(512),
    )
    flat, tree = jax.tree.flatten(scratch, is_leaf=lambda x: not isinstance(x, (dict, list)))
    n_out = 4

    def kernel(lay, feats, grads, w, wo, *rest):
        outs, refs = rest[:n_out], rest[n_out:]
        whole_kernel(lay, feats, grads, w, wo, *outs, jax.tree.unflatten(tree, refs))

    shape = (n_rows, length, width)
    out, gf, gq, gwo = pl.pallas_call(
        kernel,
        out_shape=[
            jax.ShapeDtypeStruct(shape, BF),
            jax.ShapeDtypeStruct(shape, BF),
            jax.ShapeDtypeStruct((4, 1536), F32),
            jax.ShapeDtypeStruct((4, 512), F32),
        ],
        in_specs=[pl.BlockSpec(memory_space=pltpu.SMEM), vm, vm, vm, vm],
        out_specs=[vm] * n_out,
        scratch_shapes=flat,
        compiler_params=pltpu.CompilerParams(
            collective_id=1, has_side_effects=True, vmem_limit_bytes=VMEM_LIMIT
        ),
        name="whole_layer",
    )(layout, features.reshape(shape), grad_out.reshape(shape), w_qkv, w_out)
    full = (n_clips,) + shape
    return out.reshape(full), gf.reshape(full), gq, gwo


def solution(mesh):
    return jax.shard_map(
        on_device,
        mesh=mesh,
        in_specs=(P("dp", "ctx", None, None), P(), P(), P(), P("dp", "ctx", None, None)),
        out_specs=(
            P("dp", "ctx", None, None),
            P("dp", "ctx", None, None),
            P("ctx", None),
            P("ctx", None),
        ),
        check_vma=False,
    )
```

```python
import functools

import jax
import jax.numpy as jnp
from jax import lax
from jax.experimental import pallas as pl
from jax.experimental.pallas import tpu as pltpu
from jax.sharding import PartitionSpec as P

HEADS = 8
HEAD = 64
BLOCK = 128
HALF = 256
SCALE = HEAD**-0.5
NEG = -1e30
BF = jnp.bfloat16
F32 = jnp.float32
VMEM_LIMIT = 58*1024*1024
MESH = pl.DeviceIdType.MESH
N_Y, N_Z, N_X = 2, 8, 4
SCALE_LOG2E = SCALE * 1.4426950408889634


def nn(a, b):
    return jnp.dot(a, b, preferred_element_type=F32)


def nt(a, b):
    return lax.dot_general(a, b, (((1,), (1,)), ((), ())), preferred_element_type=F32)


def eye(n):
    r = lax.broadcasted_iota(jnp.int32, (n, n), 0)
    c = lax.broadcasted_iota(jnp.int32, (n, n), 1)
    return (r == c).astype(F32).astype(BF)


def turned(x, ident):
    return nt(ident, x).astype(BF)


def wire_matrix():
    t = lax.broadcasted_iota(jnp.int32, (256, 256), 0)
    k = lax.broadcasted_iota(jnp.int32, (256, 256), 1)
    src = ((t >> 2) & 1) * 128 + (t >> 3) * 4 + (t & 3)
    return (k == src).astype(F32).astype(BF)


def unwire_matrix():
    t = lax.broadcasted_iota(jnp.int32, (256, 256), 1)
    k = lax.broadcasted_iota(jnp.int32, (256, 256), 0)
    src = ((t >> 2) & 1) * 128 + (t >> 3) * 4 + (t & 3)
    return (k == src).astype(F32).astype(BF)


def column_matrix():
    t = lax.broadcasted_iota(jnp.int32, (256, 256), 0)
    k = lax.broadcasted_iota(jnp.int32, (256, 256), 1)
    return (k == (t & 63) * 4 + (t >> 6)).astype(F32).astype(BF)


def uncolumn_matrix():
    t = lax.broadcasted_iota(jnp.int32, (256, 256), 1)
    k = lax.broadcasted_iota(jnp.int32, (256, 256), 0)
    return (k == (t & 63) * 4 + (t >> 6)).astype(F32).astype(BF)


def lanes_of_head(x, h):
    c = lax.broadcasted_iota(jnp.int32, x.shape, 1)
    return jnp.where((c >> 6) == h, x, jnp.zeros_like(x))


def soften(pieces):
    high = pieces[0]
    for x in pieces[1:]:
        high = jnp.maximum(high, x)
    top = jnp.max(high, axis=0, keepdims=True)
    return [jnp.exp2((x - top) * SCALE_LOG2E).astype(BF) for x in pieces]


def stacked(pieces, n_keys):
    rest = n_keys - BLOCK * len(pieces)
    if rest:
        pieces = pieces + [jnp.zeros((rest, BLOCK), BF)]
    return jnp.concatenate(pieces, 0)


def padded(x, h):
    parts = [jnp.zeros((HEAD * h, x.shape[1]), BF)] if h else []
    parts.append(x)
    if h < 3:
        parts.append(jnp.zeros((HEAD * (3 - h), x.shape[1]), BF))
    return jnp.concatenate(parts, 0)


def with_ones(v_t):
    return jnp.concatenate([v_t, jnp.ones((16, v_t.shape[1]), BF)], 0)


def by_head(x):
    return jnp.concatenate([lanes_of_head(x, h) for h in range(4)], 0)


def head_rows(h):
    return slice(h * HEAD, (h + 1) * HEAD)


class Place:
    def __init__(self):
        self.dp = lax.axis_index("dp")
        self.ctx = lax.axis_index("ctx")
        self.core = self.ctx % 2
        self.x = (self.ctx // 2) % N_X
        self.z = (self.ctx // (2 * N_X)) % N_Z
        self.yh = self.ctx // (2 * N_X * N_Z)

    def at(self, yh=None, z=None, x=None, core=None, dp=None):
        yh = self.yh if yh is None else yh
        z = self.z if z is None else z
        x = self.x if x is None else x
        core = self.core if core is None else core
        dp = self.dp if dp is None else dp
        return (dp, ((yh * N_Z + z) * N_X + x) * 2 + core)


def remote(src, dst, send, recv, device):
    return pltpu.make_async_remote_copy(
        src_ref=src, dst_ref=dst, send_sem=send, recv_sem=recv, device_id=device, device_id_type=MESH
    )


class Scatter:
    def __init__(self, place, g, bufs, sems):
        self.place, self.g = place, g
        self.c, self.a, self.xb, self.b, self.yb, self.d, self.zb, self.e, self.last = bufs
        self.send, self.cs, self.xs, self.ys, self.zs, self.ls = sems
        self.half = g.shape[-1] // 2
        self.copies = []

    def launch(self, copies):
        for c in copies:
            c.start()
        self.copies = copies

    def arrive(self):
        for c in self.copies:
            c.wait()

    def to_core(self):
        p, half = self.place, self.half
        theirs = pl.ds(pl.multiple_of((1 - p.core) * half, 128), half)
        self.launch([
            remote(self.g.at[:, :, :, :, theirs], self.c, self.send.at[0], self.cs.at[0],
                   p.at(core=1 - p.core))
        ])

    def to_x(self):
        p, half = self.place, self.half
        self.arrive()
        mine = pl.ds(pl.multiple_of(p.core * half, 128), half)

        @pl.loop(0, N_Z)
        def _(zz):
            for yy in range(N_Y):
                self.a[:, yy, zz] = (
                    self.g[yy, zz, :, :, mine].astype(F32) + self.c[yy, zz].astype(F32)
                ).astype(BF)

        copies = []
        for s in range(1, N_X):
            to = (p.x + s) % N_X
            copies.append(remote(self.a.at[to], self.xb.at[s - 1], self.send.at[s],
                                 self.xs.at[s - 1], p.at(x=to)))
        self.launch(copies)

    def to_y(self):
        p = self.place
        self.arrive()

        @pl.loop(0, N_Y)
        def _(yy):
            total = self.a[p.x, yy].astype(F32)
            for s in range(N_X - 1):
                total = total + self.xb[s, yy].astype(F32)
            self.b[yy] = total.astype(BF)

        here = p.yh * 2 + p.dp
        copies = []
        for s in range(1, 4):
            to = (here + s) % 4
            copies.append(remote(self.b.at[to // 2], self.yb.at[here], self.send.at[3 + s],
                                 self.ys.at[s - 1], p.at(yh=to // 2, dp=to % 2)))
        self.launch(copies)
        self.yb[here] = self.b[p.yh]

    def to_z(self):
        p = self.place
        self.arrive()
        total = self.yb[0].astype(F32)
        for s in range(1, 4):
            total = total + self.yb[s].astype(F32)
        self.d[...] = total.astype(BF)
        copies = []
        for s in range(1, N_Z):
            to = (p.z + s) % N_Z
            copies.append(remote(self.d.at[to], self.zb.at[p.z], self.send.at[6 + s],
                                 self.zs.at[s - 1], p.at(z=to)))
        self.launch(copies)
        self.zb[p.z] = self.d[p.z]

    def to_mate(self):
        p = self.place
        self.arrive()
        total = self.zb[0].astype(F32)
        for s in range(1, N_Z):
            total = total + self.zb[s].astype(F32)
        self.e[...] = total
        self.launch([
            remote(self.e, self.last, self.send.at[6 + N_Z], self.ls.at[0], p.at(core=1 - p.core))
        ])

    def result(self):
        self.arrive()
        first = self.place.core == 0
        own, other = self.e[...], self.last[...]
        full = jnp.concatenate([jnp.where(first, own, other), jnp.where(first, other, own)], 1)
        return jnp.where(first, full[:4], full[4:])


def scatter_scratch(cols):
    half = cols // 2
    sem = pltpu.SemaphoreType.DMA
    bufs = [
        pltpu.VMEM((N_Y, N_Z, N_X, 8, half), BF),
        pltpu.VMEM((N_X, N_Y, N_Z, 8, half), BF),
        pltpu.VMEM((N_X - 1, N_Y, N_Z, 8, half), BF),
        pltpu.VMEM((N_Y, N_Z, 8, half), BF),
        pltpu.VMEM((4, N_Z, 8, half), BF),
        pltpu.VMEM((N_Z, 8, half), BF),
        pltpu.VMEM((N_Z, 8, half), BF),
        pltpu.VMEM((8, half), F32),
        pltpu.VMEM((8, half), F32),
    ]
    sems = [sem((7 + N_Z,)), sem((1,)), sem((N_X - 1,)), sem((3,)), sem((N_Z - 1,)), sem((1,))]
    return dict(g=pltpu.VMEM((N_Y, N_Z, N_X, 8, cols), BF), bufs=bufs, sems=sems)


class Swap:
    def __init__(self, place, src, dst, send, recv):
        self.place, self.src, self.dst, self.send, self.recv = place, src, dst, send, recv
        self.n = src.shape[0]

    def start(self):
        p, n = self.place, self.n

        def step(s, carry):
            to = (p.ctx + s) % n
            remote(self.src.at[to], self.dst.at[p.ctx], self.send, self.recv, (p.dp, to)).start()
            return carry

        lax.fori_loop(1, n, step, 0)
        self.dst[p.ctx] = self.src[p.ctx]

    def all_but_one(self, ref, sem):
        part = ref.at[pl.ds(0, self.n - 1)]
        pltpu.make_async_copy(part, part, sem).wait()

    def arrived(self):
        self.all_but_one(self.dst, self.recv)

    def gone(self):
        self.all_but_one(self.src, self.send)


def to_wire(ref, get, perm):
    for b in range(4):
        x = get(b)
        y = nn(perm, x).astype(BF)
        ref[32 * b : 32 * b + 32] = y.reshape(32, 8, y.shape[-1])


def block_of(ref, b):
    return jnp.concatenate([ref[r, 128 * b : 128 * b + 128] for r in range(2)], 0)


def to_columns(wire, col, perm):
    for b in range(4):
        x = wire[32 * b : 32 * b + 32]
        y = nn(perm, x.reshape(256, x.shape[-1])).astype(BF)
        for c in range(4):
            col[c, 64 * b : 64 * b + 64] = y[64 * c : 64 * c + 64]


def from_columns(col, wire, perm):
    for b in range(4):
        x = jnp.concatenate([col[c, 64 * b : 64 * b + 64] for c in range(4)], 0)
        y = nn(perm, x).astype(BF)
        wire[32 * b : 32 * b + 32] = y.reshape(32, 8, y.shape[-1])


def turned_wide(x, ident):
    return jnp.concatenate([turned(x[:, :256], ident), turned(x[:, 256:], ident)], 0)


def side_by_side(w, offset):
    return jnp.concatenate([w[:, i * 512 + offset : i * 512 + offset + HALF] for i in range(3)], 1)


def row_heads(s, r, lay, feats, grads, w, wo, ident):
    n = feats.shape[0]
    qkv = nn(feats, w).astype(BF)
    q_all, k_all, v_all = (qkv[:, i * HALF : (i + 1) * HALF] for i in range(3))
    d_t = nt(wo[:HALF], grads).astype(BF).astype(F32)
    q_t, k_t, v_t = (turned(x, ident) for x in (q_all, k_all, v_all))
    tri = lax.broadcasted_iota(jnp.int32, (BLOCK, BLOCK), 0) <= lax.broadcasted_iota(
        jnp.int32, (BLOCK, BLOCK), 1
    )
    chunks = []
    width = 2 * BLOCK
    for chunk in range(n // width):
        nj = (chunk + 1) * width
        cols = slice(chunk * width, (chunk + 1) * width)
        weights, ds_all, outs, dqs, dts_all = [], [], [], [], []
        for h in range(4):
            scores = nn(k_all[:nj], padded(q_t[head_rows(h), cols], h))
            blocks = []
            for half in range(2):
                ib = 2 * chunk + half
                lanes = slice(BLOCK * half, BLOCK * half + BLOCK)
                pieces = []
                for jb in range(ib):
                    bias = jnp.where(lay[h, ib, jb] == 1, 0.0, NEG)
                    pieces.append(scores[BLOCK * jb : BLOCK * jb + BLOCK, lanes] + bias)
                pieces.append(jnp.where(tri, scores[BLOCK * ib : BLOCK * ib + BLOCK, lanes], NEG))
                blocks.append(soften(pieces))
            wts = jnp.concatenate([stacked(x, nj) for x in blocks], 1)
            product = nn(with_ones(v_t[head_rows(h), :nj]), wts)
            inv = 1.0 / product[HEAD : HEAD + 1]
            out = product[:HEAD] * inv
            dts = (d_t[head_rows(h), cols] * inv).astype(BF)
            delta = jnp.sum(out * dts.astype(F32), axis=0, keepdims=True)
            d_prob = nn(v_all[:nj], padded(dts, h))
            ds_blocks = []
            for half in range(2):
                lanes = slice(BLOCK * half, BLOCK * half + BLOCK)
                ds_blocks.append([
                    (x.astype(F32) * (d_prob[BLOCK * j : BLOCK * j + BLOCK, lanes] - delta[:, lanes])).astype(BF)
                    for j, x in enumerate(blocks[half])
                ])
            ds = jnp.concatenate([stacked(x, nj) for x in ds_blocks], 1)
            dqs.append(nn(k_t[head_rows(h), :nj], ds) * SCALE)
            weights.append(wts)
            ds_all.append(ds)
            outs.append(out)
            dts_all.append(dts)
        att_t = jnp.concatenate(outs, 0).astype(BF)
        s["att_row_t"][r, :, cols] = att_t
        s["att_row"][r, cols] = nt(ident, att_t).astype(BF)
        dq = nt(ident, jnp.concatenate(dqs, 0).astype(BF)).astype(BF)
        chunks.append((
            jnp.concatenate(weights, 1), by_head(turned(jnp.concatenate(dts_all, 0), ident)),
            jnp.concatenate(ds_all, 1), by_head(q_all[cols]), dq,
        ))
    first, second = chunks
    dv_low = nn(second[0][:width], second[1]) + nn(first[0], first[1])
    dk_low = nn(second[2][:width], second[3]) + nn(first[2], first[3])
    dv = jnp.concatenate([dv_low, nn(second[0][width:], second[1])], 0).astype(BF)
    dk = (jnp.concatenate([dk_low, nn(second[2][width:], second[3])], 0) * SCALE).astype(BF)
    d_proj = jnp.concatenate([jnp.concatenate([first[4], second[4]], 0), dk, dv], 1)
    s["dp_row"][r] = d_proj
    s["gf_row"][r] = nt(d_proj, w)


def weight_grads(feats_t, d_proj, put):
    for i in range(3):
        put(i, nn(feats_t, d_proj[:, i * HALF : (i + 1) * HALF]).astype(BF))


def put_block(ref, i, part):
    ref[:, :, :, :, i * HALF : (i + 1) * HALF] = part.reshape(N_Y, N_Z, N_X, 8, HALF)


def col_forward(s, c, w, mask, ident):
    qkv = nn(s["f_col"][c], w).astype(BF)
    s["qkv"][c] = qkv
    q_all, k_all, v_all = (qkv[:, i * HALF : (i + 1) * HALF] for i in range(3))
    q_t, v_t = turned(q_all, ident), turned(v_all, ident)
    outs = []
    for h in range(4):
        scores = nn(k_all, padded(q_t[head_rows(h)], h))
        early = soften([jnp.where(mask, scores[:BLOCK, :BLOCK], NEG)])
        late = soften([scores[:BLOCK, BLOCK:], jnp.where(mask, scores[BLOCK:, BLOCK:], NEG)])
        wts = jnp.concatenate([stacked(early, 256), stacked(late, 256)], 1)
        s["wts"][c, :, 256 * h : 256 * h + 256] = wts
        product = nn(with_ones(v_t[head_rows(h)]), wts)
        inv = 1.0 / product[HEAD : HEAD + 1]
        s["inv"][c, h : h + 1] = inv
        outs.append(product[:HEAD] * inv)
    out = jnp.concatenate(outs, 0)
    s["o"][c] = out
    s["a_col"][c] = nt(ident, out.astype(BF)).astype(BF)


def col_backward(s, c, w, mask, ident):
    qkv = s["qkv"][c]
    q_all, k_all, v_all = (qkv[:, i * HALF : (i + 1) * HALF] for i in range(3))
    k_t, d_t = turned(k_all, ident), nt(ident, s["d_col"][c])
    dqs, dts_all, ds_all = [], [], []
    for h in range(4):
        dts = (d_t[head_rows(h)] * s["inv"][c, h : h + 1]).astype(BF)
        delta = jnp.sum(s["o"][c, head_rows(h)] * dts.astype(F32), axis=0, keepdims=True)
        d_prob = nn(v_all, padded(dts, h))

        def grad(j, i):
            rows, lanes = slice(BLOCK * j, BLOCK * j + BLOCK), slice(BLOCK * i, BLOCK * i + BLOCK)
            wts = s["wts"][c, rows, 256 * h + BLOCK * i : 256 * h + BLOCK * i + BLOCK]
            return (wts.astype(F32) * (d_prob[rows, lanes] - delta[:, lanes])).astype(BF)

        ds = jnp.concatenate([stacked([grad(0, 0)], 256), stacked([grad(0, 1), grad(1, 1)], 256)], 1)
        dqs.append(nn(k_t[head_rows(h)], ds) * SCALE)
        dts_all.append(dts)
        ds_all.append(ds)
    dq = nt(ident, jnp.concatenate(dqs, 0).astype(BF)).astype(BF)
    dv = nn(s["wts"][c], by_head(turned(jnp.concatenate(dts_all, 0), ident))).astype(BF)
    dk = (nn(jnp.concatenate(ds_all, 1), by_head(q_all)) * SCALE).astype(BF)
    d_proj = jnp.concatenate([dq, dk, dv], 1)
    s["dp_col"][c] = d_proj
    s["g_col"][c] = nt(d_proj, w).astype(BF)


def whole_kernel(lay, feats_in, grads_in, w_in, wo_in, out, gf_out, gq_out, gwo_out, s):
    p = Place()
    feats, grads, w, wo = s["feats"], s["grads"], s["w"], s["wo"]
    loads = [
        pltpu.make_async_copy(src, dst, s["loads"].at[i])
        for i, (src, dst) in enumerate(((feats_in, feats), (wo_in, wo), (grads_in, grads), (w_in, w)))
    ]
    for load in loads:
        load.start()
    n_ctx = s["f_wire"].shape[0]
    barrier = pltpu.get_barrier_semaphore()

    def greet(step, carry):
        pl.semaphore_signal(
            barrier, inc=1, device_id=(p.dp, (p.ctx + step) % n_ctx), device_id_type=MESH
        )
        return carry

    lax.fori_loop(1, n_ctx, greet, 0)
    for yh in (p.yh, 1 - p.yh):
        pl.semaphore_signal(barrier, inc=1, device_id=p.at(yh=yh, dp=1 - p.dp), device_id_type=MESH)

    perm = wire_matrix()
    loads[0].wait()
    to_wire(s["f_wire"], lambda b: block_of(feats, b), perm)
    pl.semaphore_wait(barrier, n_ctx + 1)
    sems = s["swap"]
    f_swap = Swap(p, s["f_wire"], s["f_got"], sems.at[0], sems.at[1])
    d_swap = Swap(p, s["d_wire"], s["d_got"], sems.at[2], sems.at[3])
    a_swap = Swap(p, s["a_wire"], s["a_got"], sems.at[4], sems.at[5])
    g_swap = Swap(p, s["g_wire"], s["g_got"], sems.at[6], sems.at[7])
    f_swap.start()
    for load in loads[1:]:
        load.wait()
    to_wire(s["d_wire"], lambda b: nt(block_of(grads, b), wo[HALF:]).astype(BF), perm)
    d_swap.start()

    ident = eye(256)
    s["w_row"][...] = side_by_side(w, 0)
    s["w_col"][...] = side_by_side(w, HALF)
    w_row, w_col = s["w_row"], s["w_col"]

    @pl.loop(0, 2)
    def _(r):
        row_heads(s, r, lay, feats[r], grads[r], w_row[...], wo, ident)

    gq_row, gq_col, gwo = (Scatter(p, s[k]["g"], s[k]["bufs"], s[k]["sems"]) for k in ("gq_row", "gq_col", "gwo"))
    feats_t = jnp.concatenate([turned_wide(feats[r], ident) for r in range(2)], 1)
    weight_grads(feats_t, s["dp_row"][...].reshape(1024, 768), lambda i, x: put_block(gq_row.g, i, x))
    gq_row.to_core()
    part = nn(s["att_row_t"][0], grads[0]) + nn(s["att_row_t"][1], grads[1])
    gwo.g[0] = part.astype(BF).reshape(N_Z, N_X, 8, 512)

    mask = lax.broadcasted_iota(jnp.int32, (BLOCK, BLOCK), 0) <= lax.broadcasted_iota(
        jnp.int32, (BLOCK, BLOCK), 1
    )
    split, join = column_matrix(), uncolumn_matrix()
    f_swap.arrived()
    to_columns(s["f_got"], s["f_col"], split)

    @pl.loop(0, 4)
    def _(c):
        col_forward(s, c, w_col[...], mask, ident)

    from_columns(s["a_col"], s["a_wire"], join)
    a_swap.start()
    gq_row.to_x()

    d_swap.arrived()
    to_columns(s["d_got"], s["d_col"], split)

    @pl.loop(0, 4)
    def _(c):
        col_backward(s, c, w_col[...], mask, ident)

    from_columns(s["g_col"], s["g_wire"], join)
    g_swap.start()
    gq_row.to_y()
    feats_t = jnp.concatenate([turned_wide(s["f_col"][c], ident) for c in range(4)], 1)
    weight_grads(feats_t, s["dp_col"][...].reshape(1024, 768), lambda i, x: put_block(gq_col.g, i, x))
    gq_col.to_core()

    unwire = unwire_matrix()
    a_swap.arrived()
    part = None
    for b in range(4):
        x = s["a_got"][32 * b : 32 * b + 32]
        a = nn(unwire, x.reshape(256, HALF)).astype(BF)
        term = nn(turned(a, ident), block_of(grads, b))
        part = term if part is None else part + term
        s["att_col"][0, 128 * b : 128 * b + 128] = a[:128]
        s["att_col"][1, 128 * b : 128 * b + 128] = a[128:]
    gwo.g[1] = part.astype(BF).reshape(N_Z, N_X, 8, 512)
    gwo.to_core()
    gq_col.to_x()
    for r in range(2):
        both = jnp.concatenate([s["att_row"][r], s["att_col"][r]], 1)
        out[r] = nn(both, wo[...]).astype(BF)
    gwo.to_x()
    gq_row.to_z()
    gq_col.to_y()
    gwo.to_y()
    gq_col.to_z()
    gwo.to_z()

    g_swap.arrived()
    for kind in (gq_row, gq_col, gwo):
        kind.to_mate()
    for b in range(4):
        x = s["g_got"][32 * b : 32 * b + 32]
        g = nn(unwire, x.reshape(256, 512))
        for r in range(2):
            rows = slice(128 * b, 128 * b + 128)
            gf_out[r, rows] = (s["gf_row"][r, rows] + g[128 * r : 128 * r + 128]).astype(BF)
    for swap in (f_swap, d_swap, a_swap, g_swap):
        swap.gone()
    for offset, kind in ((0, gq_row), (HALF, gq_col)):
        rows = kind.result()
        for i in range(3):
            gq_out[:, i * 512 + offset : i * 512 + offset + HALF] = rows[:, i * HALF : (i + 1) * HALF]
    gwo_out[...] = gwo.result()


def on_device(features, w_qkv, w_out, layout, grad_out):
    n_clips, n_rows, length, width = features.shape
    n_ctx = lax.axis_size("ctx")
    vm = pl.BlockSpec(memory_space=pltpu.VMEM)
    vmem = pltpu.VMEM
    scratch = dict(
        f_wire=vmem((n_ctx, 8, 512), BF),
        f_got=vmem((n_ctx, 8, 512), BF),
        d_wire=vmem((n_ctx, 8, 256), BF),
        d_got=vmem((n_ctx, 8, 256), BF),
        a_wire=vmem((n_ctx, 8, 256), BF),
        a_got=vmem((n_ctx, 8, 256), BF),
        g_wire=vmem((n_ctx, 8, 512), BF),
        g_got=vmem((n_ctx, 8, 512), BF),
        swap=pltpu.SemaphoreType.DMA((8,)),
        feats=vmem((2, 512, 512), BF),
        grads=vmem((2, 512, 512), BF),
        w=vmem((512, 1536), BF),
        wo=vmem((512, 512), BF),
        loads=pltpu.SemaphoreType.DMA((4,)),
        w_row=vmem((512, 768), BF),
        w_col=vmem((512, 768), BF),
        att_row=vmem((2, 512, 256), BF),
        att_row_t=vmem((2, 256, 512), BF),
        att_col=vmem((2, 512, 256), BF),
        gf_row=vmem((2, 512, 512), F32),
        dp_row=vmem((2, 512, 768), BF),
        f_col=vmem((4, 256, 512), BF),
        d_col=vmem((4, 256, 256), BF),
        a_col=vmem((4, 256, 256), BF),
        g_col=vmem((4, 256, 512), BF),
        qkv=vmem((4, 256, 768), BF),
        wts=vmem((4, 256, 1024), BF),
        inv=vmem((4, 8, 256), F32),
        o=vmem((4, 256, 256), F32),
        dp_col=vmem((4, 256, 768), BF),
        gq_row=scatter_scratch(768),
        gq_col=scatter_scratch(768),
        gwo=scatter_scratch(512),
    )
    flat, tree = jax.tree.flatten(scratch, is_leaf=lambda x: not isinstance(x, (dict, list)))
    n_out = 4

    def kernel(lay, feats, grads, w, wo, *rest):
        outs, refs = rest[:n_out], rest[n_out:]
        whole_kernel(lay, feats, grads, w, wo, *outs, jax.tree.unflatten(tree, refs))

    shape = (n_rows, length, width)
    out, gf, gq, gwo = pl.pallas_call(
        kernel,
        out_shape=[
            jax.ShapeDtypeStruct(shape, BF),
            jax.ShapeDtypeStruct(shape, BF),
            jax.ShapeDtypeStruct((4, 1536), F32),
            jax.ShapeDtypeStruct((4, 512), F32),
        ],
        in_specs=[pl.BlockSpec(memory_space=pltpu.SMEM)] + [pl.BlockSpec(memory_space=pltpu.HBM)] * 4,
        out_specs=[vm] * n_out,
        scratch_shapes=flat,
        compiler_params=pltpu.CompilerParams(
            collective_id=1, has_side_effects=True, vmem_limit_bytes=VMEM_LIMIT
        ),
        name="whole_layer",
    )(layout, features.reshape(shape), grad_out.reshape(shape), w_qkv, w_out)
    full = (n_clips,) + shape
    return out.reshape(full), gf.reshape(full), gq, gwo


def solution(mesh):
    return jax.shard_map(
        on_device,
        mesh=mesh,
        in_specs=(P("dp", "ctx", None, None), P(), P(), P(), P("dp", "ctx", None, None)),
        out_specs=(
            P("dp", "ctx", None, None),
            P("dp", "ctx", None, None),
            P("ctx", None),
            P("ctx", None),
        ),
        check_vma=False,
    )
```

```python
import functools

import jax
import jax.numpy as jnp
from jax import lax
from jax.experimental import pallas as pl
from jax.experimental.pallas import tpu as pltpu
from jax.sharding import PartitionSpec as P

HEADS = 8
HEAD = 64
BLOCK = 128
HALF = 256
SCALE = HEAD**-0.5
NEG = -1e30
BF = jnp.bfloat16
F32 = jnp.float32
VMEM_LIMIT = 40 * 1024 * 1024
MESH = pl.DeviceIdType.MESH
N_Y, N_Z, N_X = 2, 8, 4
SCALE_LOG2E = SCALE * 1.4426950408889634


def nn(a, b):
    return jnp.dot(a, b, preferred_element_type=F32)


def nt(a, b):
    return lax.dot_general(a, b, (((1,), (1,)), ((), ())), preferred_element_type=F32)


def eye(n):
    r = lax.broadcasted_iota(jnp.int32, (n, n), 0)
    c = lax.broadcasted_iota(jnp.int32, (n, n), 1)
    return (r == c).astype(F32).astype(BF)


def turned(x, ident):
    return nt(ident, x).astype(BF)


def wire_matrix():
    t = lax.broadcasted_iota(jnp.int32, (256, 256), 0)
    k = lax.broadcasted_iota(jnp.int32, (256, 256), 1)
    src = ((t >> 2) & 1) * 128 + (t >> 3) * 4 + (t & 3)
    return (k == src).astype(F32).astype(BF)


def unwire_matrix():
    t = lax.broadcasted_iota(jnp.int32, (256, 256), 1)
    k = lax.broadcasted_iota(jnp.int32, (256, 256), 0)
    src = ((t >> 2) & 1) * 128 + (t >> 3) * 4 + (t & 3)
    return (k == src).astype(F32).astype(BF)


def column_matrix():
    t = lax.broadcasted_iota(jnp.int32, (256, 256), 0)
    k = lax.broadcasted_iota(jnp.int32, (256, 256), 1)
    return (k == (t & 63) * 4 + (t >> 6)).astype(F32).astype(BF)


def uncolumn_matrix():
    t = lax.broadcasted_iota(jnp.int32, (256, 256), 1)
    k = lax.broadcasted_iota(jnp.int32, (256, 256), 0)
    return (k == (t & 63) * 4 + (t >> 6)).astype(F32).astype(BF)


def lanes_of_head(x, h):
    c = lax.broadcasted_iota(jnp.int32, x.shape, 1)
    return jnp.where((c >> 6) == h, x, jnp.zeros_like(x))


def soften(pieces):
    high = pieces[0]
    for x in pieces[1:]:
        high = jnp.maximum(high, x)
    top = jnp.max(high, axis=0, keepdims=True)
    return [jnp.exp2((x - top) * SCALE_LOG2E).astype(BF) for x in pieces]


def stacked(pieces, n_keys):
    rest = n_keys - BLOCK * len(pieces)
    if rest:
        pieces = pieces + [jnp.zeros((rest, BLOCK), BF)]
    return jnp.concatenate(pieces, 0)


def padded(x, h):
    parts = [jnp.zeros((HEAD * h, x.shape[1]), BF)] if h else []
    parts.append(x)
    if h < 3:
        parts.append(jnp.zeros((HEAD * (3 - h), x.shape[1]), BF))
    return jnp.concatenate(parts, 0)


def with_ones(v_t):
    return jnp.concatenate([v_t, jnp.ones((16, v_t.shape[1]), BF)], 0)


def by_head(x):
    return jnp.concatenate([lanes_of_head(x, h) for h in range(4)], 0)


def head_rows(h):
    return slice(h * HEAD, (h + 1) * HEAD)


class Place:
    def __init__(self):
        self.dp = lax.axis_index("dp")
        self.ctx = lax.axis_index("ctx")
        self.core = self.ctx % 2
        self.x = (self.ctx // 2) % N_X
        self.z = (self.ctx // (2 * N_X)) % N_Z
        self.yh = self.ctx // (2 * N_X * N_Z)

    def at(self, yh=None, z=None, x=None, core=None, dp=None):
        yh = self.yh if yh is None else yh
        z = self.z if z is None else z
        x = self.x if x is None else x
        core = self.core if core is None else core
        dp = self.dp if dp is None else dp
        return (dp, ((yh * N_Z + z) * N_X + x) * 2 + core)


def remote(src, dst, send, recv, device):
    return pltpu.make_async_remote_copy(
        src_ref=src, dst_ref=dst, send_sem=send, recv_sem=recv, device_id=device, device_id_type=MESH
    )


class Scatter:
    def __init__(self, place, g, bufs, sems):
        self.place, self.g = place, g
        self.c, self.a, self.xb, self.b, self.yb, self.d, self.zb, self.e, self.last = bufs
        self.send, self.cs, self.xs, self.ys, self.zs, self.ls = sems
        self.half = g.shape[-1] // 2
        self.copies = []

    def launch(self, copies):
        for c in copies:
            c.start()
        self.copies = copies

    def arrive(self):
        for c in self.copies:
            c.wait()

    def to_core(self):
        p, half = self.place, self.half
        theirs = pl.ds(pl.multiple_of((1 - p.core) * half, 128), half)
        self.launch([
            remote(self.g.at[:, :, :, :, theirs], self.c, self.send.at[0], self.cs.at[0],
                   p.at(core=1 - p.core))
        ])

    def to_x(self):
        p, half = self.place, self.half
        self.arrive()
        mine = pl.ds(pl.multiple_of(p.core * half, 128), half)

        @pl.loop(0, N_Z)
        def _(zz):
            for yy in range(N_Y):
                self.a[:, yy, zz] = (
                    self.g[yy, zz, :, :, mine].astype(F32) + self.c[yy, zz].astype(F32)
                ).astype(BF)

        copies = []
        for s in range(1, N_X):
            to = (p.x + s) % N_X
            copies.append(remote(self.a.at[to], self.xb.at[s - 1], self.send.at[s],
                                 self.xs.at[s - 1], p.at(x=to)))
        self.launch(copies)

    def to_y(self):
        p = self.place
        self.arrive()

        @pl.loop(0, N_Y)
        def _(yy):
            total = self.a[p.x, yy].astype(F32)
            for s in range(N_X - 1):
                total = total + self.xb[s, yy].astype(F32)
            self.b[yy] = total.astype(BF)

        here = p.yh * 2 + p.dp
        copies = []
        for s in range(1, 4):
            to = (here + s) % 4
            copies.append(remote(self.b.at[to // 2], self.yb.at[here], self.send.at[3 + s],
                                 self.ys.at[s - 1], p.at(yh=to // 2, dp=to % 2)))
        self.launch(copies)
        self.yb[here] = self.b[p.yh]

    def to_z(self):
        p = self.place
        self.arrive()
        total = self.yb[0].astype(F32)
        for s in range(1, 4):
            total = total + self.yb[s].astype(F32)
        self.d[...] = total.astype(BF)
        copies = []
        for s in range(1, N_Z):
            to = (p.z + s) % N_Z
            copies.append(remote(self.d.at[to], self.zb.at[p.z], self.send.at[6 + s],
                                 self.zs.at[s - 1], p.at(z=to)))
        self.launch(copies)
        self.zb[p.z] = self.d[p.z]

    def to_mate(self):
        p = self.place
        self.arrive()
        total = self.zb[0].astype(F32)
        for s in range(1, N_Z):
            total = total + self.zb[s].astype(F32)
        self.e[...] = total
        self.launch([
            remote(self.e, self.last, self.send.at[6 + N_Z], self.ls.at[0], p.at(core=1 - p.core))
        ])

    def result(self):
        self.arrive()
        first = self.place.core == 0
        own, other = self.e[...], self.last[...]
        full = jnp.concatenate([jnp.where(first, own, other), jnp.where(first, other, own)], 1)
        return jnp.where(first, full[:4], full[4:])


def scatter_scratch(cols):
    half = cols // 2
    sem = pltpu.SemaphoreType.DMA
    bufs = [
        pltpu.VMEM((N_Y, N_Z, N_X, 8, half), BF),
        pltpu.VMEM((N_X, N_Y, N_Z, 8, half), BF),
        pltpu.VMEM((N_X - 1, N_Y, N_Z, 8, half), BF),
        pltpu.VMEM((N_Y, N_Z, 8, half), BF),
        pltpu.VMEM((4, N_Z, 8, half), BF),
        pltpu.VMEM((N_Z, 8, half), BF),
        pltpu.VMEM((N_Z, 8, half), BF),
        pltpu.VMEM((8, half), F32),
        pltpu.VMEM((8, half), F32),
    ]
    sems = [sem((7 + N_Z,)), sem((1,)), sem((N_X - 1,)), sem((3,)), sem((N_Z - 1,)), sem((1,))]
    return dict(g=pltpu.VMEM((N_Y, N_Z, N_X, 8, cols), BF), bufs=bufs, sems=sems)


class Swap:
    def __init__(self, place, src, dst, send, recv):
        self.place, self.src, self.dst, self.send, self.recv = place, src, dst, send, recv
        self.n = src.shape[0]

    def start(self):
        p, n = self.place, self.n

        def step(s, carry):
            to = (p.ctx + s) % n
            remote(self.src.at[to], self.dst.at[p.ctx], self.send, self.recv, (p.dp, to)).start()
            return carry

        lax.fori_loop(1, n, step, 0)
        self.dst[p.ctx] = self.src[p.ctx]

    def all_but_one(self, ref, sem):
        part = ref.at[pl.ds(0, self.n - 1)]
        pltpu.make_async_copy(part, part, sem).wait()

    def arrived(self):
        self.all_but_one(self.dst, self.recv)

    def gone(self):
        self.all_but_one(self.src, self.send)


def to_wire(ref, get, perm):
    for b in range(4):
        x = get(b)
        y = nn(perm, x).astype(BF)
        ref[32 * b : 32 * b + 32] = y.reshape(32, 8, y.shape[-1])


def block_of(ref, b):
    return jnp.concatenate([ref[r, 128 * b : 128 * b + 128] for r in range(2)], 0)


def to_columns(wire, col, perm):
    for b in range(4):
        x = wire[32 * b : 32 * b + 32]
        y = nn(perm, x.reshape(256, x.shape[-1])).astype(BF)
        for c in range(4):
            col[c, 64 * b : 64 * b + 64] = y[64 * c : 64 * c + 64]


def from_columns(col, wire, perm):
    for b in range(4):
        x = jnp.concatenate([col[c, 64 * b : 64 * b + 64] for c in range(4)], 0)
        y = nn(perm, x).astype(BF)
        wire[32 * b : 32 * b + 32] = y.reshape(32, 8, y.shape[-1])


def turned_wide(x, ident):
    return jnp.concatenate([turned(x[:, :256], ident), turned(x[:, 256:], ident)], 0)


def side_by_side(w, offset):
    return jnp.concatenate([w[:, i * 512 + offset : i * 512 + offset + HALF] for i in range(3)], 1)


def row_heads(s, r, lay, feats, grads, w, wo, ident):
    n = feats.shape[0]
    qkv = nn(feats, w).astype(BF)
    q_all, k_all, v_all = (qkv[:, i * HALF : (i + 1) * HALF] for i in range(3))
    d_t = nt(wo[:HALF], grads).astype(BF).astype(F32)
    q_t, k_t, v_t = (turned(x, ident) for x in (q_all, k_all, v_all))
    tri = lax.broadcasted_iota(jnp.int32, (BLOCK, BLOCK), 0) <= lax.broadcasted_iota(
        jnp.int32, (BLOCK, BLOCK), 1
    )
    chunks = []
    width = 2 * BLOCK
    for chunk in range(n // width):
        nj = (chunk + 1) * width
        cols = slice(chunk * width, (chunk + 1) * width)
        weights, ds_all, outs, dqs, dts_all = [], [], [], [], []
        for h in range(4):
            scores = nn(k_all[:nj], padded(q_t[head_rows(h), cols], h))
            blocks = []
            for half in range(2):
                ib = 2 * chunk + half
                lanes = slice(BLOCK * half, BLOCK * half + BLOCK)
                pieces = []
                for jb in range(ib):
                    bias = jnp.where(lay[h, ib, jb] == 1, 0.0, NEG)
                    pieces.append(scores[BLOCK * jb : BLOCK * jb + BLOCK, lanes] + bias)
                pieces.append(jnp.where(tri, scores[BLOCK * ib : BLOCK * ib + BLOCK, lanes], NEG))
                blocks.append(soften(pieces))
            wts = jnp.concatenate([stacked(x, nj) for x in blocks], 1)
            product = nn(with_ones(v_t[head_rows(h), :nj]), wts)
            inv = 1.0 / product[HEAD : HEAD + 1]
            out = product[:HEAD] * inv
            dts = (d_t[head_rows(h), cols] * inv).astype(BF)
            delta = jnp.sum(out * dts.astype(F32), axis=0, keepdims=True)
            d_prob = nn(v_all[:nj], padded(dts, h))
            ds_blocks = []
            for half in range(2):
                lanes = slice(BLOCK * half, BLOCK * half + BLOCK)
                ds_blocks.append([
                    (x.astype(F32) * (d_prob[BLOCK * j : BLOCK * j + BLOCK, lanes] - delta[:, lanes])).astype(BF)
                    for j, x in enumerate(blocks[half])
                ])
            ds = jnp.concatenate([stacked(x, nj) for x in ds_blocks], 1)
            dqs.append(nn(k_t[head_rows(h), :nj], ds) * SCALE)
            weights.append(wts)
            ds_all.append(ds)
            outs.append(out)
            dts_all.append(dts)
        att_t = jnp.concatenate(outs, 0).astype(BF)
        s["att_row_t"][r, :, cols] = att_t
        s["att_row"][r, cols] = nt(ident, att_t).astype(BF)
        dq = nt(ident, jnp.concatenate(dqs, 0).astype(BF)).astype(BF)
        chunks.append((
            jnp.concatenate(weights, 1), by_head(turned(jnp.concatenate(dts_all, 0), ident)),
            jnp.concatenate(ds_all, 1), by_head(q_all[cols]), dq,
        ))
    first, second = chunks
    dv_low = nn(second[0][:width], second[1]) + nn(first[0], first[1])
    dk_low = nn(second[2][:width], second[3]) + nn(first[2], first[3])
    dv = jnp.concatenate([dv_low, nn(second[0][width:], second[1])], 0).astype(BF)
    dk = (jnp.concatenate([dk_low, nn(second[2][width:], second[3])], 0) * SCALE).astype(BF)
    d_proj = jnp.concatenate([jnp.concatenate([first[4], second[4]], 0), dk, dv], 1)
    s["dp_row"][r] = d_proj


def weight_grads(feats_t, d_proj, put):
    for i in range(3):
        put(i, nn(feats_t, d_proj[:, i * HALF : (i + 1) * HALF]).astype(BF))


def put_block(ref, i, part):
    ref[:, :, :, :, i * HALF : (i + 1) * HALF] = part.reshape(N_Y, N_Z, N_X, 8, HALF)


def col_forward(s, c, w, mask, ident):
    qkv = nn(s["f_col"][c], w).astype(BF)
    s["qkv"][c] = qkv
    q_all, k_all, v_all = (qkv[:, i * HALF : (i + 1) * HALF] for i in range(3))
    q_t, v_t = turned(q_all, ident), turned(v_all, ident)
    outs = []
    for h in range(4):
        scores = nn(k_all, padded(q_t[head_rows(h)], h))
        early = soften([jnp.where(mask, scores[:BLOCK, :BLOCK], NEG)])
        late = soften([scores[:BLOCK, BLOCK:], jnp.where(mask, scores[BLOCK:, BLOCK:], NEG)])
        wts = jnp.concatenate([stacked(early, 256), stacked(late, 256)], 1)
        s["wts"][c, :, 256 * h : 256 * h + 256] = wts
        product = nn(with_ones(v_t[head_rows(h)]), wts)
        inv = 1.0 / product[HEAD : HEAD + 1]
        s["inv"][c, h : h + 1] = inv
        outs.append(product[:HEAD] * inv)
    out = jnp.concatenate(outs, 0)
    s["o"][c] = out
    s["a_col"][c] = nt(ident, out.astype(BF)).astype(BF)


def col_backward(s, c, w, mask, ident):
    qkv = s["qkv"][c]
    q_all, k_all, v_all = (qkv[:, i * HALF : (i + 1) * HALF] for i in range(3))
    k_t, d_t = turned(k_all, ident), nt(ident, s["d_col"][c])
    dqs, dts_all, ds_all = [], [], []
    for h in range(4):
        dts = (d_t[head_rows(h)] * s["inv"][c, h : h + 1]).astype(BF)
        delta = jnp.sum(s["o"][c, head_rows(h)] * dts.astype(F32), axis=0, keepdims=True)
        d_prob = nn(v_all, padded(dts, h))

        def grad(j, i):
            rows, lanes = slice(BLOCK * j, BLOCK * j + BLOCK), slice(BLOCK * i, BLOCK * i + BLOCK)
            wts = s["wts"][c, rows, 256 * h + BLOCK * i : 256 * h + BLOCK * i + BLOCK]
            return (wts.astype(F32) * (d_prob[rows, lanes] - delta[:, lanes])).astype(BF)

        ds = jnp.concatenate([stacked([grad(0, 0)], 256), stacked([grad(0, 1), grad(1, 1)], 256)], 1)
        dqs.append(nn(k_t[head_rows(h)], ds) * SCALE)
        dts_all.append(dts)
        ds_all.append(ds)
    dq = nt(ident, jnp.concatenate(dqs, 0).astype(BF)).astype(BF)
    dv = nn(s["wts"][c], by_head(turned(jnp.concatenate(dts_all, 0), ident))).astype(BF)
    dk = (nn(jnp.concatenate(ds_all, 1), by_head(q_all)) * SCALE).astype(BF)
    d_proj = jnp.concatenate([dq, dk, dv], 1)
    s["dp_col"][c] = d_proj
    s["g_col"][c] = nt(d_proj, w).astype(BF)


def whole_kernel(lay, feats_in, grads_in, w_in, wo_in, out, gf_out, gq_out, gwo_out, s):
    p = Place()
    feats, grads, w, wo = s["feats"], s["grads"], s["w"], s["wo"]
    loads = [
        pltpu.make_async_copy(src, dst, s["loads"].at[i])
        for i, (src, dst) in enumerate(((feats_in, feats), (wo_in, wo), (grads_in, grads), (w_in, w)))
    ]
    for load in loads:
        load.start()
    n_ctx = s["f_wire"].shape[0]
    barrier = pltpu.get_barrier_semaphore()

    def greet(step, carry):
        pl.semaphore_signal(
            barrier, inc=1, device_id=(p.dp, (p.ctx + step) % n_ctx), device_id_type=MESH
        )
        return carry

    lax.fori_loop(1, n_ctx, greet, 0)
    for yh in (p.yh, 1 - p.yh):
        pl.semaphore_signal(barrier, inc=1, device_id=p.at(yh=yh, dp=1 - p.dp), device_id_type=MESH)

    perm = wire_matrix()
    loads[0].wait()
    to_wire(s["f_wire"], lambda b: block_of(feats, b), perm)
    pl.semaphore_wait(barrier, n_ctx + 1)
    sems = s["swap"]
    f_swap = Swap(p, s["f_wire"], s["f_got"], sems.at[0], sems.at[1])
    d_swap = Swap(p, s["d_wire"], s["d_got"], sems.at[2], sems.at[3])
    a_swap = Swap(p, s["a_wire"], s["a_got"], sems.at[4], sems.at[5])
    g_swap = Swap(p, s["g_wire"], s["g_got"], sems.at[6], sems.at[7])
    f_swap.start()
    for load in loads[1:]:
        load.wait()
    to_wire(s["d_wire"], lambda b: nt(block_of(grads, b), wo[HALF:]).astype(BF), perm)
    d_swap.start()

    ident = eye(256)
    s["w_row"][...] = side_by_side(w, 0)
    s["w_col"][...] = side_by_side(w, HALF)
    w_row, w_col = s["w_row"], s["w_col"]

    @pl.loop(0, 2)
    def _(r):
        row_heads(s, r, lay, feats[r], grads[r], w_row[...], wo, ident)

    gq_row, gq_col, gwo = (Scatter(p, s[k]["g"], s[k]["bufs"], s[k]["sems"]) for k in ("gq_row", "gq_col", "gwo"))
    feats_t = jnp.concatenate([turned_wide(feats[r], ident) for r in range(2)], 1)
    weight_grads(feats_t, s["dp_row"][...].reshape(1024, 768), lambda i, x: put_block(gq_row.g, i, x))
    gq_row.to_core()

    mask = lax.broadcasted_iota(jnp.int32, (BLOCK, BLOCK), 0) <= lax.broadcasted_iota(
        jnp.int32, (BLOCK, BLOCK), 1
    )
    split, join = column_matrix(), uncolumn_matrix()
    f_swap.arrived()
    to_columns(s["f_got"], s["f_col"], split)

    @pl.loop(0, 2)
    def _(pair):
        for c in (2 * pair, 2 * pair + 1):
            col_forward(s, c, w_col[...], mask, ident)

    from_columns(s["a_col"], s["a_wire"], join)
    a_swap.start()
    gq_row.to_x()

    d_swap.arrived()
    to_columns(s["d_got"], s["d_col"], split)

    @pl.loop(0, 2)
    def _(pair):
        for c in (2 * pair, 2 * pair + 1):
            col_backward(s, c, w_col[...], mask, ident)

    from_columns(s["g_col"], s["g_wire"], join)
    g_swap.start()
    gq_row.to_y()
    feats_t = jnp.concatenate([turned_wide(s["f_col"][c], ident) for c in range(4)], 1)
    weight_grads(feats_t, s["dp_col"][...].reshape(1024, 768), lambda i, x: put_block(gq_col.g, i, x))
    gq_col.to_core()
    part = nn(s["att_row_t"][0], grads[0]) + nn(s["att_row_t"][1], grads[1])
    gwo.g[0] = part.astype(BF).reshape(N_Z, N_X, 8, 512)

    unwire = unwire_matrix()
    a_swap.arrived()
    part = None
    for b in range(4):
        x = s["a_got"][32 * b : 32 * b + 32]
        a = nn(unwire, x.reshape(256, HALF)).astype(BF)
        term = nn(turned(a, ident), block_of(grads, b))
        part = term if part is None else part + term
        s["att_col"][0, 128 * b : 128 * b + 128] = a[:128]
        s["att_col"][1, 128 * b : 128 * b + 128] = a[128:]
    gwo.g[1] = part.astype(BF).reshape(N_Z, N_X, 8, 512)
    gwo.to_core()
    gq_col.to_x()
    for r in range(2):
        both = jnp.concatenate([s["att_row"][r], s["att_col"][r]], 1)
        out[r] = nn(both, wo[...]).astype(BF)
    gwo.to_x()
    gq_row.to_z()
    gq_col.to_y()
    for r in range(2):
        s["gf_row"][r] = nt(s["dp_row"][r], w_row[...])
    gwo.to_y()
    gq_col.to_z()
    gwo.to_z()

    g_swap.arrived()
    for kind in (gq_row, gq_col, gwo):
        kind.to_mate()
    for b in range(4):
        x = s["g_got"][32 * b : 32 * b + 32]
        g = nn(unwire, x.reshape(256, 512))
        for r in range(2):
            rows = slice(128 * b, 128 * b + 128)
            gf_out[r, rows] = (s["gf_row"][r, rows] + g[128 * r : 128 * r + 128]).astype(BF)
    for swap in (f_swap, d_swap, a_swap, g_swap):
        swap.gone()
    for offset, kind in ((0, gq_row), (HALF, gq_col)):
        rows = kind.result()
        for i in range(3):
            gq_out[:, i * 512 + offset : i * 512 + offset + HALF] = rows[:, i * HALF : (i + 1) * HALF]
    gwo_out[...] = gwo.result()


def on_device(features, w_qkv, w_out, layout, grad_out):
    n_clips, n_rows, length, width = features.shape
    n_ctx = lax.axis_size("ctx")
    vm = pl.BlockSpec(memory_space=pltpu.VMEM)
    vmem = pltpu.VMEM
    scratch = dict(
        f_wire=vmem((n_ctx, 8, 512), BF),
        f_got=vmem((n_ctx, 8, 512), BF),
        d_wire=vmem((n_ctx, 8, 256), BF),
        d_got=vmem((n_ctx, 8, 256), BF),
        a_wire=vmem((n_ctx, 8, 256), BF),
        a_got=vmem((n_ctx, 8, 256), BF),
        g_wire=vmem((n_ctx, 8, 512), BF),
        g_got=vmem((n_ctx, 8, 512), BF),
        swap=pltpu.SemaphoreType.DMA((8,)),
        feats=vmem((2, 512, 512), BF),
        grads=vmem((2, 512, 512), BF),
        w=vmem((512, 1536), BF),
        wo=vmem((512, 512), BF),
        loads=pltpu.SemaphoreType.DMA((4,)),
        w_row=vmem((512, 768), BF),
        w_col=vmem((512, 768), BF),
        att_row=vmem((2, 512, 256), BF),
        att_row_t=vmem((2, 256, 512), BF),
        att_col=vmem((2, 512, 256), BF),
        gf_row=vmem((2, 512, 512), F32),
        dp_row=vmem((2, 512, 768), BF),
        f_col=vmem((4, 256, 512), BF),
        d_col=vmem((4, 256, 256), BF),
        a_col=vmem((4, 256, 256), BF),
        g_col=vmem((4, 256, 512), BF),
        qkv=vmem((4, 256, 768), BF),
        wts=vmem((4, 256, 1024), BF),
        inv=vmem((4, 8, 256), F32),
        o=vmem((4, 256, 256), F32),
        dp_col=vmem((4, 256, 768), BF),
        gq_row=scatter_scratch(768),
        gq_col=scatter_scratch(768),
        gwo=scatter_scratch(512),
    )
    flat, tree = jax.tree.flatten(scratch, is_leaf=lambda x: not isinstance(x, (dict, list)))
    n_out = 4

    def kernel(lay, feats, grads, w, wo, *rest):
        outs, refs = rest[:n_out], rest[n_out:]
        whole_kernel(lay, feats, grads, w, wo, *outs, jax.tree.unflatten(tree, refs))

    shape = (n_rows, length, width)
    out, gf, gq, gwo = pl.pallas_call(
        kernel,
        out_shape=[
            jax.ShapeDtypeStruct(shape, BF),
            jax.ShapeDtypeStruct(shape, BF),
            jax.ShapeDtypeStruct((4, 1536), F32),
            jax.ShapeDtypeStruct((4, 512), F32),
        ],
        in_specs=[pl.BlockSpec(memory_space=pltpu.SMEM)] + [pl.BlockSpec(memory_space=pltpu.HBM)] * 4,
        out_specs=[vm] * n_out,
        scratch_shapes=flat,
        compiler_params=pltpu.CompilerParams(
            collective_id=1, has_side_effects=True, vmem_limit_bytes=VMEM_LIMIT
        ),
        name="whole_layer",
    )(
        *(
            pltpu.with_memory_space_constraint(a, pltpu.HBM)
            for a in (layout, features.reshape(shape), grad_out.reshape(shape), w_qkv, w_out)
        )
    )
    full = (n_clips,) + shape
    return out.reshape(full), gf.reshape(full), gq, gwo


def solution(mesh):
    return jax.shard_map(
        on_device,
        mesh=mesh,
        in_specs=(P("dp", "ctx", None, None), P(), P(), P(), P("dp", "ctx", None, None)),
        out_specs=(
            P("dp", "ctx", None, None),
            P("dp", "ctx", None, None),
            P("ctx", None),
            P("ctx", None),
        ),
        check_vma=False,
    )
```

```python
import functools

import jax
import jax.numpy as jnp
from jax import lax
from jax.experimental import pallas as pl
from jax.experimental.pallas import tpu as pltpu
from jax.sharding import PartitionSpec as P

HEADS = 8
HEAD = 64
BLOCK = 128
HALF = 256
SCALE = HEAD**-0.5
NEG = -1e30
BF = jnp.bfloat16
F32 = jnp.float32
VMEM_LIMIT = 40 * 1024 * 1024
MESH = pl.DeviceIdType.MESH
N_Y, N_Z, N_X = 2, 8, 4
SCALE_LOG2E = SCALE * 1.4426950408889634


def nn(a, b):
    return jnp.dot(a, b, preferred_element_type=F32)


def nt(a, b):
    return lax.dot_general(a, b, (((1,), (1,)), ((), ())), preferred_element_type=F32)


def eye(n):
    r = lax.broadcasted_iota(jnp.int32, (n, n), 0)
    c = lax.broadcasted_iota(jnp.int32, (n, n), 1)
    return (r == c).astype(F32).astype(BF)


def turned(x, ident):
    return nt(ident, x).astype(BF)


def wire_matrix():
    t = lax.broadcasted_iota(jnp.int32, (256, 256), 0)
    k = lax.broadcasted_iota(jnp.int32, (256, 256), 1)
    src = ((t >> 2) & 1) * 128 + (t >> 3) * 4 + (t & 3)
    return (k == src).astype(F32).astype(BF)


def unwire_matrix():
    t = lax.broadcasted_iota(jnp.int32, (256, 256), 1)
    k = lax.broadcasted_iota(jnp.int32, (256, 256), 0)
    src = ((t >> 2) & 1) * 128 + (t >> 3) * 4 + (t & 3)
    return (k == src).astype(F32).astype(BF)


def column_matrix():
    t = lax.broadcasted_iota(jnp.int32, (256, 256), 0)
    k = lax.broadcasted_iota(jnp.int32, (256, 256), 1)
    return (k == (t & 63) * 4 + (t >> 6)).astype(F32).astype(BF)


def uncolumn_matrix():
    t = lax.broadcasted_iota(jnp.int32, (256, 256), 1)
    k = lax.broadcasted_iota(jnp.int32, (256, 256), 0)
    return (k == (t & 63) * 4 + (t >> 6)).astype(F32).astype(BF)


def lanes_of_head(x, h):
    c = lax.broadcasted_iota(jnp.int32, x.shape, 1)
    return jnp.where((c >> 6) == h, x, jnp.zeros_like(x))


def soften(pieces):
    high = pieces[0]
    for x in pieces[1:]:
        high = jnp.maximum(high, x)
    top = jnp.max(high, axis=0, keepdims=True)
    return [jnp.exp2((x - top) * SCALE_LOG2E).astype(BF) for x in pieces]


def stacked(pieces, n_keys):
    rest = n_keys - BLOCK * len(pieces)
    if rest:
        pieces = pieces + [jnp.zeros((rest, BLOCK), BF)]
    return jnp.concatenate(pieces, 0)


def padded(x, h):
    parts = [jnp.zeros((HEAD * h, x.shape[1]), BF)] if h else []
    parts.append(x)
    if h < 3:
        parts.append(jnp.zeros((HEAD * (3 - h), x.shape[1]), BF))
    return jnp.concatenate(parts, 0)


def with_ones(v_t):
    return jnp.concatenate([v_t, jnp.ones((16, v_t.shape[1]), BF)], 0)


def by_head(x):
    return jnp.concatenate([lanes_of_head(x, h) for h in range(4)], 0)


def head_rows(h):
    return slice(h * HEAD, (h + 1) * HEAD)


class Place:
    def __init__(self):
        self.dp = lax.axis_index("dp")
        self.ctx = lax.axis_index("ctx")
        self.core = self.ctx % 2
        self.x = (self.ctx // 2) % N_X
        self.z = (self.ctx // (2 * N_X)) % N_Z
        self.yh = self.ctx // (2 * N_X * N_Z)

    def at(self, yh=None, z=None, x=None, core=None, dp=None):
        yh = self.yh if yh is None else yh
        z = self.z if z is None else z
        x = self.x if x is None else x
        core = self.core if core is None else core
        dp = self.dp if dp is None else dp
        return (dp, ((yh * N_Z + z) * N_X + x) * 2 + core)


def remote(src, dst, send, recv, device):
    return pltpu.make_async_remote_copy(
        src_ref=src, dst_ref=dst, send_sem=send, recv_sem=recv, device_id=device, device_id_type=MESH
    )


class Scatter:
    def __init__(self, place, g, bufs, sems):
        self.place, self.g = place, g
        self.c, self.a, self.xb, self.b, self.yb, self.d, self.zb, self.e, self.last = bufs
        self.send, self.cs, self.xs, self.ys, self.zs, self.ls = sems
        self.half = g.shape[-1] // 2
        self.copies = []

    def launch(self, copies):
        for c in copies:
            c.start()
        self.copies = copies

    def arrive(self):
        for c in self.copies:
            c.wait()

    def to_core(self):
        p, half = self.place, self.half
        theirs = pl.ds(pl.multiple_of((1 - p.core) * half, 128), half)
        self.launch([
            remote(self.g.at[:, :, :, :, theirs], self.c, self.send.at[0], self.cs.at[0],
                   p.at(core=1 - p.core))
        ])

    def to_x(self):
        p, half = self.place, self.half
        self.arrive()
        mine = pl.ds(pl.multiple_of(p.core * half, 128), half)

        @pl.loop(0, N_Z)
        def _(zz):
            for yy in range(N_Y):
                self.a[:, yy, zz] = (
                    self.g[yy, zz, :, :, mine].astype(F32) + self.c[yy, zz].astype(F32)
                ).astype(BF)

        copies = []
        for s in range(1, N_X):
            to = (p.x + s) % N_X
            copies.append(remote(self.a.at[to], self.xb.at[s - 1], self.send.at[s],
                                 self.xs.at[s - 1], p.at(x=to)))
        self.launch(copies)

    def to_y(self):
        p = self.place
        self.arrive()

        @pl.loop(0, N_Y)
        def _(yy):
            total = self.a[p.x, yy].astype(F32)
            for s in range(N_X - 1):
                total = total + self.xb[s, yy].astype(F32)
            self.b[yy] = total.astype(BF)

        here = p.yh * 2 + p.dp
        copies = []
        for s in range(1, 4):
            to = (here + s) % 4
            copies.append(remote(self.b.at[to // 2], self.yb.at[here], self.send.at[3 + s],
                                 self.ys.at[s - 1], p.at(yh=to // 2, dp=to % 2)))
        self.launch(copies)
        self.yb[here] = self.b[p.yh]

    def to_z(self):
        p = self.place
        self.arrive()
        total = self.yb[0].astype(F32)
        for s in range(1, 4):
            total = total + self.yb[s].astype(F32)
        self.d[...] = total.astype(BF)
        copies = []
        for s in range(1, N_Z):
            to = (p.z + s) % N_Z
            copies.append(remote(self.d.at[to], self.zb.at[p.z], self.send.at[6 + s],
                                 self.zs.at[s - 1], p.at(z=to)))
        self.launch(copies)
        self.zb[p.z] = self.d[p.z]

    def to_mate(self):
        p = self.place
        self.arrive()
        total = self.zb[0].astype(F32)
        for s in range(1, N_Z):
            total = total + self.zb[s].astype(F32)
        self.e[...] = total
        self.launch([
            remote(self.e, self.last, self.send.at[6 + N_Z], self.ls.at[0], p.at(core=1 - p.core))
        ])

    def result(self):
        self.arrive()
        first = self.place.core == 0
        own, other = self.e[...], self.last[...]
        full = jnp.concatenate([jnp.where(first, own, other), jnp.where(first, other, own)], 1)
        return jnp.where(first, full[:4], full[4:])


def scatter_scratch(cols):
    half = cols // 2
    sem = pltpu.SemaphoreType.DMA
    bufs = [
        pltpu.VMEM((N_Y, N_Z, N_X, 8, half), BF),
        pltpu.VMEM((N_X, N_Y, N_Z, 8, half), BF),
        pltpu.VMEM((N_X - 1, N_Y, N_Z, 8, half), BF),
        pltpu.VMEM((N_Y, N_Z, 8, half), BF),
        pltpu.VMEM((4, N_Z, 8, half), BF),
        pltpu.VMEM((N_Z, 8, half), BF),
        pltpu.VMEM((N_Z, 8, half), BF),
        pltpu.VMEM((8, half), F32),
        pltpu.VMEM((8, half), F32),
    ]
    sems = [sem((7 + N_Z,)), sem((1,)), sem((N_X - 1,)), sem((3,)), sem((N_Z - 1,)), sem((1,))]
    return dict(g=pltpu.VMEM((N_Y, N_Z, N_X, 8, cols), BF), bufs=bufs, sems=sems)


class Swap:
    def __init__(self, place, src, dst, send, recv):
        self.place, self.src, self.dst, self.send, self.recv = place, src, dst, send, recv
        self.n = src.shape[0]

    def start(self):
        p, n = self.place, self.n

        def step(s, carry):
            to = (p.ctx + s) % n
            remote(self.src.at[to], self.dst.at[p.ctx], self.send, self.recv, (p.dp, to)).start()
            return carry

        lax.fori_loop(1, n, step, 0)
        self.dst[p.ctx] = self.src[p.ctx]

    def all_but_one(self, ref, sem):
        part = ref.at[pl.ds(0, self.n - 1)]
        pltpu.make_async_copy(part, part, sem).wait()

    def arrived(self):
        self.all_but_one(self.dst, self.recv)

    def gone(self):
        self.all_but_one(self.src, self.send)


def to_wire(ref, get, perm):
    for b in range(4):
        x = get(b)
        y = nn(perm, x).astype(BF)
        ref[32 * b : 32 * b + 32] = y.reshape(32, 8, y.shape[-1])


def block_of(ref, b):
    return jnp.concatenate([ref[r, 128 * b : 128 * b + 128] for r in range(2)], 0)


def to_columns(wire, col, perm):
    for b in range(4):
        x = wire[32 * b : 32 * b + 32]
        y = nn(perm, x.reshape(256, x.shape[-1])).astype(BF)
        for c in range(4):
            col[c, 64 * b : 64 * b + 64] = y[64 * c : 64 * c + 64]


def from_columns(col, wire, perm):
    for b in range(4):
        x = jnp.concatenate([col[c, 64 * b : 64 * b + 64] for c in range(4)], 0)
        y = nn(perm, x).astype(BF)
        wire[32 * b : 32 * b + 32] = y.reshape(32, 8, y.shape[-1])


def turned_wide(x, ident):
    return jnp.concatenate([turned(x[:, :256], ident), turned(x[:, 256:], ident)], 0)


def side_by_side(w, offset):
    return jnp.concatenate([w[:, i * 512 + offset : i * 512 + offset + HALF] for i in range(3)], 1)


def row_heads(s, r, lay, feats, grads, w, wo, ident):
    n = feats.shape[0]
    qkv = nn(feats, w).astype(BF)
    q_all, k_all, v_all = (qkv[:, i * HALF : (i + 1) * HALF] for i in range(3))
    d_t = nt(wo[:HALF], grads).astype(BF).astype(F32)
    q_t, k_t, v_t = (turned(x, ident) for x in (q_all, k_all, v_all))
    tri = lax.broadcasted_iota(jnp.int32, (BLOCK, BLOCK), 0) <= lax.broadcasted_iota(
        jnp.int32, (BLOCK, BLOCK), 1
    )
    chunks = []
    width = 2 * BLOCK
    for chunk in range(n // width):
        nj = (chunk + 1) * width
        cols = slice(chunk * width, (chunk + 1) * width)
        weights, ds_all, outs, dqs, dts_all = [], [], [], [], []
        for h in range(4):
            scores = nn(k_all[:nj], padded(q_t[head_rows(h), cols], h))
            blocks = []
            for half in range(2):
                ib = 2 * chunk + half
                lanes = slice(BLOCK * half, BLOCK * half + BLOCK)
                pieces = []
                for jb in range(ib):
                    bias = jnp.where(lay[h, ib, jb] == 1, 0.0, NEG)
                    pieces.append(scores[BLOCK * jb : BLOCK * jb + BLOCK, lanes] + bias)
                pieces.append(jnp.where(tri, scores[BLOCK * ib : BLOCK * ib + BLOCK, lanes], NEG))
                blocks.append(soften(pieces))
            wts = jnp.concatenate([stacked(x, nj) for x in blocks], 1)
            product = nn(with_ones(v_t[head_rows(h), :nj]), wts)
            inv = 1.0 / product[HEAD : HEAD + 1]
            out = product[:HEAD] * inv
            dts = (d_t[head_rows(h), cols] * inv).astype(BF)
            delta = jnp.sum(out * dts.astype(F32), axis=0, keepdims=True)
            d_prob = nn(v_all[:nj], padded(dts, h))
            ds_blocks = []
            for half in range(2):
                lanes = slice(BLOCK * half, BLOCK * half + BLOCK)
                ds_blocks.append([
                    (x.astype(F32) * (d_prob[BLOCK * j : BLOCK * j + BLOCK, lanes] - delta[:, lanes])).astype(BF)
                    for j, x in enumerate(blocks[half])
                ])
            ds = jnp.concatenate([stacked(x, nj) for x in ds_blocks], 1)
            dqs.append(nn(k_t[head_rows(h), :nj], ds) * SCALE)
            weights.append(wts)
            ds_all.append(ds)
            outs.append(out)
            dts_all.append(dts)
        att_t = jnp.concatenate(outs, 0).astype(BF)
        s["att_row_t"][r, :, cols] = att_t
        s["att_row"][r, cols] = nt(ident, att_t).astype(BF)
        dq = nt(ident, jnp.concatenate(dqs, 0).astype(BF)).astype(BF)
        chunks.append((
            jnp.concatenate(weights, 1), by_head(turned(jnp.concatenate(dts_all, 0), ident)),
            jnp.concatenate(ds_all, 1), by_head(q_all[cols]), dq,
        ))
    first, second = chunks
    dv_low = nn(second[0][:width], second[1]) + nn(first[0], first[1])
    dk_low = nn(second[2][:width], second[3]) + nn(first[2], first[3])
    dv = jnp.concatenate([dv_low, nn(second[0][width:], second[1])], 0).astype(BF)
    dk = (jnp.concatenate([dk_low, nn(second[2][width:], second[3])], 0) * SCALE).astype(BF)
    d_proj = jnp.concatenate([jnp.concatenate([first[4], second[4]], 0), dk, dv], 1)
    s["dp_row"][r] = d_proj


def weight_grads(feats_t, d_proj, put):
    for i in range(3):
        put(i, nn(feats_t, d_proj[:, i * HALF : (i + 1) * HALF]).astype(BF))


def put_block(ref, i, part):
    ref[:, :, :, :, i * HALF : (i + 1) * HALF] = part.reshape(N_Y, N_Z, N_X, 8, HALF)


def col_forward(s, c, w, mask, ident):
    qkv = nn(s["f_col"][c], w).astype(BF)
    s["qkv"][c] = qkv
    q_all, k_all, v_all = (qkv[:, i * HALF : (i + 1) * HALF] for i in range(3))
    q_t, v_t = turned(q_all, ident), turned(v_all, ident)
    outs = []
    for h in range(4):
        scores = nn(k_all, padded(q_t[head_rows(h)], h))
        early = soften([jnp.where(mask, scores[:BLOCK, :BLOCK], NEG)])
        late = soften([scores[:BLOCK, BLOCK:], jnp.where(mask, scores[BLOCK:, BLOCK:], NEG)])
        wts = jnp.concatenate([stacked(early, 256), stacked(late, 256)], 1)
        s["wts"][c, :, 256 * h : 256 * h + 256] = wts
        product = nn(with_ones(v_t[head_rows(h)]), wts)
        inv = 1.0 / product[HEAD : HEAD + 1]
        s["inv"][c, h : h + 1] = inv
        outs.append(product[:HEAD] * inv)
    out = jnp.concatenate(outs, 0)
    s["o"][c] = out
    s["a_col"][c] = nt(ident, out.astype(BF)).astype(BF)


def col_backward(s, c, w, mask, ident):
    qkv = s["qkv"][c]
    q_all, k_all, v_all = (qkv[:, i * HALF : (i + 1) * HALF] for i in range(3))
    k_t, d_t = turned(k_all, ident), nt(ident, s["d_col"][c])
    dqs, dts_all, ds_all = [], [], []
    for h in range(4):
        dts = (d_t[head_rows(h)] * s["inv"][c, h : h + 1]).astype(BF)
        delta = jnp.sum(s["o"][c, head_rows(h)] * dts.astype(F32), axis=0, keepdims=True)
        d_prob = nn(v_all, padded(dts, h))

        def grad(j, i):
            rows, lanes = slice(BLOCK * j, BLOCK * j + BLOCK), slice(BLOCK * i, BLOCK * i + BLOCK)
            wts = s["wts"][c, rows, 256 * h + BLOCK * i : 256 * h + BLOCK * i + BLOCK]
            return (wts.astype(F32) * (d_prob[rows, lanes] - delta[:, lanes])).astype(BF)

        ds = jnp.concatenate([stacked([grad(0, 0)], 256), stacked([grad(0, 1), grad(1, 1)], 256)], 1)
        dqs.append(nn(k_t[head_rows(h)], ds) * SCALE)
        dts_all.append(dts)
        ds_all.append(ds)
    dq = nt(ident, jnp.concatenate(dqs, 0).astype(BF)).astype(BF)
    dv = nn(s["wts"][c], by_head(turned(jnp.concatenate(dts_all, 0), ident))).astype(BF)
    dk = (nn(jnp.concatenate(ds_all, 1), by_head(q_all)) * SCALE).astype(BF)
    d_proj = jnp.concatenate([dq, dk, dv], 1)
    s["dp_col"][c] = d_proj
    s["g_col"][c] = nt(d_proj, w).astype(BF)


def whole_kernel(lay, feats_in, grads_in, w_in, wo_in, out, gf_out, gq_out, gwo_out, s):
    p = Place()
    feats, grads, w, wo = s["feats"], s["grads"], s["w"], s["wo"]
    loads = [
        pltpu.make_async_copy(src, dst, s["loads"].at[i])
        for i, (src, dst) in enumerate(((feats_in, feats), (wo_in, wo), (grads_in, grads), (w_in, w)))
    ]
    for load in loads:
        load.start()
    n_ctx = s["f_wire"].shape[0]
    barrier = pltpu.get_barrier_semaphore()

    def greet(step, carry):
        pl.semaphore_signal(
            barrier, inc=1, device_id=(p.dp, (p.ctx + step) % n_ctx), device_id_type=MESH
        )
        return carry

    lax.fori_loop(1, n_ctx, greet, 0)
    for yh in (p.yh, 1 - p.yh):
        pl.semaphore_signal(barrier, inc=1, device_id=p.at(yh=yh, dp=1 - p.dp), device_id_type=MESH)

    perm = wire_matrix()
    loads[0].wait()
    to_wire(s["f_wire"], lambda b: block_of(feats, b), perm)
    pl.semaphore_wait(barrier, n_ctx + 1)
    sems = s["swap"]
    f_swap = Swap(p, s["f_wire"], s["f_got"], sems.at[0], sems.at[1])
    d_swap = Swap(p, s["d_wire"], s["d_got"], sems.at[2], sems.at[3])
    a_swap = Swap(p, s["a_wire"], s["a_got"], sems.at[4], sems.at[5])
    g_swap = Swap(p, s["g_wire"], s["g_got"], sems.at[6], sems.at[7])
    f_swap.start()
    for load in loads[1:]:
        load.wait()
    to_wire(s["d_wire"], lambda b: nt(block_of(grads, b), wo[HALF:]).astype(BF), perm)
    d_swap.start()

    ident = eye(256)
    s["w_row"][...] = side_by_side(w, 0)
    s["w_col"][...] = side_by_side(w, HALF)
    w_row, w_col = s["w_row"], s["w_col"]

    @pl.loop(0, 2)
    def _(r):
        row_heads(s, r, lay, feats[r], grads[r], w_row[...], wo, ident)

    gq_row, gq_col, gwo = (Scatter(p, s[k]["g"], s[k]["bufs"], s[k]["sems"]) for k in ("gq_row", "gq_col", "gwo"))
    feats_t = jnp.concatenate([turned_wide(feats[r], ident) for r in range(2)], 1)
    weight_grads(feats_t, s["dp_row"][...].reshape(1024, 768), lambda i, x: put_block(gq_row.g, i, x))
    gq_row.to_core()

    mask = lax.broadcasted_iota(jnp.int32, (BLOCK, BLOCK), 0) <= lax.broadcasted_iota(
        jnp.int32, (BLOCK, BLOCK), 1
    )
    split, join = column_matrix(), uncolumn_matrix()
    f_swap.arrived()
    to_columns(s["f_got"], s["f_col"], split)

    @pl.loop(0, 2)
    def _(pair):
        for c in (2 * pair, 2 * pair + 1):
            col_forward(s, c, w_col[...], mask, ident)

    from_columns(s["a_col"], s["a_wire"], join)
    a_swap.start()
    gq_row.to_x()

    d_swap.arrived()
    to_columns(s["d_got"], s["d_col"], split)

    @pl.loop(0, 2)
    def _(pair):
        for c in (2 * pair, 2 * pair + 1):
            col_backward(s, c, w_col[...], mask, ident)

    from_columns(s["g_col"], s["g_wire"], join)
    g_swap.start()
    gq_row.to_y()
    feats_t = jnp.concatenate([turned_wide(s["f_col"][c], ident) for c in range(4)], 1)
    weight_grads(feats_t, s["dp_col"][...].reshape(1024, 768), lambda i, x: put_block(gq_col.g, i, x))
    gq_col.to_core()
    part = nn(s["att_row_t"][0], grads[0]) + nn(s["att_row_t"][1], grads[1])
    gwo.g[0] = part.astype(BF).reshape(N_Z, N_X, 8, 512)
    gq_col.to_x()

    unwire = unwire_matrix()
    a_swap.arrived()
    part = None
    for b in range(4):
        x = s["a_got"][32 * b : 32 * b + 32]
        a = nn(unwire, x.reshape(256, HALF)).astype(BF)
        term = nn(turned(a, ident), block_of(grads, b))
        part = term if part is None else part + term
        s["att_col"][0, 128 * b : 128 * b + 128] = a[:128]
        s["att_col"][1, 128 * b : 128 * b + 128] = a[128:]
    gwo.g[1] = part.astype(BF).reshape(N_Z, N_X, 8, 512)
    gwo.to_core()
    for r in range(2):
        both = jnp.concatenate([s["att_row"][r], s["att_col"][r]], 1)
        out[r] = nn(both, wo[...]).astype(BF)
    gwo.to_x()
    gq_row.to_z()
    for r in range(2):
        s["gf_row"][r] = nt(s["dp_row"][r], w_row[...])
    gq_col.to_y()
    gwo.to_y()
    gq_col.to_z()
    gwo.to_z()

    g_swap.arrived()
    for b in range(4):
        if b == 2:
            for kind in (gq_row, gq_col, gwo):
                kind.to_mate()
        x = s["g_got"][32 * b : 32 * b + 32]
        g = nn(unwire, x.reshape(256, 512))
        for r in range(2):
            rows = slice(128 * b, 128 * b + 128)
            gf_out[r, rows] = (s["gf_row"][r, rows] + g[128 * r : 128 * r + 128]).astype(BF)
    for swap in (f_swap, d_swap, a_swap, g_swap):
        swap.gone()
    for offset, kind in ((0, gq_row), (HALF, gq_col)):
        rows = kind.result()
        for i in range(3):
            gq_out[:, i * 512 + offset : i * 512 + offset + HALF] = rows[:, i * HALF : (i + 1) * HALF]
    gwo_out[...] = gwo.result()


def on_device(features, w_qkv, w_out, layout, grad_out):
    n_clips, n_rows, length, width = features.shape
    n_ctx = lax.axis_size("ctx")
    vm = pl.BlockSpec(memory_space=pltpu.VMEM)
    vmem = pltpu.VMEM
    scratch = dict(
        f_wire=vmem((n_ctx, 8, 512), BF),
        f_got=vmem((n_ctx, 8, 512), BF),
        d_wire=vmem((n_ctx, 8, 256), BF),
        d_got=vmem((n_ctx, 8, 256), BF),
        a_wire=vmem((n_ctx, 8, 256), BF),
        a_got=vmem((n_ctx, 8, 256), BF),
        g_wire=vmem((n_ctx, 8, 512), BF),
        g_got=vmem((n_ctx, 8, 512), BF),
        swap=pltpu.SemaphoreType.DMA((8,)),
        feats=vmem((2, 512, 512), BF),
        grads=vmem((2, 512, 512), BF),
        w=vmem((512, 1536), BF),
        wo=vmem((512, 512), BF),
        loads=pltpu.SemaphoreType.DMA((4,)),
        w_row=vmem((512, 768), BF),
        w_col=vmem((512, 768), BF),
        att_row=vmem((2, 512, 256), BF),
        att_row_t=vmem((2, 256, 512), BF),
        att_col=vmem((2, 512, 256), BF),
        gf_row=vmem((2, 512, 512), F32),
        dp_row=vmem((2, 512, 768), BF),
        f_col=vmem((4, 256, 512), BF),
        d_col=vmem((4, 256, 256), BF),
        a_col=vmem((4, 256, 256), BF),
        g_col=vmem((4, 256, 512), BF),
        qkv=vmem((4, 256, 768), BF),
        wts=vmem((4, 256, 1024), BF),
        inv=vmem((4, 8, 256), F32),
        o=vmem((4, 256, 256), F32),
        dp_col=vmem((4, 256, 768), BF),
        gq_row=scatter_scratch(768),
        gq_col=scatter_scratch(768),
        gwo=scatter_scratch(512),
    )
    flat, tree = jax.tree.flatten(scratch, is_leaf=lambda x: not isinstance(x, (dict, list)))
    n_out = 4

    def kernel(lay, feats, grads, w, wo, *rest):
        outs, refs = rest[:n_out], rest[n_out:]
        whole_kernel(lay, feats, grads, w, wo, *outs, jax.tree.unflatten(tree, refs))

    shape = (n_rows, length, width)
    out, gf, gq, gwo = pl.pallas_call(
        kernel,
        out_shape=[
            jax.ShapeDtypeStruct(shape, BF),
            jax.ShapeDtypeStruct(shape, BF),
            jax.ShapeDtypeStruct((4, 1536), F32),
            jax.ShapeDtypeStruct((4, 512), F32),
        ],
        in_specs=[pl.BlockSpec(memory_space=pltpu.SMEM)] + [pl.BlockSpec(memory_space=pltpu.HBM)] * 4,
        out_specs=[vm] * n_out,
        scratch_shapes=flat,
        compiler_params=pltpu.CompilerParams(
            collective_id=1, has_side_effects=True, vmem_limit_bytes=VMEM_LIMIT
        ),
        name="whole_layer",
    )(
        *(
            pltpu.with_memory_space_constraint(a, pltpu.HBM)
            for a in (layout, features.reshape(shape), grad_out.reshape(shape), w_qkv, w_out)
        )
    )
    full = (n_clips,) + shape
    return out.reshape(full), gf.reshape(full), gq, gwo


def solution(mesh):
    return jax.shard_map(
        on_device,
        mesh=mesh,
        in_specs=(P("dp", "ctx", None, None), P(), P(), P(), P("dp", "ctx", None, None)),
        out_specs=(
            P("dp", "ctx", None, None),
            P("dp", "ctx", None, None),
            P("ctx", None),
            P("ctx", None),
        ),
        check_vma=False,
    )
```

```python
import functools

import jax
import jax.numpy as jnp
from jax import lax
from jax.experimental import pallas as pl
from jax.experimental.pallas import tpu as pltpu
from jax.sharding import PartitionSpec as P

HEADS = 8
HEAD = 64
BLOCK = 128
HALF = 256
SCALE = HEAD**-0.5
NEG = -1e30
BF = jnp.bfloat16
F32 = jnp.float32
VMEM_LIMIT = 40 * 1024 * 1024
MESH = pl.DeviceIdType.MESH
N_Y, N_Z, N_X = 2, 8, 4
SCALE_LOG2E = SCALE * 1.4426950408889634


def nn(a, b):
    return jnp.dot(a, b, preferred_element_type=F32)


def nt(a, b):
    return lax.dot_general(a, b, (((1,), (1,)), ((), ())), preferred_element_type=F32)


def eye(n):
    r = lax.broadcasted_iota(jnp.int32, (n, n), 0)
    c = lax.broadcasted_iota(jnp.int32, (n, n), 1)
    return (r == c).astype(F32).astype(BF)


def turned(x, ident):
    return nt(ident, x).astype(BF)


def wire_matrix():
    t = lax.broadcasted_iota(jnp.int32, (256, 256), 0)
    k = lax.broadcasted_iota(jnp.int32, (256, 256), 1)
    src = ((t >> 2) & 1) * 128 + (t >> 3) * 4 + (t & 3)
    return (k == src).astype(F32).astype(BF)


def unwire_matrix():
    t = lax.broadcasted_iota(jnp.int32, (256, 256), 1)
    k = lax.broadcasted_iota(jnp.int32, (256, 256), 0)
    src = ((t >> 2) & 1) * 128 + (t >> 3) * 4 + (t & 3)
    return (k == src).astype(F32).astype(BF)


def column_matrix():
    t = lax.broadcasted_iota(jnp.int32, (256, 256), 0)
    k = lax.broadcasted_iota(jnp.int32, (256, 256), 1)
    return (k == (t & 63) * 4 + (t >> 6)).astype(F32).astype(BF)


def uncolumn_matrix():
    t = lax.broadcasted_iota(jnp.int32, (256, 256), 1)
    k = lax.broadcasted_iota(jnp.int32, (256, 256), 0)
    return (k == (t & 63) * 4 + (t >> 6)).astype(F32).astype(BF)


def lanes_of_head(x, h):
    c = lax.broadcasted_iota(jnp.int32, x.shape, 1)
    return jnp.where((c >> 6) == h, x, jnp.zeros_like(x))


def soften(pieces):
    high = pieces[0]
    for x in pieces[1:]:
        high = jnp.maximum(high, x)
    top = jnp.max(high, axis=0, keepdims=True)
    return [jnp.exp2((x - top) * SCALE_LOG2E).astype(BF) for x in pieces]


def stacked(pieces, n_keys):
    rest = n_keys - BLOCK * len(pieces)
    if rest:
        pieces = pieces + [jnp.zeros((rest, BLOCK), BF)]
    return jnp.concatenate(pieces, 0)


def padded(x, h):
    parts = [jnp.zeros((HEAD * h, x.shape[1]), BF)] if h else []
    parts.append(x)
    if h < 3:
        parts.append(jnp.zeros((HEAD * (3 - h), x.shape[1]), BF))
    return jnp.concatenate(parts, 0)


def with_ones(v_t):
    return jnp.concatenate([v_t, jnp.ones((16, v_t.shape[1]), BF)], 0)


def by_head(x):
    return jnp.concatenate([lanes_of_head(x, h) for h in range(4)], 0)


def head_rows(h):
    return slice(h * HEAD, (h + 1) * HEAD)


class Place:
    def __init__(self):
        self.dp = lax.axis_index("dp")
        self.ctx = lax.axis_index("ctx")
        self.core = self.ctx % 2
        self.x = (self.ctx // 2) % N_X
        self.z = (self.ctx // (2 * N_X)) % N_Z
        self.yh = self.ctx // (2 * N_X * N_Z)

    def at(self, yh=None, z=None, x=None, core=None, dp=None):
        yh = self.yh if yh is None else yh
        z = self.z if z is None else z
        x = self.x if x is None else x
        core = self.core if core is None else core
        dp = self.dp if dp is None else dp
        return (dp, ((yh * N_Z + z) * N_X + x) * 2 + core)


def remote(src, dst, send, recv, device):
    return pltpu.make_async_remote_copy(
        src_ref=src, dst_ref=dst, send_sem=send, recv_sem=recv, device_id=device, device_id_type=MESH
    )


class Scatter:
    def __init__(self, place, g, bufs, sems):
        self.place, self.g = place, g
        self.c, self.a, self.xb, self.b, self.yb, self.d, self.zb, self.e, self.last = bufs
        self.send, self.cs, self.xs, self.ys, self.zs, self.ls = sems
        self.half = g.shape[-1] // 2
        self.copies = []

    def launch(self, copies):
        for c in copies:
            c.start()
        self.copies = copies

    def arrive(self):
        for c in self.copies:
            c.wait()

    def to_core(self):
        p, half = self.place, self.half
        theirs = pl.ds(pl.multiple_of((1 - p.core) * half, 128), half)
        self.launch([
            remote(self.g.at[:, :, :, :, theirs], self.c, self.send.at[0], self.cs.at[0],
                   p.at(core=1 - p.core))
        ])

    def to_x(self):
        p, half = self.place, self.half
        self.arrive()
        mine = pl.ds(pl.multiple_of(p.core * half, 128), half)

        @pl.loop(0, N_Z)
        def _(zz):
            for yy in range(N_Y):
                self.a[:, yy, zz] = (
                    self.g[yy, zz, :, :, mine].astype(F32) + self.c[yy, zz].astype(F32)
                ).astype(BF)

        copies = []
        for s in range(1, N_X):
            to = (p.x + s) % N_X
            copies.append(remote(self.a.at[to], self.xb.at[s - 1], self.send.at[s],
                                 self.xs.at[s - 1], p.at(x=to)))
        self.launch(copies)

    def to_y(self):
        p = self.place
        self.arrive()

        @pl.loop(0, N_Y)
        def _(yy):
            total = self.a[p.x, yy].astype(F32)
            for s in range(N_X - 1):
                total = total + self.xb[s, yy].astype(F32)
            self.b[yy] = total.astype(BF)

        here = p.yh * 2 + p.dp
        copies = []
        for s in range(1, 4):
            to = (here + s) % 4
            copies.append(remote(self.b.at[to // 2], self.yb.at[here], self.send.at[3 + s],
                                 self.ys.at[s - 1], p.at(yh=to // 2, dp=to % 2)))
        self.launch(copies)
        self.yb[here] = self.b[p.yh]

    def to_z(self):
        p = self.place
        self.arrive()
        total = self.yb[0].astype(F32)
        for s in range(1, 4):
            total = total + self.yb[s].astype(F32)
        self.d[...] = total.astype(BF)
        copies = []
        for s in range(1, N_Z):
            to = (p.z + s) % N_Z
            copies.append(remote(self.d.at[to], self.zb.at[p.z], self.send.at[6 + s],
                                 self.zs.at[s - 1], p.at(z=to)))
        self.launch(copies)
        self.zb[p.z] = self.d[p.z]

    def to_mate(self):
        p = self.place
        self.arrive()
        total = self.zb[0].astype(F32)
        for s in range(1, N_Z):
            total = total + self.zb[s].astype(F32)
        self.e[...] = total
        self.launch([
            remote(self.e, self.last, self.send.at[6 + N_Z], self.ls.at[0], p.at(core=1 - p.core))
        ])

    def result(self):
        self.arrive()
        first = self.place.core == 0
        own, other = self.e[...], self.last[...]
        full = jnp.concatenate([jnp.where(first, own, other), jnp.where(first, other, own)], 1)
        return jnp.where(first, full[:4], full[4:])


def scatter_scratch(cols):
    half = cols // 2
    sem = pltpu.SemaphoreType.DMA
    bufs = [
        pltpu.VMEM((N_Y, N_Z, N_X, 8, half), BF),
        pltpu.VMEM((N_X, N_Y, N_Z, 8, half), BF),
        pltpu.VMEM((N_X - 1, N_Y, N_Z, 8, half), BF),
        pltpu.VMEM((N_Y, N_Z, 8, half), BF),
        pltpu.VMEM((4, N_Z, 8, half), BF),
        pltpu.VMEM((N_Z, 8, half), BF),
        pltpu.VMEM((N_Z, 8, half), BF),
        pltpu.VMEM((8, half), F32),
        pltpu.VMEM((8, half), F32),
    ]
    sems = [sem((7 + N_Z,)), sem((1,)), sem((N_X - 1,)), sem((3,)), sem((N_Z - 1,)), sem((1,))]
    return dict(g=pltpu.VMEM((N_Y, N_Z, N_X, 8, cols), BF), bufs=bufs, sems=sems)


class Swap:
    def __init__(self, place, src, dst, send, recv):
        self.place, self.src, self.dst, self.send, self.recv = place, src, dst, send, recv
        self.n = src.shape[0]

    def start(self):
        p, n = self.place, self.n

        def step(s, carry):
            to = lax.rem(p.ctx + s, n)
            remote(self.src.at[to], self.dst.at[p.ctx], self.send, self.recv, (p.dp, to)).start()
            return carry

        lax.fori_loop(1, n, step, 0, unroll=4)
        self.dst[p.ctx] = self.src[p.ctx]

    def all_but_one(self, ref, sem):
        part = ref.at[pl.ds(0, self.n - 1)]
        pltpu.make_async_copy(part, part, sem).wait()

    def arrived(self):
        self.all_but_one(self.dst, self.recv)

    def gone(self):
        self.all_but_one(self.src, self.send)


def to_wire(ref, get, perm):
    for b in range(4):
        x = get(b)
        y = nn(perm, x).astype(BF)
        ref[32 * b : 32 * b + 32] = y.reshape(32, 8, y.shape[-1])


def block_of(ref, b):
    return jnp.concatenate([ref[r, 128 * b : 128 * b + 128] for r in range(2)], 0)


def to_columns(wire, col, perm):
    for b in range(4):
        x = wire[32 * b : 32 * b + 32]
        y = nn(perm, x.reshape(256, x.shape[-1])).astype(BF)
        for c in range(4):
            col[c, 64 * b : 64 * b + 64] = y[64 * c : 64 * c + 64]


def from_columns(col, wire, perm):
    for b in range(4):
        x = jnp.concatenate([col[c, 64 * b : 64 * b + 64] for c in range(4)], 0)
        y = nn(perm, x).astype(BF)
        wire[32 * b : 32 * b + 32] = y.reshape(32, 8, y.shape[-1])


def turned_wide(x, ident):
    return jnp.concatenate([turned(x[:, :256], ident), turned(x[:, 256:], ident)], 0)


def side_by_side(w, offset):
    return jnp.concatenate([w[:, i * 512 + offset : i * 512 + offset + HALF] for i in range(3)], 1)


def row_heads(s, r, lay, feats, grads, w, wo, ident):
    n = feats.shape[0]
    qkv = nn(feats, w).astype(BF)
    q_all, k_all, v_all = (qkv[:, i * HALF : (i + 1) * HALF] for i in range(3))
    d_t = nt(wo[:HALF], grads).astype(BF).astype(F32)
    q_t, k_t, v_t = (turned(x, ident) for x in (q_all, k_all, v_all))
    tri = lax.broadcasted_iota(jnp.int32, (BLOCK, BLOCK), 0) <= lax.broadcasted_iota(
        jnp.int32, (BLOCK, BLOCK), 1
    )
    chunks = []
    width = 2 * BLOCK
    for chunk in range(n // width):
        nj = (chunk + 1) * width
        cols = slice(chunk * width, (chunk + 1) * width)
        weights, ds_all, outs, dqs, dts_all = [], [], [], [], []
        for h in range(4):
            scores = nn(k_all[:nj], padded(q_t[head_rows(h), cols], h))
            blocks = []
            for half in range(2):
                ib = 2 * chunk + half
                lanes = slice(BLOCK * half, BLOCK * half + BLOCK)
                pieces = []
                for jb in range(ib):
                    bias = jnp.where(lay[h, ib, jb] == 1, 0.0, NEG)
                    pieces.append(scores[BLOCK * jb : BLOCK * jb + BLOCK, lanes] + bias)
                pieces.append(jnp.where(tri, scores[BLOCK * ib : BLOCK * ib + BLOCK, lanes], NEG))
                blocks.append(soften(pieces))
            wts = jnp.concatenate([stacked(x, nj) for x in blocks], 1)
            product = nn(with_ones(v_t[head_rows(h), :nj]), wts)
            inv = 1.0 / product[HEAD : HEAD + 1]
            out = product[:HEAD] * inv
            dts = (d_t[head_rows(h), cols] * inv).astype(BF)
            delta = jnp.sum(out * dts.astype(F32), axis=0, keepdims=True)
            d_prob = nn(v_all[:nj], padded(dts, h))
            ds_blocks = []
            for half in range(2):
                lanes = slice(BLOCK * half, BLOCK * half + BLOCK)
                ds_blocks.append([
                    (x.astype(F32) * (d_prob[BLOCK * j : BLOCK * j + BLOCK, lanes] - delta[:, lanes])).astype(BF)
                    for j, x in enumerate(blocks[half])
                ])
            ds = jnp.concatenate([stacked(x, nj) for x in ds_blocks], 1)
            dqs.append(nn(k_t[head_rows(h), :nj], ds) * SCALE)
            weights.append(wts)
            ds_all.append(ds)
            outs.append(out)
            dts_all.append(dts)
        att_t = jnp.concatenate(outs, 0).astype(BF)
        s["att_row_t"][r, :, cols] = att_t
        s["att_row"][r, cols] = nt(ident, att_t).astype(BF)
        dq = nt(ident, jnp.concatenate(dqs, 0).astype(BF)).astype(BF)
        chunks.append((
            jnp.concatenate(weights, 1), by_head(turned(jnp.concatenate(dts_all, 0), ident)),
            jnp.concatenate(ds_all, 1), by_head(q_all[cols]), dq,
        ))
    first, second = chunks
    dv_low = nn(second[0][:width], second[1]) + nn(first[0], first[1])
    dk_low = nn(second[2][:width], second[3]) + nn(first[2], first[3])
    dv = jnp.concatenate([dv_low, nn(second[0][width:], second[1])], 0).astype(BF)
    dk = (jnp.concatenate([dk_low, nn(second[2][width:], second[3])], 0) * SCALE).astype(BF)
    d_proj = jnp.concatenate([jnp.concatenate([first[4], second[4]], 0), dk, dv], 1)
    s["dp_row"][r] = d_proj


def weight_grads(feats_t, d_proj, put):
    for i in range(3):
        put(i, nn(feats_t, d_proj[:, i * HALF : (i + 1) * HALF]).astype(BF))


def put_block(ref, i, part):
    ref[:, :, :, :, i * HALF : (i + 1) * HALF] = part.reshape(N_Y, N_Z, N_X, 8, HALF)


def col_forward(s, c, w, mask, ident):
    qkv = nn(s["f_col"][c], w).astype(BF)
    s["qkv"][c] = qkv
    q_all, k_all, v_all = (qkv[:, i * HALF : (i + 1) * HALF] for i in range(3))
    q_t, v_t = turned(q_all, ident), turned(v_all, ident)
    outs = []
    for h in range(4):
        scores = nn(k_all, padded(q_t[head_rows(h)], h))
        early = soften([jnp.where(mask, scores[:BLOCK, :BLOCK], NEG)])
        late = soften([scores[:BLOCK, BLOCK:], jnp.where(mask, scores[BLOCK:, BLOCK:], NEG)])
        wts = jnp.concatenate([stacked(early, 256), stacked(late, 256)], 1)
        s["wts"][c, :, 256 * h : 256 * h + 256] = wts
        product = nn(with_ones(v_t[head_rows(h)]), wts)
        inv = 1.0 / product[HEAD : HEAD + 1]
        s["inv"][c, h : h + 1] = inv
        outs.append(product[:HEAD] * inv)
    out = jnp.concatenate(outs, 0)
    s["o"][c] = out
    s["a_col"][c] = nt(ident, out.astype(BF)).astype(BF)


def col_backward(s, c, w, mask, ident):
    qkv = s["qkv"][c]
    q_all, k_all, v_all = (qkv[:, i * HALF : (i + 1) * HALF] for i in range(3))
    k_t, d_t = turned(k_all, ident), nt(ident, s["d_col"][c])
    dqs, dts_all, ds_all = [], [], []
    for h in range(4):
        dts = (d_t[head_rows(h)] * s["inv"][c, h : h + 1]).astype(BF)
        delta = jnp.sum(s["o"][c, head_rows(h)] * dts.astype(F32), axis=0, keepdims=True)
        d_prob = nn(v_all, padded(dts, h))

        def grad(j, i):
            rows, lanes = slice(BLOCK * j, BLOCK * j + BLOCK), slice(BLOCK * i, BLOCK * i + BLOCK)
            wts = s["wts"][c, rows, 256 * h + BLOCK * i : 256 * h + BLOCK * i + BLOCK]
            return (wts.astype(F32) * (d_prob[rows, lanes] - delta[:, lanes])).astype(BF)

        ds = jnp.concatenate([stacked([grad(0, 0)], 256), stacked([grad(0, 1), grad(1, 1)], 256)], 1)
        dqs.append(nn(k_t[head_rows(h)], ds) * SCALE)
        dts_all.append(dts)
        ds_all.append(ds)
    dq = nt(ident, jnp.concatenate(dqs, 0).astype(BF)).astype(BF)
    dv = nn(s["wts"][c], by_head(turned(jnp.concatenate(dts_all, 0), ident))).astype(BF)
    dk = (nn(jnp.concatenate(ds_all, 1), by_head(q_all)) * SCALE).astype(BF)
    d_proj = jnp.concatenate([dq, dk, dv], 1)
    s["dp_col"][c] = d_proj
    s["g_col"][c] = nt(d_proj, w).astype(BF)


def whole_kernel(lay, feats_in, grads_in, w_in, wo_in, out, gf_out, gq_out, gwo_out, s):
    p = Place()
    feats, grads, w, wo = s["feats"], s["grads"], s["w"], s["wo"]
    loads = [
        pltpu.make_async_copy(src, dst, s["loads"].at[i])
        for i, (src, dst) in enumerate(((feats_in, feats), (wo_in, wo), (grads_in, grads), (w_in, w)))
    ]
    for load in loads:
        load.start()
    n_ctx = s["f_wire"].shape[0]
    barrier = pltpu.get_barrier_semaphore()

    def greet(step, carry):
        pl.semaphore_signal(
            barrier, inc=1, device_id=(p.dp, lax.rem(p.ctx + step, n_ctx)), device_id_type=MESH
        )
        return carry

    lax.fori_loop(1, n_ctx, greet, 0, unroll=4)
    for yh in (p.yh, 1 - p.yh):
        pl.semaphore_signal(barrier, inc=1, device_id=p.at(yh=yh, dp=1 - p.dp), device_id_type=MESH)

    perm = wire_matrix()
    loads[0].wait()
    to_wire(s["f_wire"], lambda b: block_of(feats, b), perm)
    pl.semaphore_wait(barrier, n_ctx + 1)
    sems = s["swap"]
    f_swap = Swap(p, s["f_wire"], s["f_got"], sems.at[0], sems.at[1])
    d_swap = Swap(p, s["d_wire"], s["d_got"], sems.at[2], sems.at[3])
    a_swap = Swap(p, s["a_wire"], s["a_got"], sems.at[4], sems.at[5])
    g_swap = Swap(p, s["g_wire"], s["g_got"], sems.at[6], sems.at[7])
    f_swap.start()
    for load in loads[1:]:
        load.wait()
    to_wire(s["d_wire"], lambda b: nt(block_of(grads, b), wo[HALF:]).astype(BF), perm)
    d_swap.start()

    ident = eye(256)
    s["w_row"][...] = side_by_side(w, 0)
    s["w_col"][...] = side_by_side(w, HALF)
    w_row, w_col = s["w_row"], s["w_col"]

    @pl.loop(0, 2)
    def _(r):
        row_heads(s, r, lay, feats[r], grads[r], w_row[...], wo, ident)

    gq_row, gq_col, gwo = (Scatter(p, s[k]["g"], s[k]["bufs"], s[k]["sems"]) for k in ("gq_row", "gq_col", "gwo"))
    feats_t = jnp.concatenate([turned_wide(feats[r], ident) for r in range(2)], 1)
    weight_grads(feats_t, s["dp_row"][...].reshape(1024, 768), lambda i, x: put_block(gq_row.g, i, x))
    gq_row.to_core()

    mask = lax.broadcasted_iota(jnp.int32, (BLOCK, BLOCK), 0) <= lax.broadcasted_iota(
        jnp.int32, (BLOCK, BLOCK), 1
    )
    split, join = column_matrix(), uncolumn_matrix()
    f_swap.arrived()
    to_columns(s["f_got"], s["f_col"], split)

    @pl.loop(0, 2)
    def _(pair):
        for c in (2 * pair, 2 * pair + 1):
            col_forward(s, c, w_col[...], mask, ident)

    from_columns(s["a_col"], s["a_wire"], join)
    a_swap.start()
    gq_row.to_x()

    d_swap.arrived()
    to_columns(s["d_got"], s["d_col"], split)

    @pl.loop(0, 2)
    def _(pair):
        for c in (2 * pair, 2 * pair + 1):
            col_backward(s, c, w_col[...], mask, ident)

    from_columns(s["g_col"], s["g_wire"], join)
    g_swap.start()
    gq_row.to_y()
    feats_t = jnp.concatenate([turned_wide(s["f_col"][c], ident) for c in range(4)], 1)
    weight_grads(feats_t, s["dp_col"][...].reshape(1024, 768), lambda i, x: put_block(gq_col.g, i, x))
    gq_col.to_core()
    part = nn(s["att_row_t"][0], grads[0]) + nn(s["att_row_t"][1], grads[1])
    gwo.g[0] = part.astype(BF).reshape(N_Z, N_X, 8, 512)
    gq_col.to_x()

    unwire = unwire_matrix()
    a_swap.arrived()
    part = None
    for b in range(4):
        x = s["a_got"][32 * b : 32 * b + 32]
        a = nn(unwire, x.reshape(256, HALF)).astype(BF)
        term = nn(turned(a, ident), block_of(grads, b))
        part = term if part is None else part + term
        s["att_col"][0, 128 * b : 128 * b + 128] = a[:128]
        s["att_col"][1, 128 * b : 128 * b + 128] = a[128:]
    gwo.g[1] = part.astype(BF).reshape(N_Z, N_X, 8, 512)
    gwo.to_core()
    for r in range(2):
        both = jnp.concatenate([s["att_row"][r], s["att_col"][r]], 1)
        out[r] = nn(both, wo[...]).astype(BF)
    gwo.to_x()
    gq_row.to_z()
    for r in range(2):
        s["gf_row"][r] = nt(s["dp_row"][r], w_row[...])
    gq_col.to_y()
    gwo.to_y()
    gq_col.to_z()
    gwo.to_z()

    g_swap.arrived()
    for b in range(4):
        if b == 2:
            for kind in (gq_row, gq_col, gwo):
                kind.to_mate()
        x = s["g_got"][32 * b : 32 * b + 32]
        g = nn(unwire, x.reshape(256, 512))
        for r in range(2):
            rows = slice(128 * b, 128 * b + 128)
            gf_out[r, rows] = (s["gf_row"][r, rows] + g[128 * r : 128 * r + 128]).astype(BF)
    for swap in (f_swap, d_swap, a_swap, g_swap):
        swap.gone()
    for offset, kind in ((0, gq_row), (HALF, gq_col)):
        rows = kind.result()
        for i in range(3):
            gq_out[:, i * 512 + offset : i * 512 + offset + HALF] = rows[:, i * HALF : (i + 1) * HALF]
    gwo_out[...] = gwo.result()


def on_device(features, w_qkv, w_out, layout, grad_out):
    n_clips, n_rows, length, width = features.shape
    n_ctx = lax.axis_size("ctx")
    vm = pl.BlockSpec(memory_space=pltpu.VMEM)
    vmem = pltpu.VMEM
    scratch = dict(
        f_wire=vmem((n_ctx, 8, 512), BF),
        f_got=vmem((n_ctx, 8, 512), BF),
        d_wire=vmem((n_ctx, 8, 256), BF),
        d_got=vmem((n_ctx, 8, 256), BF),
        a_wire=vmem((n_ctx, 8, 256), BF),
        a_got=vmem((n_ctx, 8, 256), BF),
        g_wire=vmem((n_ctx, 8, 512), BF),
        g_got=vmem((n_ctx, 8, 512), BF),
        swap=pltpu.SemaphoreType.DMA((8,)),
        feats=vmem((2, 512, 512), BF),
        grads=vmem((2, 512, 512), BF),
        w=vmem((512, 1536), BF),
        wo=vmem((512, 512), BF),
        loads=pltpu.SemaphoreType.DMA((4,)),
        w_row=vmem((512, 768), BF),
        w_col=vmem((512, 768), BF),
        att_row=vmem((2, 512, 256), BF),
        att_row_t=vmem((2, 256, 512), BF),
        att_col=vmem((2, 512, 256), BF),
        gf_row=vmem((2, 512, 512), F32),
        dp_row=vmem((2, 512, 768), BF),
        f_col=vmem((4, 256, 512), BF),
        d_col=vmem((4, 256, 256), BF),
        a_col=vmem((4, 256, 256), BF),
        g_col=vmem((4, 256, 512), BF),
        qkv=vmem((4, 256, 768), BF),
        wts=vmem((4, 256, 1024), BF),
        inv=vmem((4, 8, 256), F32),
        o=vmem((4, 256, 256), F32),
        dp_col=vmem((4, 256, 768), BF),
        gq_row=scatter_scratch(768),
        gq_col=scatter_scratch(768),
        gwo=scatter_scratch(512),
    )
    flat, tree = jax.tree.flatten(scratch, is_leaf=lambda x: not isinstance(x, (dict, list)))
    n_out = 4

    def kernel(lay, feats, grads, w, wo, *rest):
        outs, refs = rest[:n_out], rest[n_out:]
        whole_kernel(lay, feats, grads, w, wo, *outs, jax.tree.unflatten(tree, refs))

    shape = (n_rows, length, width)
    out, gf, gq, gwo = pl.pallas_call(
        kernel,
        out_shape=[
            jax.ShapeDtypeStruct(shape, BF),
            jax.ShapeDtypeStruct(shape, BF),
            jax.ShapeDtypeStruct((4, 1536), F32),
            jax.ShapeDtypeStruct((4, 512), F32),
        ],
        in_specs=[pl.BlockSpec(memory_space=pltpu.SMEM)] + [pl.BlockSpec(memory_space=pltpu.HBM)] * 4,
        out_specs=[vm] * n_out,
        scratch_shapes=flat,
        compiler_params=pltpu.CompilerParams(
            collective_id=1, has_side_effects=True, vmem_limit_bytes=VMEM_LIMIT
        ),
        name="whole_layer",
    )(
        *(
            pltpu.with_memory_space_constraint(a, pltpu.HBM)
            for a in (layout, features.reshape(shape), grad_out.reshape(shape), w_qkv, w_out)
        )
    )
    full = (n_clips,) + shape
    return out.reshape(full), gf.reshape(full), gq, gwo


def solution(mesh):
    return jax.shard_map(
        on_device,
        mesh=mesh,
        in_specs=(P("dp", "ctx", None, None), P(), P(), P(), P("dp", "ctx", None, None)),
        out_specs=(
            P("dp", "ctx", None, None),
            P("dp", "ctx", None, None),
            P("ctx", None),
            P("ctx", None),
        ),
        check_vma=False,
    )
```

```python
import functools

import jax
import jax.numpy as jnp
from jax import lax
from jax.experimental import pallas as pl
from jax.experimental.pallas import tpu as pltpu
from jax.sharding import PartitionSpec as P

HEADS = 8
HEAD = 64
BLOCK = 128
HALF = 256
SCALE = HEAD**-0.5
NEG = -1e30
BF = jnp.bfloat16
F32 = jnp.float32
VMEM_LIMIT = 40 * 1024 * 1024
MESH = pl.DeviceIdType.MESH
N_Y, N_Z, N_X = 2, 8, 4
SCALE_LOG2E = SCALE * 1.4426950408889634


def nn(a, b):
    return jnp.dot(a, b, preferred_element_type=F32)


def nt(a, b):
    return lax.dot_general(a, b, (((1,), (1,)), ((), ())), preferred_element_type=F32)


def eye(n):
    r = lax.broadcasted_iota(jnp.int32, (n, n), 0)
    c = lax.broadcasted_iota(jnp.int32, (n, n), 1)
    return (r == c).astype(F32).astype(BF)


def turned(x, ident):
    return nt(ident, x).astype(BF)


def wire_matrix():
    t = lax.broadcasted_iota(jnp.int32, (256, 256), 0)
    k = lax.broadcasted_iota(jnp.int32, (256, 256), 1)
    src = ((t >> 2) & 1) * 128 + (t >> 3) * 4 + (t & 3)
    return (k == src).astype(F32).astype(BF)


def unwire_matrix():
    t = lax.broadcasted_iota(jnp.int32, (256, 256), 1)
    k = lax.broadcasted_iota(jnp.int32, (256, 256), 0)
    src = ((t >> 2) & 1) * 128 + (t >> 3) * 4 + (t & 3)
    return (k == src).astype(F32).astype(BF)


def column_matrix():
    t = lax.broadcasted_iota(jnp.int32, (256, 256), 0)
    k = lax.broadcasted_iota(jnp.int32, (256, 256), 1)
    return (k == (t & 63) * 4 + (t >> 6)).astype(F32).astype(BF)


def uncolumn_matrix():
    t = lax.broadcasted_iota(jnp.int32, (256, 256), 1)
    k = lax.broadcasted_iota(jnp.int32, (256, 256), 0)
    return (k == (t & 63) * 4 + (t >> 6)).astype(F32).astype(BF)


def lanes_of_head(x, h):
    c = lax.broadcasted_iota(jnp.int32, x.shape, 1)
    return jnp.where((c >> 6) == h, x, jnp.zeros_like(x))


def soften(pieces):
    high = pieces[0]
    for x in pieces[1:]:
        high = jnp.maximum(high, x)
    top = jnp.max(high, axis=0, keepdims=True)
    return [jnp.exp2((x - top) * SCALE_LOG2E).astype(BF) for x in pieces]


def stacked(pieces, n_keys):
    rest = n_keys - BLOCK * len(pieces)
    if rest:
        pieces = pieces + [jnp.zeros((rest, BLOCK), BF)]
    return jnp.concatenate(pieces, 0)


def padded(x, h):
    parts = [jnp.zeros((HEAD * h, x.shape[1]), BF)] if h else []
    parts.append(x)
    if h < 3:
        parts.append(jnp.zeros((HEAD * (3 - h), x.shape[1]), BF))
    return jnp.concatenate(parts, 0)


def with_ones(v_t):
    return jnp.concatenate([v_t, jnp.ones((16, v_t.shape[1]), BF)], 0)


def by_head(x):
    return jnp.concatenate([lanes_of_head(x, h) for h in range(4)], 0)


def head_rows(h):
    return slice(h * HEAD, (h + 1) * HEAD)


class Place:
    def __init__(self):
        self.dp = lax.axis_index("dp")
        self.ctx = lax.axis_index("ctx")
        self.core = self.ctx % 2
        self.x = (self.ctx // 2) % N_X
        self.z = (self.ctx // (2 * N_X)) % N_Z
        self.yh = self.ctx // (2 * N_X * N_Z)

    def at(self, yh=None, z=None, x=None, core=None, dp=None):
        yh = self.yh if yh is None else yh
        z = self.z if z is None else z
        x = self.x if x is None else x
        core = self.core if core is None else core
        dp = self.dp if dp is None else dp
        return (dp, ((yh * N_Z + z) * N_X + x) * 2 + core)


def remote(src, dst, send, recv, device):
    return pltpu.make_async_remote_copy(
        src_ref=src, dst_ref=dst, send_sem=send, recv_sem=recv, device_id=device, device_id_type=MESH
    )


class Scatter:
    def __init__(self, place, g, bufs, sems):
        self.place, self.g = place, g
        self.c, self.a, self.xb, self.b, self.yb, self.d, self.zb, self.e, self.last = bufs
        self.send, self.cs, self.xs, self.ys, self.zs, self.ls = sems
        self.half = g.shape[-1] // 2
        self.copies = []

    def launch(self, copies):
        for c in copies:
            c.start()
        self.copies = copies

    def arrive(self):
        for c in self.copies:
            c.wait()

    def to_core(self):
        p, half = self.place, self.half
        theirs = pl.ds(pl.multiple_of((1 - p.core) * half, 128), half)
        self.launch([
            remote(self.g.at[:, :, :, :, theirs], self.c, self.send.at[0], self.cs.at[0],
                   p.at(core=1 - p.core))
        ])

    def to_x(self):
        p, half = self.place, self.half
        self.arrive()
        mine = pl.ds(pl.multiple_of(p.core * half, 128), half)

        @pl.loop(0, N_Z)
        def _(zz):
            for yy in range(N_Y):
                self.a[:, yy, zz] = (
                    self.g[yy, zz, :, :, mine].astype(F32) + self.c[yy, zz].astype(F32)
                ).astype(BF)

        copies = []
        for s in range(1, N_X):
            to = (p.x + s) % N_X
            copies.append(remote(self.a.at[to], self.xb.at[s - 1], self.send.at[s],
                                 self.xs.at[s - 1], p.at(x=to)))
        self.launch(copies)

    def to_y(self):
        p = self.place
        self.arrive()

        @pl.loop(0, N_Y)
        def _(yy):
            total = self.a[p.x, yy].astype(F32)
            for s in range(N_X - 1):
                total = total + self.xb[s, yy].astype(F32)
            self.b[yy] = total.astype(BF)

        here = p.yh * 2 + p.dp
        copies = []
        for s in range(1, 4):
            to = (here + s) % 4
            copies.append(remote(self.b.at[to // 2], self.yb.at[here], self.send.at[3 + s],
                                 self.ys.at[s - 1], p.at(yh=to // 2, dp=to % 2)))
        self.launch(copies)
        self.yb[here] = self.b[p.yh]

    def to_z(self):
        p = self.place
        self.arrive()
        total = self.yb[0].astype(F32)
        for s in range(1, 4):
            total = total + self.yb[s].astype(F32)
        self.d[...] = total.astype(BF)
        copies = []
        for s in range(1, N_Z):
            to = (p.z + s) % N_Z
            copies.append(remote(self.d.at[to], self.zb.at[p.z], self.send.at[6 + s],
                                 self.zs.at[s - 1], p.at(z=to)))
        self.launch(copies)
        self.zb[p.z] = self.d[p.z]

    def to_mate(self):
        p = self.place
        self.arrive()
        total = self.zb[0].astype(F32)
        for s in range(1, N_Z):
            total = total + self.zb[s].astype(F32)
        self.e[...] = total
        self.launch([
            remote(self.e, self.last, self.send.at[6 + N_Z], self.ls.at[0], p.at(core=1 - p.core))
        ])

    def result(self):
        self.arrive()
        first = self.place.core == 0
        own, other = self.e[...], self.last[...]
        full = jnp.concatenate([jnp.where(first, own, other), jnp.where(first, other, own)], 1)
        return jnp.where(first, full[:4], full[4:])


def scatter_scratch(cols):
    half = cols // 2
    sem = pltpu.SemaphoreType.DMA
    bufs = [
        pltpu.VMEM((N_Y, N_Z, N_X, 8, half), BF),
        pltpu.VMEM((N_X, N_Y, N_Z, 8, half), BF),
        pltpu.VMEM((N_X - 1, N_Y, N_Z, 8, half), BF),
        pltpu.VMEM((N_Y, N_Z, 8, half), BF),
        pltpu.VMEM((4, N_Z, 8, half), BF),
        pltpu.VMEM((N_Z, 8, half), BF),
        pltpu.VMEM((N_Z, 8, half), BF),
        pltpu.VMEM((8, half), F32),
        pltpu.VMEM((8, half), F32),
    ]
    sems = [sem((7 + N_Z,)), sem((1,)), sem((N_X - 1,)), sem((3,)), sem((N_Z - 1,)), sem((1,))]
    return dict(g=pltpu.VMEM((N_Y, N_Z, N_X, 8, cols), BF), bufs=bufs, sems=sems)


class Swap:
    def __init__(self, place, src, dst, send, recv):
        self.place, self.src, self.dst, self.send, self.recv = place, src, dst, send, recv
        self.n = src.shape[0]

    def start(self):
        p, n = self.place, self.n

        def step(s, carry):
            to = (p.ctx + s) % n
            remote(self.src.at[to], self.dst.at[p.ctx], self.send, self.recv, (p.dp, to)).start()
            return carry

        lax.fori_loop(1, n, step, 0)
        self.dst[p.ctx] = self.src[p.ctx]

    def all_but_one(self, ref, sem):
        part = ref.at[pl.ds(0, self.n - 1)]
        pltpu.make_async_copy(part, part, sem).wait()

    def arrived(self):
        self.all_but_one(self.dst, self.recv)

    def gone(self):
        self.all_but_one(self.src, self.send)


def to_wire(ref, get, perm):
    for b in range(4):
        x = get(b)
        y = nn(perm, x).astype(BF)
        ref[32 * b : 32 * b + 32] = y.reshape(32, 8, y.shape[-1])


def block_of(ref, b):
    return jnp.concatenate([ref[r, 128 * b : 128 * b + 128] for r in range(2)], 0)


def to_columns(wire, col, perm):
    for b in range(4):
        x = wire[32 * b : 32 * b + 32]
        y = nn(perm, x.reshape(256, x.shape[-1])).astype(BF)
        for c in range(4):
            col[c, 64 * b : 64 * b + 64] = y[64 * c : 64 * c + 64]


def from_columns(col, wire, perm):
    for b in range(4):
        x = jnp.concatenate([col[c, 64 * b : 64 * b + 64] for c in range(4)], 0)
        y = nn(perm, x).astype(BF)
        wire[32 * b : 32 * b + 32] = y.reshape(32, 8, y.shape[-1])


def turned_wide(x, ident):
    return jnp.concatenate([turned(x[:, :256], ident), turned(x[:, 256:], ident)], 0)


def side_by_side(w, offset):
    return jnp.concatenate([w[:, i * 512 + offset : i * 512 + offset + HALF] for i in range(3)], 1)


def row_heads(s, r, lay, feats, grads, w, wo, ident):
    n = feats.shape[0]
    qkv = nn(feats, w).astype(BF)
    q_all, k_all, v_all = (qkv[:, i * HALF : (i + 1) * HALF] for i in range(3))
    d_t = nt(wo[:HALF], grads).astype(BF).astype(F32)
    q_t, k_t, v_t = (turned(x, ident) for x in (q_all, k_all, v_all))
    tri = lax.broadcasted_iota(jnp.int32, (BLOCK, BLOCK), 0) <= lax.broadcasted_iota(
        jnp.int32, (BLOCK, BLOCK), 1
    )
    chunks = []
    width = 2 * BLOCK
    for chunk in range(n // width):
        nj = (chunk + 1) * width
        cols = slice(chunk * width, (chunk + 1) * width)
        weights, ds_all, outs, dqs, dts_all = [], [], [], [], []
        for h in range(4):
            scores = nn(k_all[:nj], padded(q_t[head_rows(h), cols], h))
            blocks = []
            for half in range(2):
                ib = 2 * chunk + half
                lanes = slice(BLOCK * half, BLOCK * half + BLOCK)
                pieces = []
                for jb in range(ib):
                    bias = jnp.where(lay[h, ib, jb] == 1, 0.0, NEG)
                    pieces.append(scores[BLOCK * jb : BLOCK * jb + BLOCK, lanes] + bias)
                pieces.append(jnp.where(tri, scores[BLOCK * ib : BLOCK * ib + BLOCK, lanes], NEG))
                blocks.append(soften(pieces))
            wts = jnp.concatenate([stacked(x, nj) for x in blocks], 1)
            product = nn(with_ones(v_t[head_rows(h), :nj]), wts)
            inv = 1.0 / product[HEAD : HEAD + 1]
            out = product[:HEAD] * inv
            dts = (d_t[head_rows(h), cols] * inv).astype(BF)
            delta = jnp.sum(out * dts.astype(F32), axis=0, keepdims=True)
            d_prob = nn(v_all[:nj], padded(dts, h))
            ds_blocks = []
            for half in range(2):
                lanes = slice(BLOCK * half, BLOCK * half + BLOCK)
                ds_blocks.append([
                    (x.astype(F32) * (d_prob[BLOCK * j : BLOCK * j + BLOCK, lanes] - delta[:, lanes])).astype(BF)
                    for j, x in enumerate(blocks[half])
                ])
            ds = jnp.concatenate([stacked(x, nj) for x in ds_blocks], 1)
            dqs.append(nn(k_t[head_rows(h), :nj], ds) * SCALE)
            weights.append(wts)
            ds_all.append(ds)
            outs.append(out)
            dts_all.append(dts)
        att_t = jnp.concatenate(outs, 0).astype(BF)
        s["att_row_t"][r, :, cols] = att_t
        s["att_row"][r, cols] = nt(ident, att_t).astype(BF)
        dq = nt(ident, jnp.concatenate(dqs, 0).astype(BF)).astype(BF)
        chunks.append((
            jnp.concatenate(weights, 1), by_head(turned(jnp.concatenate(dts_all, 0), ident)),
            jnp.concatenate(ds_all, 1), by_head(q_all[cols]), dq,
        ))
    first, second = chunks
    dv_low = nn(second[0][:width], second[1]) + nn(first[0], first[1])
    dk_low = nn(second[2][:width], second[3]) + nn(first[2], first[3])
    dv = jnp.concatenate([dv_low, nn(second[0][width:], second[1])], 0).astype(BF)
    dk = (jnp.concatenate([dk_low, nn(second[2][width:], second[3])], 0) * SCALE).astype(BF)
    d_proj = jnp.concatenate([jnp.concatenate([first[4], second[4]], 0), dk, dv], 1)
    s["dp_row"][r] = d_proj


def weight_grads(feats_t, d_proj, put):
    for i in range(3):
        put(i, nn(feats_t, d_proj[:, i * HALF : (i + 1) * HALF]).astype(BF))


def put_block(ref, i, part):
    ref[:, :, :, :, i * HALF : (i + 1) * HALF] = part.reshape(N_Y, N_Z, N_X, 8, HALF)


def col_forward(s, c, w, mask, ident):
    qkv = nn(s["f_col"][c], w).astype(BF)
    s["qkv"][c] = qkv
    q_all, k_all, v_all = (qkv[:, i * HALF : (i + 1) * HALF] for i in range(3))
    q_t, v_t = turned(q_all, ident), turned(v_all, ident)
    outs = []
    for h in range(4):
        scores = nn(k_all, padded(q_t[head_rows(h)], h))
        early = soften([jnp.where(mask, scores[:BLOCK, :BLOCK], NEG)])
        late = soften([scores[:BLOCK, BLOCK:], jnp.where(mask, scores[BLOCK:, BLOCK:], NEG)])
        wts = jnp.concatenate([stacked(early, 256), stacked(late, 256)], 1)
        s["wts"][c, :, 256 * h : 256 * h + 256] = wts
        product = nn(with_ones(v_t[head_rows(h)]), wts)
        inv = 1.0 / product[HEAD : HEAD + 1]
        s["inv"][c, h : h + 1] = inv
        outs.append(product[:HEAD] * inv)
    out = jnp.concatenate(outs, 0)
    s["o"][c] = out
    s["a_col"][c] = nt(ident, out.astype(BF)).astype(BF)


def col_backward(s, c, w, mask, ident):
    qkv = s["qkv"][c]
    q_all, k_all, v_all = (qkv[:, i * HALF : (i + 1) * HALF] for i in range(3))
    k_t, d_t = turned(k_all, ident), nt(ident, s["d_col"][c])
    dqs, dts_all, ds_all = [], [], []
    for h in range(4):
        dts = (d_t[head_rows(h)] * s["inv"][c, h : h + 1]).astype(BF)
        delta = jnp.sum(s["o"][c, head_rows(h)] * dts.astype(F32), axis=0, keepdims=True)
        d_prob = nn(v_all, padded(dts, h))

        def grad(j, i):
            rows, lanes = slice(BLOCK * j, BLOCK * j + BLOCK), slice(BLOCK * i, BLOCK * i + BLOCK)
            wts = s["wts"][c, rows, 256 * h + BLOCK * i : 256 * h + BLOCK * i + BLOCK]
            return (wts.astype(F32) * (d_prob[rows, lanes] - delta[:, lanes])).astype(BF)

        ds = jnp.concatenate([stacked([grad(0, 0)], 256), stacked([grad(0, 1), grad(1, 1)], 256)], 1)
        dqs.append(nn(k_t[head_rows(h)], ds) * SCALE)
        dts_all.append(dts)
        ds_all.append(ds)
    dq = nt(ident, jnp.concatenate(dqs, 0).astype(BF)).astype(BF)
    dv = nn(s["wts"][c], by_head(turned(jnp.concatenate(dts_all, 0), ident))).astype(BF)
    dk = (nn(jnp.concatenate(ds_all, 1), by_head(q_all)) * SCALE).astype(BF)
    d_proj = jnp.concatenate([dq, dk, dv], 1)
    s["dp_col"][c] = d_proj
    s["g_col"][c] = nt(d_proj, w).astype(BF)


def whole_kernel(lay, feats_in, grads_in, w_in, wo_in, out, gf_out, gq_out, gwo_out, s):
    p = Place()
    feats, grads, w, wo = s["feats"], s["grads"], s["w"], s["wo"]
    loads = [
        pltpu.make_async_copy(src, dst, s["loads"].at[i])
        for i, (src, dst) in enumerate(((feats_in, feats), (wo_in, wo), (grads_in, grads), (w_in, w)))
    ]
    for load in loads:
        load.start()
    n_ctx = s["f_wire"].shape[0]
    barrier = pltpu.get_barrier_semaphore()

    def greet(step, carry):
        pl.semaphore_signal(
            barrier, inc=1, device_id=(p.dp, (p.ctx + step) % n_ctx), device_id_type=MESH
        )
        return carry

    lax.fori_loop(1, n_ctx, greet, 0)
    for yh in (p.yh, 1 - p.yh):
        pl.semaphore_signal(barrier, inc=1, device_id=p.at(yh=yh, dp=1 - p.dp), device_id_type=MESH)

    perm = wire_matrix()
    loads[0].wait()
    to_wire(s["f_wire"], lambda b: block_of(feats, b), perm)
    pl.semaphore_wait(barrier, n_ctx + 1)
    sems = s["swap"]
    f_swap = Swap(p, s["f_wire"], s["f_got"], sems.at[0], sems.at[1])
    d_swap = Swap(p, s["d_wire"], s["d_got"], sems.at[2], sems.at[3])
    a_swap = Swap(p, s["a_wire"], s["a_got"], sems.at[4], sems.at[5])
    g_swap = Swap(p, s["g_wire"], s["g_got"], sems.at[6], sems.at[7])
    f_swap.start()
    for load in loads[1:]:
        load.wait()
    to_wire(s["d_wire"], lambda b: nt(block_of(grads, b), wo[HALF:]).astype(BF), perm)
    d_swap.start()

    ident = eye(256)
    s["w_row"][...] = side_by_side(w, 0)
    s["w_col"][...] = side_by_side(w, HALF)
    w_row, w_col = s["w_row"], s["w_col"]

    @pl.loop(0, 2)
    def _(r):
        row_heads(s, r, lay, feats[r], grads[r], w_row[...], wo, ident)

    gq_row, gq_col, gwo = (Scatter(p, s[k]["g"], s[k]["bufs"], s[k]["sems"]) for k in ("gq_row", "gq_col", "gwo"))
    feats_t = jnp.concatenate([turned_wide(feats[r], ident) for r in range(2)], 1)
    weight_grads(feats_t, s["dp_row"][...].reshape(1024, 768), lambda i, x: put_block(gq_row.g, i, x))
    gq_row.to_core()

    mask = lax.broadcasted_iota(jnp.int32, (BLOCK, BLOCK), 0) <= lax.broadcasted_iota(
        jnp.int32, (BLOCK, BLOCK), 1
    )
    split, join = column_matrix(), uncolumn_matrix()
    f_swap.arrived()
    to_columns(s["f_got"], s["f_col"], split)

    @pl.loop(0, 4)
    def _(c):
        col_forward(s, c, w_col[...], mask, ident)

    from_columns(s["a_col"], s["a_wire"], join)
    a_swap.start()
    gq_row.to_x()

    d_swap.arrived()
    to_columns(s["d_got"], s["d_col"], split)

    @pl.loop(0, 4)
    def _(c):
        col_backward(s, c, w_col[...], mask, ident)

    from_columns(s["g_col"], s["g_wire"], join)
    g_swap.start()
    gq_row.to_y()
    feats_t = jnp.concatenate([turned_wide(s["f_col"][c], ident) for c in range(4)], 1)
    weight_grads(feats_t, s["dp_col"][...].reshape(1024, 768), lambda i, x: put_block(gq_col.g, i, x))
    gq_col.to_core()
    part = nn(s["att_row_t"][0], grads[0]) + nn(s["att_row_t"][1], grads[1])
    gwo.g[0] = part.astype(BF).reshape(N_Z, N_X, 8, 512)
    gq_col.to_x()

    unwire = unwire_matrix()
    a_swap.arrived()
    part = None
    for b in range(4):
        x = s["a_got"][32 * b : 32 * b + 32]
        a = nn(unwire, x.reshape(256, HALF)).astype(BF)
        term = nn(turned(a, ident), block_of(grads, b))
        part = term if part is None else part + term
        s["att_col"][0, 128 * b : 128 * b + 128] = a[:128]
        s["att_col"][1, 128 * b : 128 * b + 128] = a[128:]
    gwo.g[1] = part.astype(BF).reshape(N_Z, N_X, 8, 512)
    gwo.to_core()
    for r in range(2):
        both = jnp.concatenate([s["att_row"][r], s["att_col"][r]], 1)
        out[r] = nn(both, wo[...]).astype(BF)
    gwo.to_x()
    gq_row.to_z()
    for r in range(2):
        s["gf_row"][r] = nt(s["dp_row"][r], w_row[...])
    gq_col.to_y()
    gwo.to_y()
    gq_col.to_z()
    gwo.to_z()

    g_swap.arrived()
    for b in range(4):
        if b == 2:
            for kind in (gq_row, gq_col, gwo):
                kind.to_mate()
        x = s["g_got"][32 * b : 32 * b + 32]
        g = nn(unwire, x.reshape(256, 512))
        for r in range(2):
            rows = slice(128 * b, 128 * b + 128)
            gf_out[r, rows] = (s["gf_row"][r, rows] + g[128 * r : 128 * r + 128]).astype(BF)
    for swap in (f_swap, d_swap, a_swap, g_swap):
        swap.gone()
    for offset, kind in ((0, gq_row), (HALF, gq_col)):
        rows = kind.result()
        for i in range(3):
            gq_out[:, i * 512 + offset : i * 512 + offset + HALF] = rows[:, i * HALF : (i + 1) * HALF]
    gwo_out[...] = gwo.result()


def on_device(features, w_qkv, w_out, layout, grad_out):
    n_clips, n_rows, length, width = features.shape
    n_ctx = lax.axis_size("ctx")
    vm = pl.BlockSpec(memory_space=pltpu.VMEM)
    vmem = pltpu.VMEM
    scratch = dict(
        f_wire=vmem((n_ctx, 8, 512), BF),
        f_got=vmem((n_ctx, 8, 512), BF),
        d_wire=vmem((n_ctx, 8, 256), BF),
        d_got=vmem((n_ctx, 8, 256), BF),
        a_wire=vmem((n_ctx, 8, 256), BF),
        a_got=vmem((n_ctx, 8, 256), BF),
        g_wire=vmem((n_ctx, 8, 512), BF),
        g_got=vmem((n_ctx, 8, 512), BF),
        swap=pltpu.SemaphoreType.DMA((8,)),
        feats=vmem((2, 512, 512), BF),
        grads=vmem((2, 512, 512), BF),
        w=vmem((512, 1536), BF),
        wo=vmem((512, 512), BF),
        loads=pltpu.SemaphoreType.DMA((4,)),
        w_row=vmem((512, 768), BF),
        w_col=vmem((512, 768), BF),
        att_row=vmem((2, 512, 256), BF),
        att_row_t=vmem((2, 256, 512), BF),
        att_col=vmem((2, 512, 256), BF),
        gf_row=vmem((2, 512, 512), F32),
        dp_row=vmem((2, 512, 768), BF),
        f_col=vmem((4, 256, 512), BF),
        d_col=vmem((4, 256, 256), BF),
        a_col=vmem((4, 256, 256), BF),
        g_col=vmem((4, 256, 512), BF),
        qkv=vmem((4, 256, 768), BF),
        wts=vmem((4, 256, 1024), BF),
        inv=vmem((4, 8, 256), F32),
        o=vmem((4, 256, 256), F32),
        dp_col=vmem((4, 256, 768), BF),
        gq_row=scatter_scratch(768),
        gq_col=scatter_scratch(768),
        gwo=scatter_scratch(512),
    )
    flat, tree = jax.tree.flatten(scratch, is_leaf=lambda x: not isinstance(x, (dict, list)))
    n_out = 4

    def kernel(lay, feats, grads, w, wo, *rest):
        outs, refs = rest[:n_out], rest[n_out:]
        whole_kernel(lay, feats, grads, w, wo, *outs, jax.tree.unflatten(tree, refs))

    shape = (n_rows, length, width)
    out, gf, gq, gwo = pl.pallas_call(
        kernel,
        out_shape=[
            jax.ShapeDtypeStruct(shape, BF),
            jax.ShapeDtypeStruct(shape, BF),
            jax.ShapeDtypeStruct((4, 1536), F32),
            jax.ShapeDtypeStruct((4, 512), F32),
        ],
        in_specs=[pl.BlockSpec(memory_space=pltpu.SMEM)] + [pl.BlockSpec(memory_space=pltpu.HBM)] * 4,
        out_specs=[vm] * n_out,
        scratch_shapes=flat,
        compiler_params=pltpu.CompilerParams(
            collective_id=1, has_side_effects=True, vmem_limit_bytes=VMEM_LIMIT
        ),
        name="whole_layer",
    )(
        *(
            pltpu.with_memory_space_constraint(a, pltpu.HBM)
            for a in (layout, features.reshape(shape), grad_out.reshape(shape), w_qkv, w_out)
        )
    )
    full = (n_clips,) + shape
    return out.reshape(full), gf.reshape(full), gq, gwo


def solution(mesh):
    return jax.shard_map(
        on_device,
        mesh=mesh,
        in_specs=(P("dp", "ctx", None, None), P(), P(), P(), P("dp", "ctx", None, None)),
        out_specs=(
            P("dp", "ctx", None, None),
            P("dp", "ctx", None, None),
            P("ctx", None),
            P("ctx", None),
        ),
        check_vma=False,
    )
```
